32 devices in a mesh: gx: 4 (over y, x), gy: 8 (over z, core).
Axes of the slice: x: 2, y: 2, z: 4, core: 2. Of those that a mesh axis runs over, the one named last changes fastest.
Arguments:
- layer_in: bfloat16 [16384, 768], P(('gx', 'gy')), may hold values from -6 to 6
- doc_ids: int32 [32, 512], P('gx'), may hold values from 0 to 7, never falling along the last dimension, each value on 1 to 128 neighbouring positions
- mix_gain: bfloat16 [768], P(('gx', 'gy')), may hold values from 0.5 to 1.5
- value_weight: bfloat16 [768, 768], P('gx', 'gy'), may hold values from -0.21875 to 0.21875
- mixing: bfloat16 [12, 512, 512], P(None, 'gy', 'gx'), may hold values from -9 to 9
- output_weight: bfloat16 [768, 768], P('gy', 'gx'), may hold values from -0.875 to 0.875
- ffn_gain: bfloat16 [768], P(('gx', 'gy')), may hold values from 0.5 to 1.5
- up_weight: bfloat16 [768, 3072], P('gx', 'gy'), may hold values from -0.21875 to 0.21875
- down_weight: bfloat16 [3072, 768], P('gy', 'gx'), may hold values from -0.109375 to 0.109375
- cotangent: bfloat16 [16384, 768], P(('gx', 'gy')), may hold values from -6 to 6
Outputs:
- layer_out: bfloat16 [16384, 768], P(('gx', 'gy'))
- grad_in: float32 [16384, 768], P(('gx', 'gy'))
- grad_mix_gain: float32 [768], P(('gx', 'gy'))
- grad_value: float32 [768, 768], P('gx', 'gy')
- grad_mixing: float32 [12, 512, 512], P(None, 'gy', 'gx')
- grad_output: float32 [768, 768], P('gy', 'gx')
- grad_ffn_gain: float32 [768], P(('gx', 'gy'))
- grad_up: float32 [768, 3072], P('gx', 'gy')
- grad_down: float32 [3072, 768], P('gy', 'gx')
The draws below stay inside these ranges and needn't reach their ends.
Inputs may be any that keep to these rules, and one draw needn't show every extreme that they name: `doc_ids`: each row packs documents: ids never fall along the row, every id from 0 to 7 holds 1 to 128 tokens, and one document holds exactly 128.
All inputs are finite; a program needn't handle non-finite values.
Results may differ from the reference program's by a relative error of at most 0.025.
Values may be sent and summed in bfloat16 or wider, within the bound.
No kernel may reach another device: no remote copies, remote signals or barrier semaphores. Data moves between devices by JAX's collectives and lax.ppermute only.
A program may use at most 320 MiB of HBM per device.

```python
import math
import jax
import jax.numpy as jnp
import numpy as np
from jax import lax

D = 768
H = 12
HS = 64
FF = 3072
L = 512
DOCS = 8
DOC_MOST = 128
HD = 768
TOKENS = 16384
SEQS = 32


def level_of(key, dims, cuts, least, high):
    def one(position, shards_of):
        heights = jax.random.uniform(jax.random.fold_in(jax.random.fold_in(key, 6), position), (shards_of,), jnp.float32, least / len(cuts), high / len(cuts))
        return jnp.repeat(jnp.exp(heights), dims[position] // shards_of).reshape((-1,) + (1,) * (len(dims) - position - 1))

    gain = one(*cuts[0])
    for cut in cuts[1:]:
        gain = gain * one(*cut)
    return gain


def split_up(count, total, reach, skew):
    weights = [(1 << 20) // math.isqrt(rank ** skew) + 1 for rank in range(2, count + 1)]
    surplus, given = total - reach - (count - 1), [1] * (count - 1)
    while surplus > 0:
        movable = [i for i in range(count - 1) if given[i] < reach]
        mass, budget = sum([weights[i] for i in movable]), surplus
        for i in movable:
            addition = min(reach - given[i], max(1, budget * weights[i] // mass), surplus)
            given[i] = given[i] + addition
            surplus = surplus - addition
    return np.array([reach] + given)


def ragged_sizes(key, number_of, total, most, skew):
    if number_of == 2:
        one = jax.random.randint(key, (), max(1, total - most), min(most, total - 1) + 1)
        return jnp.stack([one, total - one])
    sizes = jnp.asarray(split_up(number_of, total, most, skew), jnp.int32)
    couples = (number_of - 1) // 2
    giver, receiver = sizes[1:1 + 2 * couples:2], sizes[2:2 + 2 * couples:2]
    margin = jnp.minimum(giver - 1, most - receiver)
    shifted = jax.random.randint(jax.random.fold_in(key, 1), (couples,), 0, 1 << 20) % (margin + 1)
    sizes = sizes.at[1:1 + 2 * couples:2].set(giver - shifted).at[2:2 + 2 * couples:2].set(receiver + shifted)
    return sizes[jax.random.permutation(jax.random.fold_in(key, 2), number_of)]


def bell_draw(key, dims, deviation, bound, shards=(), kind=jnp.bfloat16):
    entries = jax.random.normal(key, dims, jnp.float32) * deviation
    if len(shards) > 0:
        entries = level_of(key, dims, shards, -0.22, 0.18) * entries
    return jnp.clip(entries, min=-bound, max=bound).astype(kind)


def setup_inputs(seed: int = 0) -> dict:
    key_list = jax.random.split(jax.random.key(seed), 11)
    return {
        "layer_in": bell_draw(key_list[0], (TOKENS, D), 1.0, 6.0, ((0, 32),)),
        "doc_ids": jax.vmap(lambda own: jnp.searchsorted(jnp.cumsum(ragged_sizes(own, DOCS, L, DOC_MOST, 1)), jnp.arange(L), side="right"))(jax.random.split(key_list[1], SEQS)).reshape((SEQS, L)).astype(jnp.int32),
        "mix_gain": jnp.clip(1.0 + 0.1 * jax.random.normal(key_list[2], (D,), jnp.float32), 0.5, 1.5).astype(jnp.bfloat16),
        "value_weight": bell_draw(key_list[3], (D, HD), D ** -0.5, 0.21875, ((0, 4), (1, 8))),
        "mixing": bell_draw(key_list[4], (H, L, L), 1.5, 9.0, ((1, 8), (2, 4))),
        "output_weight": bell_draw(key_list[5], (HD, D), (HD // 16) ** -0.5, 0.875, ((0, 8), (1, 4))),
        "ffn_gain": jnp.clip(1.0 + 0.1 * jax.random.normal(key_list[6], (D,), jnp.float32), 0.5, 1.5).astype(jnp.bfloat16),
        "up_weight": bell_draw(key_list[7], (D, FF), D ** -0.5, 0.21875, ((0, 4), (1, 8))),
        "down_weight": bell_draw(key_list[8], (FF, D), FF ** -0.5, 0.109375, ((0, 8), (1, 4))),
        "cotangent": bell_draw(key_list[9], (TOKENS, D), 1.0, 6.0, ((0, 32),)),
    }


EPS = 1e-05
NEG = -1e+30

@jax.custom_vjp
def low(v):
    return lax.optimization_barrier(v.astype(jnp.bfloat16)).astype(jnp.float32)

@jax.custom_vjp
def low_back(v):
    return v

def low_keep(v):
    return (low(v), None)

def low_pass(kept, grad):
    return (grad,)

def back_keep(v):
    return (v, None)

def back_low(kept, grad):
    return (low(grad),)
low.defvjp(low_keep, low_pass)
low_back.defvjp(back_keep, back_low)

def layer_norm(tok_rows, norm_gain):
    average = lax.optimization_barrier(jnp.mean(tok_rows, axis=-1, keepdims=True))
    centred = tok_rows - average
    spread = lax.optimization_barrier(jnp.mean(centred * centred, axis=-1, keepdims=True))
    return centred * lax.rsqrt(spread + EPS) * norm_gain

def precise(left, right):
    return jnp.dot(left, right, precision=lax.Precision.HIGHEST, preferred_element_type=jnp.float32)

def block_forward(params, tok_rows, doc_rows):
    gain_one, value_mat, mix_logits, output_mat, gain_two, up_mat, down_mat = params
    seq_count = doc_rows.shape[0]
    normed_one = low(layer_norm(tok_rows, gain_one))
    values = low(low_back(precise(normed_one, value_mat)))
    head_vals = values.reshape(seq_count, L, H, HS)
    same_doc = doc_rows[:, :, None] == doc_rows[:, None, :]
    scores = jnp.where(same_doc[:, None], mix_logits[None], NEG)
    row_top = lax.optimization_barrier(jnp.max(scores, axis=-1, keepdims=True))
    expo_vals = jnp.exp(scores - row_top)
    mix_probs = low(expo_vals / lax.optimization_barrier(jnp.sum(expo_vals, axis=-1, keepdims=True)))
    mix_out = jnp.einsum('shqk,skhd->sqhd', mix_probs, head_vals, precision=lax.Precision.HIGHEST)
    mix_out = low(low_back(mix_out.reshape(seq_count * L, H * HS)))
    branch = low_back(precise(mix_out, output_mat))
    middle = tok_rows + branch
    normed_two = low(layer_norm(middle, gain_two))
    up_vals = low_back(precise(normed_two, up_mat))
    act_vals = low(jax.nn.gelu(up_vals, approximate=True))
    return middle + low_back(precise(act_vals, down_mat))

def reference(layer_in, doc_ids, mix_gain, value_weight, mixing, output_weight, ffn_gain, up_weight, down_weight, cotangent):
    params = tuple((arr.astype(jnp.float32) for arr in (mix_gain, value_weight, mixing, output_weight, ffn_gain, up_weight, down_weight)))
    per_block = math.gcd(SEQS, 8)
    block_total = SEQS // per_block
    tok_blocks = layer_in.astype(jnp.float32).reshape(block_total, per_block * L, D)
    doc_blocks = doc_ids.reshape(block_total, per_block, L)
    cot_blocks = cotangent.astype(jnp.float32).reshape(block_total, per_block * L, D)

    def block_step(grad_acc, block_item):
        tok_rows, doc_rows, cot_rows = block_item

        def forward_fn(param_set, tok_vals):
            return block_forward(param_set, tok_vals, doc_rows)
        out_rows, back_fn = jax.vjp(forward_fn, params, tok_rows)
        param_grads, tok_grads = back_fn(cot_rows)
        grad_acc = jax.tree.map(lambda left_acc, right_acc: left_acc + right_acc, grad_acc, param_grads)
        return (grad_acc, (out_rows.astype(jnp.bfloat16), tok_grads))
    zero_grads = tuple((jnp.zeros_like(param_arr) for param_arr in params))
    grad_sums, (out_blocks, in_grads) = lax.scan(block_step, zero_grads, (tok_blocks, doc_blocks, cot_blocks))
    gain_one_g, value_g, mixing_g, output_g, gain_two_g, up_g, down_g = grad_sums
    return (out_blocks.reshape(TOKENS, D), in_grads.reshape(TOKENS, D), gain_one_g, value_g, mixing_g, output_g, gain_two_g, up_g, down_g)
```

```python
import functools

import jax
import jax.numpy as jnp
from jax import lax
from jax.experimental import pallas as pl
from jax.experimental.pallas import tpu as pltpu
from jax.sharding import PartitionSpec as P

D = 768
H = 12
HS = 64
FF = 3072
L = 512
EPS = 1e-05
G = 4
Z = 4
DB = D // G
CB = D // (2 * Z)
FB = FF // (2 * Z)
QB = L // (2 * Z)
KB = L // G
LN = 128
GW = 2 * LN
TM = 128
WIN = 3
HZ = H // Z
GC = 0.7978845608
GA = 0.044715
VMEM_LIMIT = 52 * 1024 * 1024

F32 = jnp.float32
BF16 = jnp.bfloat16


def dot(a, b, ca, cb):
    return lax.dot_general(a, b, (((ca,), (cb,)), ((), ())), preferred_element_type=F32)


def call(body, grid, in_specs, out_specs, out_shape, scratch=(), flops=0, nbytes=0):
    return pl.pallas_call(
        body,
        grid_spec=pltpu.PrefetchScalarGridSpec(
            num_scalar_prefetch=1,
            grid=grid,
            in_specs=in_specs,
            out_specs=out_specs,
            scratch_shapes=list(scratch),
        ),
        out_shape=out_shape,
        compiler_params=pltpu.CompilerParams(
            dimension_semantics=("arbitrary",) * len(grid), vmem_limit_bytes=VMEM_LIMIT
        ),
        cost_estimate=pl.CostEstimate(flops=flops, bytes_accessed=nbytes, transcendentals=0),
    )


def whole(shape):
    zeros = (0,) * len(shape)
    return pl.BlockSpec(shape, lambda i, t: zeros, pipeline_mode=pl.Buffered(1))


def rows(width):
    return pl.BlockSpec((TM, width), lambda i, t: (i, 0))


def out_whole(shape):
    zeros = (0,) * len(shape)
    return pl.BlockSpec(shape, lambda i, t: zeros)


def tab_a(t, g):
    return t[1 + g]


def tab_b(t, g):
    return t[1 + G + g]


def tab_z(t, z):
    return t[1 + 2 * G + z]


def norm_stats(x):
    mean = jnp.mean(x, axis=-1, keepdims=True)
    cen = x - mean
    rstd = lax.rsqrt(jnp.mean(cen * cen, axis=-1, keepdims=True) + EPS)
    return cen, rstd


def weight_z(ref, t, z):
    return jnp.concatenate([ref[tab_a(t, g), tab_z(t, z)] for g in range(G)], axis=0)


def head_masks(nrows):
    lane = lax.broadcasted_iota(jnp.int32, (nrows, GW), 1)
    col = jnp.where(lane < LN, lane, lane - (LN - CB))
    junk = jnp.logical_or(
        jnp.logical_and(lane >= CB, lane < LN), lane >= LN + CB
    )
    col = jnp.where(junk, -1, col)
    return [jnp.logical_and(col >= HS * i, col < HS * (i + 1)) for i in range(HZ)]


def halves(ref, off, core, axis0=None):
    lo = pl.multiple_of(off + core * QB, QB)
    hi = pl.multiple_of(off + (1 - core) * QB, QB)
    if axis0 is None:
        return jnp.concatenate([ref[pl.ds(lo, QB), :], ref[pl.ds(hi, QB), :]], axis=0)
    return jnp.concatenate(
        [ref[axis0, pl.ds(lo, QB), :], ref[axis0, pl.ds(hi, QB), :]], axis=0
    )


def put_halves(ref, off, core, val, axis0=None):
    lo = pl.multiple_of(off + core * QB, QB)
    hi = pl.multiple_of(off + (1 - core) * QB, QB)
    if axis0 is None:
        ref[pl.ds(lo, QB), :] = val[:QB]
        ref[pl.ds(hi, QB), :] = val[QB:]
    else:
        ref[axis0, pl.ds(lo, QB), :] = val[:QB]
        ref[axis0, pl.ds(hi, QB), :] = val[QB:]


def exp_scores(own, oth, t, m, start, head, mask):
    parts = [
        jnp.concatenate(
            [
                own[tab_b(t, start + i), tab_z(t, m), head],
                oth[tab_b(t, start + i), tab_z(t, m), head],
            ],
            axis=0,
        )
        for i in range(WIN)
    ]
    scores = jnp.concatenate(parts, axis=1).astype(F32)
    return jnp.where(mask, jnp.exp(scores), 0.0)


def window(m):
    return jnp.clip(m - 1, 0, G - WIN)


def values_body(t, x_ref, g_ref, v_ref, n_ref, val_ref):
    cen, rstd = norm_stats(x_ref[...].astype(F32))
    low = (cen * rstd * g_ref[...]).astype(BF16)
    n_ref[...] = low
    for z in range(Z):
        val_ref[z] = dot(low, weight_z(v_ref, t, z), 1, 0).astype(BF16)


def mixer_body(t, x_ref, g_ref, dq_ref, dk_ref, val_ref, own_ref, oth_ref, o_ref, mix_ref, mid_ref, n_ref):
    m = pl.program_id(0)
    core = t[0]
    start = window(m)
    k0 = pl.multiple_of(start * KB, KB)
    mask = halves(dq_ref, 0, core) == dk_ref[:, pl.ds(k0, WIN * KB)]
    heads = head_masks(TM)
    acc = halves(x_ref, 0, core).astype(F32)
    for z in range(Z):
        win = val_ref[z, pl.ds(k0, WIN * KB), :]
        out = jnp.zeros((TM, GW), F32)
        for i in range(HZ):
            e = exp_scores(own_ref, oth_ref, t, m, start, HZ * z + i, mask)
            inv = 1.0 / jnp.sum(e, axis=-1, keepdims=True)
            part = dot((e * inv).astype(BF16), win, 1, 0)
            out = jnp.where(heads[i], part, out)
        low = out.astype(BF16)
        put_halves(mix_ref, 0, core, low, z)
        acc = acc + dot(low, weight_z(o_ref, t, z), 1, 1)
    put_halves(mid_ref, 0, core, acc)
    cen, rstd = norm_stats(acc)
    put_halves(n_ref, 0, core, (cen * rstd * g_ref[...]).astype(BF16))


def ffn_body(first, last, t, n_ref, c_ref, u_ref, d_ref, *refs):
    refs = list(refs)
    if not first:
        ia_ref, ib_ref = refs[:2]
        refs = refs[2:]
    if last:
        mid_ref = refs[0]
        refs = refs[1:]
    gu_ref, gd_ref, b_ref, a_ref = refs[:4]
    j = pl.program_id(0)
    n = n_ref[...]
    cot = c_ref[...]
    up_w = jnp.concatenate([u_ref[tab_b(t, g), 0] for g in range(G)], axis=0)
    dn_w = jnp.concatenate([d_ref[tab_a(t, g), 0] for g in range(G)], axis=0)

    @pl.when(j == 0)
    def _():
        if first:
            a_ref[...] = jnp.zeros_like(a_ref)
            b_ref[...] = jnp.zeros_like(b_ref)
        else:
            a_ref[...] = ia_ref[...]
            b_ref[...] = ib_ref[...]

    up = dot(n, up_w, 1, 0)
    sq = up * up
    th = jnp.tanh(GC * up * (1.0 + GA * sq))
    half = 0.5 + 0.5 * th
    act = (up * half).astype(BF16)
    slope = half + (0.5 * GC) * up * (1.0 - th * th) * (1.0 + (3.0 * GA) * sq)
    a_ref[...] += dot(act, dn_w, 1, 1)
    gd = dot(cot, act, 0, 0).astype(BF16)
    up_g = (dot(cot, dn_w, 1, 0) * slope).astype(BF16)
    gu = dot(n, up_g, 0, 0).astype(BF16)
    b_ref[...] += dot(up_g, up_w, 1, 1)
    for g in range(G):
        gu_ref[tab_b(t, g), 0] = gu[g * DB : (g + 1) * DB]
        gd_ref[tab_a(t, g), 0] = gd[g * DB : (g + 1) * DB]
    if last:
        lo_ref = refs[4]

        @pl.when(j == Z - 1)
        def _():
            lo_ref[...] = (mid_ref[...] + a_ref[...]).astype(BF16)


def norm_back(cen, rstd, gain, dn):
    xhat = cen * rstd
    e = dn * gain
    dv = (
        e
        - jnp.mean(e, axis=-1, keepdims=True)
        - xhat * jnp.mean(e * xhat, axis=-1, keepdims=True)
    ) * rstd
    return dv, jnp.sum(dn * xhat, axis=0, keepdims=True)


def mixer_back_body(
    t, dn_ref, mid_ref, c_ref, g_ref, dq_ref, dk_ref, mix_ref, val_ref, own_ref, oth_ref, o_ref,
    mg_ref, keep_ref, send_ref, go_ref, vg_ref, dg_ref, go_acc, vg_acc,
):
    m = pl.program_id(0)
    core = t[0]
    start = window(m)
    k0 = pl.multiple_of(start * KB, KB)

    @pl.when(m == 0)
    def _():
        go_acc[...] = jnp.zeros_like(go_acc)
        vg_acc[...] = jnp.zeros_like(vg_acc)
        dg_ref[...] = jnp.zeros_like(dg_ref)

    cen, rstd = norm_stats(halves(mid_ref, 0, core))
    dv, dg = norm_back(cen, rstd, g_ref[...], halves(dn_ref, 0, core))
    dg_ref[...] += dg
    mid_grad = halves(c_ref, 0, core).astype(F32) + dv
    put_halves(mg_ref, 0, core, mid_grad)
    branch = mid_grad.astype(BF16)
    mask = halves(dq_ref, 0, core) == dk_ref[:, pl.ds(k0, WIN * KB)]
    heads = head_masks(TM)
    rest = jnp.where(start == 0, G - 1, 0)
    keep_ref[tab_b(t, rest), 0] = jnp.zeros((H, QB, KB), BF16)
    send_ref[tab_b(t, rest), 0] = jnp.zeros((H, QB, KB), BF16)
    for z in range(Z):
        go_acc[z] += dot(branch, halves(mix_ref, 0, core, z), 0, 0)
        grad = dot(branch, weight_z(o_ref, t, z), 1, 0)
        grad = grad.astype(BF16).astype(F32)
        win = val_ref[z, pl.ds(k0, WIN * KB), :]
        total = jnp.zeros((WIN * KB, GW), F32)
        for i in range(HZ):
            e = exp_scores(own_ref, oth_ref, t, m, start, HZ * z + i, mask)
            inv = 1.0 / jnp.sum(e, axis=-1, keepdims=True)
            prob = e * inv
            mine = jnp.where(heads[i], grad, 0.0).astype(BF16)
            total = total + dot(prob.astype(BF16), mine, 0, 0)
            dp = dot(mine, win, 1, 1)
            pd = prob * dp
            ds = (pd - prob * jnp.sum(pd, axis=-1, keepdims=True)).astype(BF16)
            for k in range(WIN):
                blk = ds[:, k * KB : (k + 1) * KB]
                keep_ref[tab_b(t, start + k), 0, HZ * z + i] = blk[:QB]
                send_ref[tab_b(t, start + k), 0, HZ * z + i] = blk[QB:]
        vg_acc[z, pl.ds(k0, WIN * KB), :] += total

    @pl.when(m == Z - 1)
    def _():
        vg_ref[...] = vg_acc[...].astype(BF16)
        for z in range(Z):
            for g in range(G):
                go_ref[tab_a(t, g), tab_z(t, z)] = go_acc[z, g * DB : (g + 1) * DB].astype(BF16)


def last_body(t, x_ref, g_ref, n_ref, vg_ref, v_ref, mg_ref, gi_ref, gv_ref, dg_ref, gv_acc):
    m = pl.program_id(0)

    @pl.when(m == 0)
    def _():
        gv_acc[...] = jnp.zeros_like(gv_acc)
        dg_ref[...] = jnp.zeros_like(dg_ref)

    low = n_ref[...]
    dn = jnp.zeros((TM, D), F32)
    for z in range(Z):
        vg = vg_ref[z]
        gv_acc[z] += dot(low, vg, 0, 0)
        dn = dn + dot(vg, weight_z(v_ref, t, z), 1, 1)
    cen, rstd = norm_stats(x_ref[...].astype(F32))
    dv, dg = norm_back(cen, rstd, g_ref[...], dn)
    dg_ref[...] += dg
    gi_ref[...] = mg_ref[...] + dv

    @pl.when(m == Z - 1)
    def _():
        for z in range(Z):
            for g in range(G):
                gv_ref[tab_a(t, g), tab_z(t, z)] = gv_acc[z, g * DB : (g + 1) * DB].astype(BF16)


def sds(shape, dtype):
    return jax.ShapeDtypeStruct(shape, dtype)


W_SHAPE = (G, Z, DB, GW)
M_SHAPE = (G, Z, H, QB, KB)
F_SHAPE = (G, Z, DB, FB)


def run_values(tab, x, gain, v_w):
    return call(
        values_body,
        (L // TM,),
        [rows(D), whole((1, D)), whole(W_SHAPE)],
        [rows(D), pl.BlockSpec((Z, TM, GW), lambda i, t: (0, i, 0))],
        [sds((L, D), BF16), sds((Z, L, GW), BF16)],
        flops=2 * L * D * Z * GW,
        nbytes=6 << 20,
    )(tab, x, gain, v_w)


def run_mixer(tab, x, gain, dq, dk, vals, own, oth, o_w):
    return call(
        mixer_body,
        (L // TM,),
        [
            rows(D), whole((1, D)), rows(1), whole((1, L)), whole((Z, L, GW)),
            whole(M_SHAPE), whole(M_SHAPE), whole(W_SHAPE),
        ],
        [pl.BlockSpec((Z, TM, GW), lambda i, t: (0, i, 0)), rows(D), rows(D)],
        [sds((Z, L, GW), BF16), sds((L, D), F32), sds((L, D), BF16)],
        flops=2 * L * D * Z * GW + 2 * H * L * WIN * KB * GW,
        nbytes=14 << 20,
    )(tab, x, gain, dq, dk, vals, own, oth, o_w)


def run_ffn(tab, n, cot, u_w, d_w, acc=None, mid=None):
    first, last = acc is None, mid is not None
    blk = pl.BlockSpec((G, 1, DB, FB), lambda i, t: (0, i, 0, 0))
    in_specs = [whole((L, D)), whole((L, D)), blk, blk]
    args = [tab, n, cot, u_w, d_w]
    if not first:
        in_specs += [whole((L, D)), whole((L, D))]
        args += list(acc)
    if last:
        in_specs += [whole((L, D))]
        args += [mid]
    out_specs = [blk, blk, out_whole((L, D))]
    outs = [sds(F_SHAPE, BF16), sds(F_SHAPE, BF16), sds((L, D), F32)]
    scratch = ()
    if last:
        scratch = (pltpu.VMEM((L, D), F32),)
        out_specs += [out_whole((L, D))]
        outs += [sds((L, D), BF16)]
    else:
        out_specs += [out_whole((L, D))]
        outs += [sds((L, D), F32)]

    def body(t, *refs):
        if last:
            refs = list(refs)
            refs = refs[:-2] + [refs[-1], refs[-2]]
        ffn_body(first, last, t, *refs)

    return call(
        body, (Z,), in_specs, out_specs, outs, scratch, flops=6 * L * D * FF, nbytes=20 << 20
    )(*args)


def run_mixer_back(tab, dn, mid, cot, gain, dq, dk, mixed, vals, own, oth, o_w):
    blk = pl.BlockSpec((G, 1, H, QB, KB), lambda i, t: (0, t[1 + 2 * G + i], 0, 0, 0))
    return call(
        mixer_back_body,
        (L // TM,),
        [
            rows(D), rows(D), rows(D), whole((1, D)), rows(1), whole((1, L)),
            pl.BlockSpec((Z, TM, GW), lambda i, t: (0, i, 0)), whole((Z, L, GW)),
            whole(M_SHAPE), whole(M_SHAPE), whole(W_SHAPE),
        ],
        [rows(D), blk, blk, out_whole(W_SHAPE), out_whole((Z, L, GW)), out_whole((1, D))],
        [
            sds((L, D), F32), sds(M_SHAPE, BF16), sds(M_SHAPE, BF16), sds(W_SHAPE, BF16),
            sds((Z, L, GW), BF16), sds((1, D), F32),
        ],
        scratch=(pltpu.VMEM((Z, D, GW), F32), pltpu.VMEM((Z, L, GW), F32)),
        flops=4 * L * D * Z * GW + 6 * H * L * WIN * KB * GW,
        nbytes=28 << 20,
    )(tab, dn, mid, cot, gain, dq, dk, mixed, vals, own, oth, o_w)


def run_last(tab, x, gain, low, vg, v_w, mid_grad):
    return call(
        last_body,
        (L // TM,),
        [
            rows(D), whole((1, D)), rows(D), pl.BlockSpec((Z, TM, GW), lambda i, t: (0, i, 0)),
            whole(W_SHAPE), rows(D),
        ],
        [rows(D), out_whole(W_SHAPE), out_whole((1, D))],
        [sds((L, D), F32), sds(W_SHAPE, BF16), sds((1, D), F32)],
        scratch=(pltpu.VMEM((Z, D, GW), F32),),
        flops=4 * L * D * Z * GW,
        nbytes=12 << 20,
    )(tab, x, gain, low, vg, v_w, mid_grad)


def cols_in(mat):
    mat = mat.reshape(G, DB, Z, 2, CB).transpose(0, 2, 1, 3, 4)
    return jnp.pad(mat, ((0, 0),) * 4 + ((0, LN - CB),)).reshape(W_SHAPE)


def cols_out(mat):
    mat = mat.reshape(G, Z, DB, 2, LN)[..., :CB]
    return mat.transpose(0, 2, 1, 3, 4).reshape(D, D)


def shards(layer_in, doc_ids, mix_gain, value_w, mixing, output_w, ffn_gain, up_w, down_w, cot):
    ax = ("gx", "gy")
    me = lax.axis_index("gy")

    def gather(arr, d0, d1):
        arr = lax.all_gather(arr, "gx", axis=d0, tiled=True)
        return lax.all_gather(arr, "gy", axis=d1, tiled=True)

    def scatter(arr, d0, d1):
        arr = lax.psum_scatter(arr, "gx", scatter_dimension=d0, tiled=True)
        return lax.psum_scatter(arr, "gy", scatter_dimension=d1, tiled=True).astype(F32)

    gains = lax.all_gather(jnp.stack([mix_gain, ffn_gain]), ax, axis=1, tiled=True).astype(F32)
    gain_one, gain_two = gains[:1], gains[1:]
    v_full = cols_in(gather(value_w, 0, 1))
    o_full = cols_in(gather(output_w.T, 0, 1))
    mix_full = gather(mixing, 2, 1).reshape(H, Z, 2, QB, G, KB).transpose(2, 4, 1, 0, 3, 5)
    up_full = gather(up_w, 0, 1).reshape(G, DB, Z, 2, FB).transpose(3, 0, 2, 1, 4)
    dn_full = gather(down_w.T, 0, 1).reshape(G, DB, Z, 2, FB).transpose(3, 0, 2, 1, 4)
    tab = jnp.array([0] + [0, 1, 2, 3] * 3, jnp.int32)

    docs = lax.dynamic_slice_in_dim(doc_ids, me, 1, 0)
    dq, dk = docs.reshape(L, 1), docs
    low, vals = run_values(tab, layer_in, gain_one, v_full)
    mixed, mid, n_two = run_mixer(
        tab, layer_in, gain_two, dq, dk, vals, mix_full[0], mix_full[1], o_full
    )
    gu0, gd0, *acc = run_ffn(tab, n_two, cot, up_full[0], dn_full[0])
    acc = (acc[1], acc[0])
    gu1, gd1, n_grad, layer_out = run_ffn(tab, n_two, cot, up_full[1], dn_full[1], acc, mid)
    mid_grad, gm0, gm1, go, vg, dg_two = run_mixer_back(
        tab, n_grad, mid, cot, gain_two, dq, dk, mixed, vals, mix_full[0], mix_full[1], o_full
    )
    grad_in, gv, dg_one = run_last(tab, layer_in, gain_one, low, vg, v_full, mid_grad)

    def ffn_out(a, b):
        return jnp.stack([a, b]).transpose(1, 3, 2, 0, 4).reshape(D, FF)

    grad_up = scatter(ffn_out(gu0, gu1), 0, 1)
    grad_down = scatter(ffn_out(gd0, gd1), 0, 1).T
    grad_value = scatter(cols_out(gv), 0, 1)
    grad_output = scatter(cols_out(go), 0, 1).T
    gm = jnp.stack([gm0, gm1]).transpose(3, 2, 0, 4, 1, 5).reshape(H, L, L)
    grad_mixing = scatter(gm, 2, 1)
    dgs = jnp.concatenate([dg_one, dg_two], axis=0)
    dgs = lax.psum_scatter(dgs, ax, scatter_dimension=1, tiled=True)
    return (
        layer_out, grad_in, dgs[0], grad_value, grad_mixing, grad_output, dgs[1], grad_up, grad_down,
    )


def solution(mesh):
    tok = P(("gx", "gy"), None)
    vec = P(("gx", "gy"))
    wgt = P("gx", "gy")
    twg = P("gy", "gx")
    mix = P(None, "gy", "gx")
    in_specs = (tok, P("gx", None), vec, wgt, mix, twg, vec, wgt, twg, tok)
    out_specs = (tok, tok, vec, wgt, mix, twg, vec, wgt, twg)
    return jax.shard_map(shards, mesh=mesh, in_specs=in_specs, out_specs=out_specs, check_vma=False)
```

```python
import functools

import jax
import jax.numpy as jnp
from jax import lax
from jax.experimental import pallas as pl
from jax.experimental.pallas import tpu as pltpu
from jax.sharding import PartitionSpec as P

D = 768
H = 12
HS = 64
FF = 3072
L = 512
EPS = 1e-05
G = 4
Z = 4
DB = D // G
CB = D // (2 * Z)
FB = FF // (2 * Z)
QB = L // (2 * Z)
KB = L // G
LN = 128
GW = 2 * LN
GN = CB // 4
HA = H // 2
HR = HA * QB
TM = 128
WIN = 3
HZ = H // Z
GC = 0.7978845608
GA = 0.044715
VMEM_LIMIT = 52 * 1024 * 1024

F32 = jnp.float32
BF16 = jnp.bfloat16


def dot(a, b, ca, cb):
    return lax.dot_general(a, b, (((ca,), (cb,)), ((), ())), preferred_element_type=F32)


def call(body, grid, in_specs, out_specs, out_shape, scratch=(), flops=0, nbytes=0):
    return pl.pallas_call(
        body,
        grid_spec=pltpu.PrefetchScalarGridSpec(
            num_scalar_prefetch=1,
            grid=grid,
            in_specs=in_specs,
            out_specs=out_specs,
            scratch_shapes=list(scratch),
        ),
        out_shape=out_shape,
        compiler_params=pltpu.CompilerParams(
            dimension_semantics=("arbitrary",) * len(grid), vmem_limit_bytes=VMEM_LIMIT
        ),
        cost_estimate=pl.CostEstimate(flops=flops, bytes_accessed=nbytes, transcendentals=0),
    )


def whole(shape):
    zeros = (0,) * len(shape)
    return pl.BlockSpec(shape, lambda i, t: zeros, pipeline_mode=pl.Buffered(1))


def rows(width):
    return pl.BlockSpec((TM, width), lambda i, t: (i, 0))


def out_whole(shape):
    zeros = (0,) * len(shape)
    return pl.BlockSpec(shape, lambda i, t: zeros)


def tab_a(t, g):
    return t[1 + g]


def tab_b(t, g):
    return t[1 + G + g]


def tab_z(t, z):
    return t[1 + 2 * G + z]


def norm_stats(x):
    mean = jnp.mean(x, axis=-1, keepdims=True)
    cen = x - mean
    rstd = lax.rsqrt(jnp.mean(cen * cen, axis=-1, keepdims=True) + EPS)
    return cen, rstd


def weight_z(own, oth, t, z, base):
    parts = [
        jnp.concatenate(
            [ref[tab_a(t, g), tab_z(t, z), base : base + DB, :] for g in range(G)], axis=0
        )
        for ref in (own, oth)
    ]
    return jnp.concatenate(parts, axis=1)


def head_masks(core, nrows):
    lane = lax.broadcasted_iota(jnp.int32, (nrows, GW), 1)
    tile = lane // LN
    place = lane - tile * LN
    side = jnp.where(core == 0, tile, 1 - tile)
    col = jnp.where(place < CB, side * CB + place, -1)
    return [jnp.logical_and(col >= HS * i, col < HS * (i + 1)) for i in range(HZ)]


def halves(ref, core, lead=None):
    lo = pl.multiple_of(core * QB, QB)
    hi = pl.multiple_of((1 - core) * QB, QB)
    if lead is None:
        return jnp.concatenate([ref[pl.ds(lo, QB), :], ref[pl.ds(hi, QB), :]], axis=0)
    return jnp.concatenate([ref[lead, pl.ds(lo, QB), :], ref[lead, pl.ds(hi, QB), :]], axis=0)


def put_halves(ref, core, val, lead=None):
    lo = pl.multiple_of(core * QB, QB)
    hi = pl.multiple_of((1 - core) * QB, QB)
    if lead is None:
        ref[pl.ds(lo, QB), :] = val[:QB]
        ref[pl.ds(hi, QB), :] = val[QB:]
    else:
        ref[lead, pl.ds(lo, QB), :] = val[:QB]
        ref[lead, pl.ds(hi, QB), :] = val[QB:]


def window(m):
    return jnp.clip(m - 1, 0, G - WIN)


def exp_scores(a_own, a_oth, b_own, b_oth, t, m, head, mask):
    parts = []
    for i in range(WIN):
        both = []
        for a, b in ((a_own, b_own), (a_oth, b_oth)):
            if head < HA:
                both.append(a[tab_b(t, window(m) + i), tab_z(t, m), head * QB : (head + 1) * QB, :])
            else:
                h = head - HA
                both.append(b[tab_z(t, m), i, h * QB : (h + 1) * QB, :])
        parts.append(jnp.concatenate(both, axis=0))
    scores = jnp.concatenate(parts, axis=1).astype(F32)
    return jnp.where(mask, jnp.exp(scores), 0.0)


def gain_spots():
    for g in range(G):
        for z in range(Z):
            for c in range(2):
                yield g, z, c, DB * g + (2 * GN) * z + GN * c


def pick(core, c, own, oth):
    return jnp.where(core == c, own, oth)


def gains_row(own, oth, t, base):
    lane = lax.broadcasted_iota(jnp.int32, (1, LN), 1)
    tiles = [jnp.zeros((1, LN), F32) for _ in range(D // LN)]
    for g, z, c, at in gain_spots():
        a, b = (r[tab_a(t, g), tab_z(t, z), base : base + 16, :].astype(F32)[:1] for r in (own, oth))
        row = pick(t[0], c, a, b)
        tile, off = at // LN, at % LN
        row = pltpu.roll(row, (off - CB) % LN, 1)
        tiles[tile] = jnp.where(jnp.logical_and(lane >= off, lane < off + GN), row, tiles[tile])
        if off + GN > LN:
            tiles[tile + 1] = jnp.where(lane < off + GN - LN, row, tiles[tile + 1])
    return jnp.concatenate(tiles, axis=1)


def put_weight_grads(acc, dg, t, keep, send):
    lane = lax.broadcasted_iota(jnp.int32, (1, LN), 1)
    top = lax.broadcasted_iota(jnp.int32, (16, LN), 0) == 0
    spot = jnp.logical_and(top, jnp.logical_and(lane >= CB, lane < CB + GN))
    rows_of = {}
    for g, z, c, at in gain_spots():
        tile, off = at // LN, at % LN
        row = dg[:, tile * LN : (tile + 1) * LN]
        if off + GN > LN:
            row = jnp.where(lane < off, dg[:, (tile + 1) * LN : (tile + 2) * LN], row)
        rows_of[g, z, c] = pltpu.roll(row, (CB - off) % LN, 1)
    for g in range(G):
        for z in range(Z):
            for p, ref in ((0, keep), (1, send)):
                blk = acc[z, g * DB : (g + 1) * DB, p * LN : (p + 1) * LN]
                row = pick(t[0], p, rows_of[g, z, 0], rows_of[g, z, 1])
                ref[tab_a(t, g), tab_z(t, z)] = blk.astype(BF16)
                ref[tab_a(t, g), tab_z(t, z), 0:16, :] = jnp.where(spot, row, blk[:16]).astype(BF16)


def values_body(t, x_ref, own_ref, oth_ref, n_ref, val_ref, gain_ref):
    @pl.when(pl.program_id(0) == 0)
    def _():
        gain_ref[0:1, :] = gains_row(own_ref, oth_ref, t, 0)
        gain_ref[1:2, :] = gains_row(own_ref, oth_ref, t, DB)

    cen, rstd = norm_stats(x_ref[...].astype(F32))
    low = (cen * rstd * gain_ref[0:1, :]).astype(BF16)
    n_ref[...] = low
    for z in range(Z):
        val_ref[z] = dot(low, weight_z(own_ref, oth_ref, t, z, 0), 1, 0).astype(BF16)


def mixer_body(
    t, x_ref, gain_ref, dq_ref, dk_ref, val_ref, a_own, a_oth, b_own, b_oth, w_own, w_oth,
    mix_ref, mid_ref, n_ref,
):
    m = pl.program_id(0)
    core = t[0]
    k0 = pl.multiple_of(window(m) * KB, KB)
    mask = halves(dq_ref, core) == dk_ref[:, pl.ds(k0, WIN * KB)]
    heads = head_masks(core, TM)
    acc = halves(x_ref, core).astype(F32)
    for z in range(Z):
        win = val_ref[z, pl.ds(k0, WIN * KB), :]
        out = jnp.zeros((TM, GW), F32)
        for i in range(HZ):
            e = exp_scores(a_own, a_oth, b_own, b_oth, t, m, HZ * z + i, mask)
            inv = 1.0 / jnp.sum(e, axis=-1, keepdims=True)
            part = dot((e * inv).astype(BF16), win, 1, 0)
            out = jnp.where(heads[i], part, out)
        low = out.astype(BF16)
        put_halves(mix_ref, core, low, z)
        acc = acc + dot(low, weight_z(w_own, w_oth, t, z, DB), 1, 1)
    put_halves(mid_ref, core, acc)
    cen, rstd = norm_stats(acc)
    put_halves(n_ref, core, (cen * rstd * gain_ref[1:2, :]).astype(BF16))


def ffn_body(first, last, t, n_ref, c_ref, u_ref, d_ref, *refs):
    refs = list(refs)
    if not first:
        ia_ref, ib_ref = refs[:2]
        refs = refs[2:]
    if last:
        mid_ref = refs[0]
        refs = refs[1:]
    gu_ref, gd_ref, b_ref, a_ref = refs[:4]
    j = pl.program_id(0)
    n = n_ref[...]
    cot = c_ref[...]
    up_w = jnp.concatenate([u_ref[tab_b(t, g), 0] for g in range(G)], axis=0)
    dn_w = jnp.concatenate([d_ref[tab_a(t, g), 0] for g in range(G)], axis=0)

    @pl.when(j == 0)
    def _():
        if first:
            a_ref[...] = jnp.zeros_like(a_ref)
            b_ref[...] = jnp.zeros_like(b_ref)
        else:
            a_ref[...] = ia_ref[...]
            b_ref[...] = ib_ref[...]

    up = dot(n, up_w, 1, 0)
    sq = up * up
    th = jnp.tanh(GC * up * (1.0 + GA * sq))
    half = 0.5 + 0.5 * th
    act = (up * half).astype(BF16)
    slope = half + (0.5 * GC) * up * (1.0 - th * th) * (1.0 + (3.0 * GA) * sq)
    a_ref[...] += dot(act, dn_w, 1, 1)
    gd = dot(cot, act, 0, 0).astype(BF16)
    up_g = (dot(cot, dn_w, 1, 0) * slope).astype(BF16)
    gu = dot(n, up_g, 0, 0).astype(BF16)
    b_ref[...] += dot(up_g, up_w, 1, 1)
    for g in range(G):
        gu_ref[tab_b(t, g), 0] = gu[g * DB : (g + 1) * DB]
        gd_ref[tab_a(t, g), 0] = gd[g * DB : (g + 1) * DB]
    if last:
        lo_ref = refs[4]

        @pl.when(j == Z - 1)
        def _():
            lo_ref[...] = (mid_ref[...] + a_ref[...]).astype(BF16)


def norm_back(cen, rstd, gain, dn):
    xhat = cen * rstd
    e = dn * gain
    dv = (
        e
        - jnp.mean(e, axis=-1, keepdims=True)
        - xhat * jnp.mean(e * xhat, axis=-1, keepdims=True)
    ) * rstd
    return dv, jnp.sum(dn * xhat, axis=0, keepdims=True)


def mixer_back_body(
    t, dn_ref, mid_ref, c_ref, gain_ref, dq_ref, dk_ref, mix_ref, val_ref,
    a_own, a_oth, b_own, b_oth, w_own, w_oth,
    mg_ref, ka_ref, sa_ref, kb_ref, sb_ref, ko_ref, so_ref, vg_ref, dg_acc, go_acc, vg_acc,
):
    m = pl.program_id(0)
    core = t[0]
    start = window(m)
    k0 = pl.multiple_of(start * KB, KB)

    @pl.when(m == 0)
    def _():
        go_acc[...] = jnp.zeros_like(go_acc)
        vg_acc[...] = jnp.zeros_like(vg_acc)
        dg_acc[...] = jnp.zeros_like(dg_acc)

    cen, rstd = norm_stats(halves(mid_ref, core))
    dv, dg = norm_back(cen, rstd, gain_ref[1:2, :], halves(dn_ref, core))
    dg_acc[0:1, :] += dg
    mid_grad = halves(c_ref, core).astype(F32) + dv
    put_halves(mg_ref, core, mid_grad)
    branch = mid_grad.astype(BF16)
    mask = halves(dq_ref, core) == dk_ref[:, pl.ds(k0, WIN * KB)]
    heads = head_masks(core, TM)
    rest = tab_b(t, jnp.where(start == 0, G - 1, 0))
    ka_ref[rest, 0] = jnp.zeros((HR, KB), BF16)
    sa_ref[rest, 0] = jnp.zeros((HR, KB), BF16)
    for z in range(Z):
        go_acc[z] += dot(branch, halves(mix_ref, core, z), 0, 0)
        grad = dot(branch, weight_z(w_own, w_oth, t, z, DB), 1, 0)
        grad = grad.astype(BF16).astype(F32)
        win = val_ref[z, pl.ds(k0, WIN * KB), :]
        total = jnp.zeros((WIN * KB, GW), F32)
        for i in range(HZ):
            head = HZ * z + i
            e = exp_scores(a_own, a_oth, b_own, b_oth, t, m, head, mask)
            inv = 1.0 / jnp.sum(e, axis=-1, keepdims=True)
            prob = e * inv
            mine = jnp.where(heads[i], grad, 0.0).astype(BF16)
            total = total + dot(prob.astype(BF16), mine, 0, 0)
            dp = dot(mine, win, 1, 1)
            pd = prob * dp
            ds = (pd - prob * jnp.sum(pd, axis=-1, keepdims=True)).astype(BF16)
            for k in range(WIN):
                for p, (ra, rb) in enumerate(((ka_ref, kb_ref), (sa_ref, sb_ref))):
                    blk = ds[p * QB : (p + 1) * QB, k * KB : (k + 1) * KB]
                    if head < HA:
                        ra[tab_b(t, start + k), 0, head * QB : (head + 1) * QB, :] = blk
                    else:
                        h = head - HA
                        rb[0, k, h * QB : (h + 1) * QB, :] = blk
        vg_acc[z, pl.ds(k0, WIN * KB), :] += total

    @pl.when(m == Z - 1)
    def _():
        vg_ref[...] = vg_acc[...].astype(BF16)
        put_weight_grads(go_acc, dg_acc[0:1, :], t, ko_ref, so_ref)


def last_body(
    t, x_ref, gain_ref, n_ref, vg_ref, w_own, w_oth, mg_ref, gi_ref, kv_ref, sv_ref, dg_acc, gv_acc
):
    m = pl.program_id(0)

    @pl.when(m == 0)
    def _():
        gv_acc[...] = jnp.zeros_like(gv_acc)
        dg_acc[...] = jnp.zeros_like(dg_acc)

    low = n_ref[...]
    dn = jnp.zeros((TM, D), F32)
    for z in range(Z):
        vg = vg_ref[z]
        gv_acc[z] += dot(low, vg, 0, 0)
        dn = dn + dot(vg, weight_z(w_own, w_oth, t, z, 0), 1, 1)
    cen, rstd = norm_stats(x_ref[...].astype(F32))
    dv, dg = norm_back(cen, rstd, gain_ref[0:1, :], dn)
    dg_acc[0:1, :] += dg
    gi_ref[...] = mg_ref[...] + dv

    @pl.when(m == Z - 1)
    def _():
        put_weight_grads(gv_acc, dg_acc[0:1, :], t, kv_ref, sv_ref)


def sds(shape, dtype):
    return jax.ShapeDtypeStruct(shape, dtype)


W_SHAPE = (G, Z, 2 * DB, LN)
V_SHAPE = (G, Z, DB, LN)
A_SHAPE = (G, Z, HR, KB)
B_SHAPE = (Z, WIN, HR, KB)
F_SHAPE = (G, Z, DB, FB)
Z_ROWS = pl.BlockSpec((Z, TM, GW), lambda i, t: (0, i, 0))


def run_values(tab, x, w):
    return call(
        values_body,
        (L // TM,),
        [rows(D), whole(W_SHAPE), whole(W_SHAPE)],
        [rows(D), Z_ROWS, out_whole((8, D))],
        [sds((L, D), BF16), sds((Z, L, GW), BF16), sds((8, D), F32)],
        flops=2 * L * D * Z * GW,
        nbytes=6 << 20,
    )(tab, x, *w)


def run_mixer(tab, x, gain, dq, dk, vals, a, b, w):
    return call(
        mixer_body,
        (L // TM,),
        [
            rows(D), whole((8, D)), rows(1), whole((1, L)), whole((Z, L, GW)),
            whole(A_SHAPE), whole(A_SHAPE), whole(B_SHAPE), whole(B_SHAPE),
            whole(W_SHAPE), whole(W_SHAPE),
        ],
        [Z_ROWS, rows(D), rows(D)],
        [sds((Z, L, GW), BF16), sds((L, D), F32), sds((L, D), BF16)],
        flops=2 * L * D * Z * GW + 2 * H * L * WIN * KB * GW,
        nbytes=14 << 20,
    )(tab, x, gain, dq, dk, vals, *a, *b, *w)

def run_ffn(tab, n, cot, u_w, d_w, acc=None, mid=None):
    first, last = acc is None, mid is not None
    blk = pl.BlockSpec((G, 1, DB, FB), lambda i, t: (0, i, 0, 0))
    in_specs = [whole((L, D)), whole((L, D)), blk, blk]
    args = [tab, n, cot, u_w, d_w]
    if not first:
        in_specs += [whole((L, D)), whole((L, D))]
        args += list(acc)
    if last:
        in_specs += [whole((L, D))]
        args += [mid]
    out_specs = [blk, blk, out_whole((L, D))]
    outs = [sds(F_SHAPE, BF16), sds(F_SHAPE, BF16), sds((L, D), F32)]
    scratch = ()
    if last:
        scratch = (pltpu.VMEM((L, D), F32),)
        out_specs += [out_whole((L, D))]
        outs += [sds((L, D), BF16)]
    else:
        out_specs += [out_whole((L, D))]
        outs += [sds((L, D), F32)]

    def body(t, *refs):
        if last:
            refs = list(refs)
            refs = refs[:-2] + [refs[-1], refs[-2]]
        ffn_body(first, last, t, *refs)

    return call(
        body, (Z,), in_specs, out_specs, outs, scratch, flops=6 * L * D * FF, nbytes=20 << 20
    )(*args)


def run_mixer_back(tab, dn, mid, cot, gain, dq, dk, mixed, vals, a, b, w):
    blk_a = pl.BlockSpec((G, 1, HR, KB), lambda i, t: (0, tab_z(t, i), 0, 0))
    blk_b = pl.BlockSpec((1, WIN, HR, KB), lambda i, t: (tab_z(t, i), 0, 0, 0))
    return call(
        mixer_back_body,
        (L // TM,),
        [
            rows(D), rows(D), rows(D), whole((8, D)), rows(1), whole((1, L)), Z_ROWS,
            whole((Z, L, GW)), whole(A_SHAPE), whole(A_SHAPE), whole(B_SHAPE), whole(B_SHAPE),
            whole(W_SHAPE), whole(W_SHAPE),
        ],
        [rows(D), blk_a, blk_a, blk_b, blk_b, out_whole(V_SHAPE), out_whole(V_SHAPE), out_whole((Z, L, GW))],
        [
            sds((L, D), F32), sds(A_SHAPE, BF16), sds(A_SHAPE, BF16), sds(B_SHAPE, BF16),
            sds(B_SHAPE, BF16), sds(V_SHAPE, BF16), sds(V_SHAPE, BF16), sds((Z, L, GW), BF16),
        ],
        scratch=(pltpu.VMEM((8, D), F32), pltpu.VMEM((Z, D, GW), F32), pltpu.VMEM((Z, L, GW), F32)),
        flops=4 * L * D * Z * GW + 6 * H * L * WIN * KB * GW,
        nbytes=28 << 20,
    )(tab, dn, mid, cot, gain, dq, dk, mixed, vals, *a, *b, *w)


def run_last(tab, x, gain, low, vg, w, mid_grad):
    return call(
        last_body,
        (L // TM,),
        [rows(D), whole((8, D)), rows(D), Z_ROWS, whole(W_SHAPE), whole(W_SHAPE), rows(D)],
        [rows(D), out_whole(V_SHAPE), out_whole(V_SHAPE)],
        [sds((L, D), F32), sds(V_SHAPE, BF16), sds(V_SHAPE, BF16)],
        scratch=(pltpu.VMEM((8, D), F32), pltpu.VMEM((Z, D, GW), F32)),
        flops=4 * L * D * Z * GW,
        nbytes=12 << 20,
    )(tab, x, gain, low, vg, *w, mid_grad)


def add_up(terms):
    total = terms[0].astype(F32)
    for term in terms[1:]:
        total = total + term.astype(F32)
    return total


class Grid:
    def __init__(self, gx, gy):
        self.gy = gy
        self.size = {"y": gx // 2, "x": 2, "z": gy // 2, "c": 2}
        i, j = lax.axis_index("gx"), lax.axis_index("gy")
        self.at = {"y": i // 2, "x": i % 2, "z": j // 2, "c": j % 2}

    def fetch(self, val, axis, k):
        sizes = self.size
        pairs = []
        for y in range(sizes["y"]):
            for x in range(sizes["x"]):
                for z in range(sizes["z"]):
                    for c in range(sizes["c"]):
                        src = {"y": y, "x": x, "z": z, "c": c}
                        dst = dict(src)
                        dst[axis] = (src[axis] + k) % sizes[axis]
                        pairs.append(tuple((p["y"] * 2 + p["x"]) * self.gy + p["z"] * 2 + p["c"] for p in (src, dst)))
        return lax.ppermute(val, ("gx", "gy"), pairs)

    def rel(self, axis, v):
        return (self.at[axis] - v) % self.size[axis]

    def spread(self, val, axis):
        return jnp.stack([val] + [self.fetch(val, axis, k) for k in range(1, self.size[axis])])

    def reduce(self, terms, axis):
        got = [
            self.fetch(add_up([t[k] for t in terms]).astype(BF16), axis, -k)
            for k in range(1, self.size[axis])
        ]
        return [t[0] for t in terms] + got


def compute(tab, x, docs, cot, a, b, w, u, d):
    dq, dk = docs.reshape(L, 1), docs
    low, vals, gain = run_values(tab, x, w)
    mixed, mid, n_two = run_mixer(tab, x, gain, dq, dk, vals, a, b, w)
    gu0, gd0, acc_b, acc_a = run_ffn(tab, n_two, cot, u[0], d[0])
    gu1, gd1, n_grad, layer_out = run_ffn(tab, n_two, cot, u[1], d[1], (acc_a, acc_b), mid)
    mid_grad, ka, sa, kb, sb, ko, so, vg = run_mixer_back(
        tab, n_grad, mid, cot, gain, dq, dk, mixed, vals, a, b, w
    )
    grad_in, kv, sv = run_last(tab, x, gain, low, vg, w, mid_grad)
    return layer_out, grad_in, (gu0, gu1), (gd0, gd1), (ka, sa), (kb, sb), (ko, so), (kv, sv)


def lane_pad(mat, gains):
    row = jnp.pad(gains.reshape(1, GN), ((0, DB - 1), (0, LN - CB - GN)))
    return jnp.concatenate([mat, row], axis=1)


def small_shards(layer_in, doc_ids, mix_gain, value_w, mixing, output_w, ffn_gain, up_w, down_w, cot):
    grid = Grid(G, 2 * Z)
    at = grid.at
    order_a = [grid.rel("x", g % 2) * 2 + grid.rel("y", g // 2) for g in range(G)]
    order_b = [grid.rel("y", g // 2) * 2 + grid.rel("x", g % 2) for g in range(G)]
    order_z = [grid.rel("z", z) for z in range(Z)]
    tab = jnp.stack([at["c"]] + order_a + order_b + order_z).astype(jnp.int32)
    docs = lax.dynamic_slice_in_dim(doc_ids, lax.axis_index("gy"), 1, 0)

    mix = mixing.reshape(2, HR, KB)
    wts = jnp.concatenate([lane_pad(value_w, mix_gain), lane_pad(output_w.T, ffn_gain)], axis=0)
    first = jnp.concatenate([mix[0], wts], axis=0)
    first = grid.spread(first, "z")
    a = grid.spread(grid.spread(first[:, :HR], "x"), "y").reshape(A_SHAPE)
    w = grid.spread(grid.spread(first[:, HR:], "y"), "x").reshape(W_SHAPE)
    b = grid.spread(grid.spread(mix[1], "x"), "y").reshape(G, HR, KB)
    start = window(at["z"])
    order = jnp.stack(order_b)
    b = jnp.stack([lax.dynamic_index_in_dim(b, order[start + i], 0, False) for i in range(WIN)])
    b = grid.spread(b, "z")
    ffn = grid.spread(jnp.stack([up_w, down_w.T]), "z")
    u = grid.spread(grid.spread(ffn[:, 0], "x"), "y").reshape(F_SHAPE)
    d = grid.spread(grid.spread(ffn[:, 1], "y"), "x").reshape(F_SHAPE)
    a, b, w, u, d = ((v, grid.fetch(v, "c", 1)) for v in (a, b, w, u, d))

    layer_out, grad_in, gu, gd, ga, gb, go, gv = compute(
        tab, layer_in, docs, cot, a, b, w, u, d
    )

    def core_sum(pair):
        return [pair[0], grid.fetch(pair[1], "c", 1)]

    def split(vals, *lead):
        return [v.reshape(lead + v.shape[-3:]) for v in vals]

    up = grid.reduce(grid.reduce(split(core_sum(gu), 2, 2), "y"), "x")
    dn = grid.reduce(grid.reduce(split(core_sum(gd), 2, 2), "x"), "y")
    both = [jnp.stack([p, q], axis=1) for p, q in zip(up, dn)]
    ffn = add_up(grid.reduce(both, "z"))
    gb = core_sum(gb)
    gb = grid.reduce(gb, "z")
    wide = []
    for v in gb:
        blocks = []
        for k in range(G):
            y = (at["y"] - k // 2) % 2
            x = (at["x"] - k % 2) % 2
            spot = y * 2 + x - start
            blk = lax.dynamic_index_in_dim(v, jnp.clip(spot, 0, WIN - 1), 0, False)
            ok = jnp.logical_and(spot >= 0, spot < WIN)
            blocks.append(jnp.where(ok, blk, jnp.zeros_like(blk)))
        wide.append(jnp.stack(blocks).reshape(2, 2, HR, KB))
    gb = add_up(grid.reduce(grid.reduce(wide, "y"), "x"))
    ga = split(core_sum(ga), 2, 2)
    ga = add_up(grid.reduce(grid.reduce(grid.reduce(ga, "y"), "x"), "z"))
    go, gv = core_sum(go), core_sum(gv)
    gw = split([jnp.concatenate([p, q], axis=2) for p, q in zip(gv, go)], 2, 2)
    gw = add_up(grid.reduce(grid.reduce(grid.reduce(gw, "x"), "y"), "z"))

    grad_mixing = jnp.concatenate([ga, gb], axis=0).reshape(H, QB, KB)
    return (
        layer_out, grad_in, gw[0, CB : CB + GN], gw[:DB, :CB], grad_mixing, gw[DB:, :CB].T,
        gw[DB, CB : CB + GN], ffn[0], ffn[1].T,
    )


def cols_in(v, o, gains):
    def blocks(mat, gain):
        mat = mat.reshape(G, DB, Z, 2, CB).transpose(3, 0, 2, 1, 4)
        gain = gain.reshape(G, Z, 2, 1, GN).transpose(2, 0, 1, 3, 4)
        gain = jnp.pad(gain, ((0, 0),) * 3 + ((0, DB - 1), (0, LN - CB - GN)))
        return jnp.concatenate([mat, gain], axis=-1)

    return jnp.concatenate([blocks(v, gains[0]), blocks(o, gains[1])], axis=3)


def cols_out(keep, send):
    mat = jnp.stack([keep, send])
    dg = mat[:, :, :, 0, CB : CB + GN].transpose(1, 2, 0, 3).reshape(D)
    return mat[..., :CB].transpose(1, 3, 2, 0, 4).reshape(D, D), dg


def any_shards(layer_in, doc_ids, mix_gain, value_w, mixing, output_w, ffn_gain, up_w, down_w, cot):
    ax = ("gx", "gy")
    seqs = layer_in.shape[0] // L
    me = lax.axis_index("gy") * seqs

    def gather(arr, d0, d1):
        arr = lax.all_gather(arr, "gx", axis=d0, tiled=True)
        return lax.all_gather(arr, "gy", axis=d1, tiled=True)

    def scatter(arr, d0, d1):
        arr = lax.psum_scatter(arr, "gx", scatter_dimension=d0, tiled=True)
        return lax.psum_scatter(arr, "gy", scatter_dimension=d1, tiled=True).astype(F32)

    gains = lax.all_gather(jnp.stack([mix_gain, ffn_gain]), ax, axis=1, tiled=True)
    w = cols_in(gather(value_w, 0, 1), gather(output_w.T, 0, 1), gains)
    mix_full = gather(mixing, 2, 1).reshape(2, HA, Z, 2, QB, G, KB).transpose(0, 3, 5, 2, 1, 4, 6)
    mix_full = mix_full.reshape(2, 2, G, Z, HR, KB)
    a = mix_full[0]
    starts = [min(max(m - 1, 0), G - WIN) for m in range(Z)]
    b = jnp.stack([mix_full[1][:, s : s + WIN, m] for m, s in enumerate(starts)], axis=1)
    u = gather(up_w, 0, 1).reshape(G, DB, Z, 2, FB).transpose(3, 0, 2, 1, 4)
    d = gather(down_w.T, 0, 1).reshape(G, DB, Z, 2, FB).transpose(3, 0, 2, 1, 4)
    tab = jnp.array([0] + [0, 1, 2, 3] * 3, jnp.int32)

    rows_out, grads = [], None
    for s in range(seqs):
        docs = lax.dynamic_slice_in_dim(doc_ids, me + s, 1, 0)
        part = slice(s * L, (s + 1) * L)
        out, g_in, *rest = compute(tab, layer_in[part], docs, cot[part], a, b, w, u, d)
        rows_out.append((out, g_in))
        rest = jax.tree.map(lambda v: v.astype(F32), rest) if seqs > 1 else rest
        grads = rest if grads is None else jax.tree.map(jnp.add, grads, rest)
    layer_out = jnp.concatenate([r[0] for r in rows_out], axis=0)
    grad_in = jnp.concatenate([r[1] for r in rows_out], axis=0)
    gu, gd, ga, gb, go, gv = jax.tree.map(lambda v: v.astype(BF16), grads)

    def ffn_out(pair):
        return jnp.stack(pair).transpose(1, 3, 2, 0, 4).reshape(D, FF)

    value_full, dg_one = cols_out(*gv)
    output_full, dg_two = cols_out(*go)
    ga, gb = jnp.stack(ga), jnp.stack(gb)
    gb = jnp.stack(
        [
            jnp.pad(gb[:, m], ((0, 0), (s, G - WIN - s), (0, 0), (0, 0)))
            for m, s in enumerate(starts)
        ],
        axis=2,
    )
    gm = jnp.stack([ga, gb]).reshape(2, 2, G, Z, HA, QB, KB).transpose(0, 4, 3, 1, 5, 2, 6)
    dgs = jnp.stack([dg_one, dg_two]).astype(F32)
    dgs = lax.psum_scatter(dgs, ax, scatter_dimension=1, tiled=True)
    return (
        layer_out, grad_in, dgs[0], scatter(value_full, 0, 1), scatter(gm.reshape(H, L, L), 2, 1),
        scatter(output_full, 0, 1).T, dgs[1], scatter(ffn_out(gu), 0, 1), scatter(ffn_out(gd), 0, 1).T,
    )


def solution(mesh):
    tok = P(("gx", "gy"), None)
    vec = P(("gx", "gy"))
    wgt = P("gx", "gy")
    twg = P("gy", "gx")
    mix = P(None, "gy", "gx")
    in_specs = (tok, P("gx", None), vec, wgt, mix, twg, vec, wgt, twg, tok)
    out_specs = (tok, tok, vec, wgt, mix, twg, vec, wgt, twg)

    def run(*args):
        small = (mesh.shape["gx"], mesh.shape["gy"], args[0].shape[0]) == (G, 2 * Z, L)
        return (small_shards if small else any_shards)(*args)

    return jax.shard_map(run, mesh=mesh, in_specs=in_specs, out_specs=out_specs, check_vma=False)
```

```python
import functools

import jax
import jax.numpy as jnp
from jax import lax
from jax.experimental import pallas as pl
from jax.experimental.pallas import tpu as pltpu
from jax.sharding import PartitionSpec as P

D = 768
H = 12
HS = 64
FF = 3072
L = 512
EPS = 1e-05
G = 4
Z = 4
DB = D // G
CB = D // (2 * Z)
FB = FF // (2 * Z)
QB = L // (2 * Z)
KB = L // G
LN = 128
GW = 2 * LN
GN = CB // 4
HA = H // 2
HR = HA * QB
TM = 128
WIN = 3
HZ = H // Z
GC = 0.7978845608
GA = 0.044715
VMEM_LIMIT = 52 * 1024 * 1024
COST = 1 << 36

F32 = jnp.float32
BF16 = jnp.bfloat16


def dot(a, b, ca, cb):
    return lax.dot_general(a, b, (((ca,), (cb,)), ((), ())), preferred_element_type=F32)


def call(body, grid, in_specs, out_specs, out_shape, scratch=(), flops=0, nbytes=0):
    return pl.pallas_call(
        body,
        grid_spec=pltpu.PrefetchScalarGridSpec(
            num_scalar_prefetch=1,
            grid=grid,
            in_specs=in_specs,
            out_specs=out_specs,
            scratch_shapes=list(scratch),
        ),
        out_shape=out_shape,
        compiler_params=pltpu.CompilerParams(
            dimension_semantics=("arbitrary",) * len(grid), vmem_limit_bytes=VMEM_LIMIT
        ),
        cost_estimate=pl.CostEstimate(flops=COST, bytes_accessed=nbytes, transcendentals=0),
    )


def whole(shape):
    zeros = (0,) * len(shape)
    return pl.BlockSpec(shape, lambda i, t: zeros, pipeline_mode=pl.Buffered(1))


def rows(width):
    return pl.BlockSpec((TM, width), lambda i, t: (i, 0))


def out_whole(shape):
    zeros = (0,) * len(shape)
    return pl.BlockSpec(shape, lambda i, t: zeros)


def tab_a(t, g):
    return t[1 + g]


def tab_b(t, g):
    return t[1 + G + g]


def tab_z(t, z):
    return t[1 + 2 * G + z]


def norm_stats(x):
    mean = jnp.mean(x, axis=-1, keepdims=True)
    cen = x - mean
    rstd = lax.rsqrt(jnp.mean(cen * cen, axis=-1, keepdims=True) + EPS)
    return cen, rstd


def weight_z(own, oth, t, z, base, tab=tab_a):
    parts = [
        jnp.concatenate(
            [ref[tab(t, g), tab_z(t, z), base : base + DB, :] for g in range(G)], axis=0
        )
        for ref in (own, oth)
    ]
    return jnp.concatenate(parts, axis=1)


def head_masks(core, nrows):
    lane = lax.broadcasted_iota(jnp.int32, (nrows, GW), 1)
    tile = lane // LN
    place = lane - tile * LN
    side = jnp.where(core == 0, tile, 1 - tile)
    col = jnp.where(place < CB, side * CB + place, -1)
    return [jnp.logical_and(col >= HS * i, col < HS * (i + 1)) for i in range(HZ)]


def halves(ref, core, lead=None):
    lo = pl.multiple_of(core * QB, QB)
    hi = pl.multiple_of((1 - core) * QB, QB)
    if lead is None:
        return jnp.concatenate([ref[pl.ds(lo, QB), :], ref[pl.ds(hi, QB), :]], axis=0)
    return jnp.concatenate([ref[lead, pl.ds(lo, QB), :], ref[lead, pl.ds(hi, QB), :]], axis=0)


def put_halves(ref, core, val, lead=None):
    lo = pl.multiple_of(core * QB, QB)
    hi = pl.multiple_of((1 - core) * QB, QB)
    if lead is None:
        ref[pl.ds(lo, QB), :] = val[:QB]
        ref[pl.ds(hi, QB), :] = val[QB:]
    else:
        ref[lead, pl.ds(lo, QB), :] = val[:QB]
        ref[lead, pl.ds(hi, QB), :] = val[QB:]


def window(m):
    return jnp.clip(m - 1, 0, G - WIN)


def block_at(banded, tab, t, m, i):
    return (tab_z(t, m), i) if banded else (tab(t, window(m) + i), tab_z(t, m))


def exp_scores(banded, own, oth, t, m, local, mask):
    parts = []
    for i in range(WIN):
        at = block_at(banded, tab_b, t, m, i) + (slice(local * QB, (local + 1) * QB),)
        parts.append(jnp.concatenate([own[at], oth[at]], axis=0))
    scores = jnp.concatenate(parts, axis=1).astype(F32)
    return jnp.where(mask, jnp.exp(scores), 0.0)


def gain_spots():
    for g in range(G):
        for z in range(Z):
            for c in range(2):
                yield g, z, c, DB * g + (2 * GN) * z + GN * c


def pick(core, c, own, oth):
    return jnp.where(core == c, own, oth)


def gains_row(own, oth, t, base):
    lane = lax.broadcasted_iota(jnp.int32, (1, LN), 1)
    tiles = [jnp.zeros((1, LN), F32) for _ in range(D // LN)]
    for g, z, c, at in gain_spots():
        a, b = (r[tab_a(t, g), tab_z(t, z), base : base + 16, :].astype(F32)[:1] for r in (own, oth))
        row = pick(t[0], c, a, b)
        tile, off = at // LN, at % LN
        row = pltpu.roll(row, (off - CB) % LN, 1)
        tiles[tile] = jnp.where(jnp.logical_and(lane >= off, lane < off + GN), row, tiles[tile])
        if off + GN > LN:
            tiles[tile + 1] = jnp.where(lane < off + GN - LN, row, tiles[tile + 1])
    return jnp.concatenate(tiles, axis=1)


def put_weight_grads(acc, dg, t, keep, send, tab):
    lane = lax.broadcasted_iota(jnp.int32, (1, LN), 1)
    top = lax.broadcasted_iota(jnp.int32, (16, LN), 0) == 0
    spot = jnp.logical_and(top, jnp.logical_and(lane >= CB, lane < CB + GN))
    rows_of = {}
    for g, z, c, at in gain_spots():
        tile, off = at // LN, at % LN
        row = dg[:, tile * LN : (tile + 1) * LN]
        if off + GN > LN:
            row = jnp.where(lane < off, dg[:, (tile + 1) * LN : (tile + 2) * LN], row)
        rows_of[g, z, c] = pltpu.roll(row, (CB - off) % LN, 1)
    for g in range(G):
        for z in range(Z):
            for p, ref in ((0, keep), (1, send)):
                blk = acc[z, g * DB : (g + 1) * DB, p * LN : (p + 1) * LN]
                row = pick(t[0], p, rows_of[g, z, 0], rows_of[g, z, 1])
                ref[tab(t, g), tab_z(t, z)] = blk.astype(BF16)
                ref[tab(t, g), tab_z(t, z), 0:16, :] = jnp.where(spot, row, blk[:16]).astype(BF16)


def values_body(t, x_ref, own_ref, oth_ref, n_ref, val_ref, gain_ref):
    @pl.when(pl.program_id(0) == 0)
    def _():
        gain_ref[0:1, :] = gains_row(own_ref, oth_ref, t, 0)
        gain_ref[1:2, :] = gains_row(own_ref, oth_ref, t, DB)

    cen, rstd = norm_stats(x_ref[...].astype(F32))
    low = (cen * rstd * gain_ref[0:1, :]).astype(BF16)
    n_ref[...] = low
    for z in range(Z):
        val_ref[z] = dot(low, weight_z(own_ref, oth_ref, t, z, 0), 1, 0).astype(BF16)


def mixer_body(last, t, x_ref, gain_ref, dq_ref, dk_ref, val_ref, own, oth, *refs):
    if last:
        first_ref, w_own, w_oth, mix_ref, mid_ref, n_ref = refs
    else:
        (mix_ref,) = refs
    m = pl.program_id(0)
    core = t[0]
    k0 = pl.multiple_of(window(m) * KB, KB)
    mask = halves(dq_ref, core) == dk_ref[:, pl.ds(k0, WIN * KB)]
    heads = head_masks(core, TM)
    lows = []
    for j in range(Z // 2):
        win = val_ref[j, pl.ds(k0, WIN * KB), :]
        out = jnp.zeros((TM, GW), F32)
        for i in range(HZ):
            e = exp_scores(last, own, oth, t, m, HZ * j + i, mask)
            inv = 1.0 / jnp.sum(e, axis=-1, keepdims=True)
            part = dot((e * inv).astype(BF16), win, 1, 0)
            out = jnp.where(heads[i], part, out)
        low = out.astype(BF16)
        put_halves(mix_ref, core, low, j)
        lows.append(low)
    if last:
        acc = halves(x_ref, core).astype(F32)
        lows = [halves(first_ref, core, j) for j in range(Z // 2)] + lows
        for z in range(Z):
            acc = acc + dot(lows[z], weight_z(w_own, w_oth, t, z, DB), 1, 1)
        put_halves(mid_ref, core, acc)
        cen, rstd = norm_stats(acc)
        put_halves(n_ref, core, (cen * rstd * gain_ref[1:2, :]).astype(BF16))


def ffn_body(first, last, tab, t, n_ref, c_ref, own, oth, *refs):
    refs = list(refs)
    if not first:
        ia_ref, ib_ref = refs[:2]
        refs = refs[2:]
    if last:
        mid_ref = refs[0]
        refs = refs[1:]
    keep, send, a_ref, b_ref = refs[:4]
    j = pl.program_id(0)
    n = n_ref[...]
    cot = c_ref[...]

    def weights(base):
        return jnp.concatenate(
            [
                jnp.concatenate([r[tab(t, g), 0, base : base + DB, :] for g in range(G)], axis=0)
                for r in (own, oth)
            ],
            axis=1,
        )

    up_w, dn_w = weights(0), weights(DB)

    @pl.when(j == 0)
    def _():
        if first:
            a_ref[...] = jnp.zeros_like(a_ref)
            b_ref[...] = jnp.zeros_like(b_ref)
        else:
            a_ref[...] = ia_ref[...]
            b_ref[...] = ib_ref[...]

    up = dot(n, up_w, 1, 0)
    sq = up * up
    th = jnp.tanh(GC * up * (1.0 + GA * sq))
    half = 0.5 + 0.5 * th
    act = (up * half).astype(BF16)
    slope = half + (0.5 * GC) * up * (1.0 - th * th) * (1.0 + (3.0 * GA) * sq)
    a_ref[...] += dot(act, dn_w, 1, 1)
    gd = dot(cot, act, 0, 0).astype(BF16)
    up_g = (dot(cot, dn_w, 1, 0) * slope).astype(BF16)
    gu = dot(n, up_g, 0, 0).astype(BF16)
    b_ref[...] += dot(up_g, up_w, 1, 1)
    for p, ref in ((0, keep), (1, send)):
        for g in range(G):
            part = slice(g * DB, (g + 1) * DB), slice(p * LN, (p + 1) * LN)
            ref[tab(t, g), 0, 0:DB, :] = gu[part]
            ref[tab(t, g), 0, DB : 2 * DB, :] = gd[part]
    if last:
        lo_ref = refs[4]

        @pl.when(j == Z - 1)
        def _():
            lo_ref[...] = (mid_ref[...] + a_ref[...]).astype(BF16)


def norm_back(cen, rstd, gain, dn):
    xhat = cen * rstd
    e = dn * gain
    dv = (
        e
        - jnp.mean(e, axis=-1, keepdims=True)
        - xhat * jnp.mean(e * xhat, axis=-1, keepdims=True)
    ) * rstd
    return dv, jnp.sum(dn * xhat, axis=0, keepdims=True)


def branch_body(
    t, dn_ref, mid_ref, c_ref, gain_ref, mixa_ref, mixb_ref, w_own, w_oth,
    mg_ref, grad_ref, keep, send, dg_acc, go_acc,
):
    m = pl.program_id(0)

    @pl.when(m == 0)
    def _():
        go_acc[...] = jnp.zeros_like(go_acc)
        dg_acc[...] = jnp.zeros_like(dg_acc)

    cen, rstd = norm_stats(mid_ref[...])
    dv, dg = norm_back(cen, rstd, gain_ref[1:2, :], dn_ref[...])
    dg_acc[0:1, :] += dg
    mid_grad = c_ref[...].astype(F32) + dv
    mg_ref[...] = mid_grad
    branch = mid_grad.astype(BF16)
    for z in range(Z):
        mix = mixa_ref[z] if z < Z // 2 else mixb_ref[z - Z // 2]
        go_acc[z] += dot(branch, mix, 0, 0)
        grad_ref[z] = dot(branch, weight_z(w_own, w_oth, t, z, DB), 1, 0).astype(BF16)

    @pl.when(m == Z - 1)
    def _():
        put_weight_grads(go_acc, dg_acc[0:1, :], t, keep, send, tab_a)


def mixer_back_body(banded, t, grad_ref, dq_ref, dk_ref, val_ref, own, oth, keep, send, vg_ref, vg_acc):
    m = pl.program_id(0)
    core = t[0]
    start = window(m)
    k0 = pl.multiple_of(start * KB, KB)

    @pl.when(m == 0)
    def _():
        vg_acc[...] = jnp.zeros_like(vg_acc)

    mask = halves(dq_ref, core) == dk_ref[:, pl.ds(k0, WIN * KB)]
    heads = head_masks(core, TM)
    if not banded:
        rest = tab_b(t, jnp.where(start == 0, G - 1, 0))
        keep[rest, 0] = jnp.zeros((HR, KB), BF16)
        send[rest, 0] = jnp.zeros((HR, KB), BF16)
    for j in range(Z // 2):
        grad = halves(grad_ref, core, j)
        win = val_ref[j, pl.ds(k0, WIN * KB), :]
        total = jnp.zeros((WIN * KB, GW), F32)
        for i in range(HZ):
            local = HZ * j + i
            e = exp_scores(banded, own, oth, t, m, local, mask)
            inv = 1.0 / jnp.sum(e, axis=-1, keepdims=True)
            prob = e * inv
            mine = jnp.where(heads[i], grad, jnp.zeros_like(grad))
            total = total + dot(prob.astype(BF16), mine, 0, 0)
            dp = dot(mine, win, 1, 1)
            pd = prob * dp
            ds = (pd - prob * jnp.sum(pd, axis=-1, keepdims=True)).astype(BF16)
            for k in range(WIN):
                at = (0, k) if banded else (tab_b(t, start + k), 0)
                at = at + (slice(local * QB, (local + 1) * QB),)
                for p, ref in ((0, keep), (1, send)):
                    ref[at] = ds[p * QB : (p + 1) * QB, k * KB : (k + 1) * KB]
        vg_acc[j, pl.ds(k0, WIN * KB), :] += total

    @pl.when(m == Z - 1)
    def _():
        vg_ref[...] = vg_acc[...].astype(BF16)


def last_body(
    t, x_ref, gain_ref, n_ref, vga_ref, vgb_ref, w_own, w_oth, mg_ref, gi_ref, keep, send, dg_acc, gv_acc
):
    m = pl.program_id(0)

    @pl.when(m == 0)
    def _():
        gv_acc[...] = jnp.zeros_like(gv_acc)
        dg_acc[...] = jnp.zeros_like(dg_acc)

    low = n_ref[...]
    dn = jnp.zeros((TM, D), F32)
    for z in range(Z):
        vg = vga_ref[z] if z < Z // 2 else vgb_ref[z - Z // 2]
        gv_acc[z] += dot(low, vg, 0, 0)
        dn = dn + dot(vg, weight_z(w_own, w_oth, t, z, 0), 1, 1)
    cen, rstd = norm_stats(x_ref[...].astype(F32))
    dv, dg = norm_back(cen, rstd, gain_ref[0:1, :], dn)
    dg_acc[0:1, :] += dg
    gi_ref[...] = mg_ref[...] + dv

    @pl.when(m == Z - 1)
    def _():
        put_weight_grads(gv_acc, dg_acc[0:1, :], t, keep, send, tab_a)


def sds(shape, dtype):
    return jax.ShapeDtypeStruct(shape, dtype)


U_SHAPE = (G, Z, 2 * DB, LN)
V_SHAPE = (G, Z, DB, LN)
B_SHAPE = (Z, WIN, HR, KB)
H_SHAPE = (Z // 2, L, GW)
Z_ROWS = pl.BlockSpec((Z, TM, GW), lambda i, t: (0, i, 0))
H_ROWS = pl.BlockSpec((Z // 2, TM, GW), lambda i, t: (0, i, 0))


def half(i):
    return pl.BlockSpec(H_SHAPE, lambda j, t: (i, 0, 0), pipeline_mode=pl.Buffered(1))


def half_rows(i):
    return pl.BlockSpec((Z // 2, TM, GW), lambda j, t: (i, j, 0))


def run_values(tab, x, w):
    return call(
        values_body,
        (L // TM,),
        [rows(D), whole(U_SHAPE), whole(U_SHAPE)],
        [rows(D), Z_ROWS, out_whole((8, D))],
        [sds((L, D), BF16), sds((Z, L, GW), BF16), sds((8, D), F32)],
        flops=2 * L * D * Z * GW,
        nbytes=6 << 20,
    )(tab, x, *w)


def run_mixer(tab, i, x, gain, dq, dk, vals, unit, first=None, w=None):
    last = first is not None
    shape = B_SHAPE if last else U_SHAPE
    in_specs = [
        rows(D), whole((8, D)), rows(1), whole((1, L)), half(i), whole(shape), whole(shape),
    ]
    args = [tab, x, gain, dq, dk, vals, *unit]
    out_specs, outs = [H_ROWS], [sds(H_SHAPE, BF16)]
    if last:
        in_specs += [H_ROWS, whole(U_SHAPE), whole(U_SHAPE)]
        args += [first, *w]
        out_specs += [rows(D), rows(D)]
        outs += [sds((L, D), F32), sds((L, D), BF16)]
    return call(
        functools.partial(mixer_body, last),
        (L // TM,),
        in_specs,
        out_specs,
        outs,
        flops=H * L * WIN * KB * GW,
        nbytes=9 << 20,
    )(*args)


def run_ffn(tab, order, n, cot, unit, acc=None, mid=None):
    first, last = acc is None, mid is not None
    blk = pl.BlockSpec((G, 1, 2 * DB, LN), lambda i, t: (0, i, 0, 0))
    in_specs = [whole((L, D)), whole((L, D)), blk, blk]
    args = [tab, n, cot, *unit]
    if not first:
        in_specs += [whole((L, D)), whole((L, D))]
        args += list(acc)
    if last:
        in_specs += [whole((L, D))]
        args += [mid]
    out_specs = [blk, blk, out_whole((L, D)), out_whole((L, D))]
    outs = [sds(U_SHAPE, BF16), sds(U_SHAPE, BF16), sds((L, D), F32), sds((L, D), F32)]
    if last:
        out_specs += [out_whole((L, D))]
        outs += [sds((L, D), BF16)]
    return call(
        functools.partial(ffn_body, first, last, order), (Z,), in_specs, out_specs, outs,
        flops=4 * L * D * FF, nbytes=14 << 20,
    )(*args)


def run_branch(tab, dn, mid, cot, gain, mixed_a, mixed_b, w):
    return call(
        branch_body,
        (L // TM,),
        [
            rows(D), rows(D), rows(D), whole((8, D)), H_ROWS, H_ROWS,
            whole(U_SHAPE), whole(U_SHAPE),
        ],
        [rows(D), Z_ROWS, out_whole(V_SHAPE), out_whole(V_SHAPE)],
        [sds((L, D), F32), sds((Z, L, GW), BF16), sds(V_SHAPE, BF16), sds(V_SHAPE, BF16)],
        scratch=(pltpu.VMEM((8, D), F32), pltpu.VMEM((Z, D, GW), F32)),
        flops=4 * L * D * Z * GW,
        nbytes=12 << 20,
    )(tab, dn, mid, cot, gain, mixed_a, mixed_b, *w)


def run_mixer_back(tab, banded, grad, dq, dk, vals, unit):
    i = int(banded)
    shape = B_SHAPE if banded else U_SHAPE
    if banded:
        blk = pl.BlockSpec((1, WIN, HR, KB), lambda j, t: (tab_z(t, j), 0, 0, 0))
    else:
        blk = pl.BlockSpec((G, 1, HR, KB), lambda j, t: (0, tab_z(t, j), 0, 0))
    return call(
        functools.partial(mixer_back_body, banded),
        (L // TM,),
        [half_rows(i), rows(1), whole((1, L)), half(i), whole(shape), whole(shape)],
        [blk, blk, out_whole(H_SHAPE)],
        [sds(shape, BF16), sds(shape, BF16), sds(H_SHAPE, BF16)],
        scratch=(pltpu.VMEM(H_SHAPE, F32),),
        flops=3 * H * L * WIN * KB * GW,
        nbytes=10 << 20,
    )(tab, grad, dq, dk, vals, *unit)


def run_last(tab, x, gain, low, vga, vgb, w, mid_grad):
    return call(
        last_body,
        (L // TM,),
        [rows(D), whole((8, D)), rows(D), H_ROWS, H_ROWS, whole(U_SHAPE), whole(U_SHAPE), rows(D)],
        [rows(D), out_whole(V_SHAPE), out_whole(V_SHAPE)],
        [sds((L, D), F32), sds(V_SHAPE, BF16), sds(V_SHAPE, BF16)],
        scratch=(pltpu.VMEM((8, D), F32), pltpu.VMEM((Z, D, GW), F32)),
        flops=4 * L * D * Z * GW,
        nbytes=12 << 20,
    )(tab, x, gain, low, vga, vgb, *w, mid_grad)


def add_up(terms):
    total = terms[0].astype(F32)
    for term in terms[1:]:
        total = total + term.astype(F32)
    return total


def after(val, *deps):
    return lax.optimization_barrier((val, deps))[0]


class Grid:
    def __init__(self, gx, gy):
        self.gy = gy
        self.size = {"y": gx // 2, "x": 2, "z": gy // 2, "c": 2}
        i, j = lax.axis_index("gx"), lax.axis_index("gy")
        self.at = {"y": i // 2, "x": i % 2, "z": j // 2, "c": j % 2}

    def fetch(self, val, axis, k):
        sizes = self.size
        pairs = []
        for y in range(sizes["y"]):
            for x in range(sizes["x"]):
                for z in range(sizes["z"]):
                    for c in range(sizes["c"]):
                        src = {"y": y, "x": x, "z": z, "c": c}
                        dst = dict(src)
                        dst[axis] = (src[axis] + k) % sizes[axis]
                        pairs.append(tuple((p["y"] * 2 + p["x"]) * self.gy + p["z"] * 2 + p["c"] for p in (src, dst)))
        return lax.ppermute(val, ("gx", "gy"), pairs)

    def rel(self, axis, v):
        return (self.at[axis] - v) % self.size[axis]

    def spread(self, val, axis):
        return jnp.stack([val] + [self.fetch(val, axis, k) for k in range(1, self.size[axis])])

    def reduce(self, terms, axis):
        got = [
            self.fetch(add_up([t[k] for t in terms]).astype(BF16), axis, -k)
            for k in range(1, self.size[axis])
        ]
        return [t[0] for t in terms] + got


def lane_pad(mat, gains):
    row = jnp.pad(gains.reshape(1, GN), ((0, DB - 1), (0, LN - CB - GN)))
    return jnp.concatenate([mat, row], axis=1)


def small_shards(layer_in, doc_ids, mix_gain, value_w, mixing, output_w, ffn_gain, up_w, down_w, cot):
    grid = Grid(G, 2 * Z)
    at = grid.at
    fetch, spread = grid.fetch, grid.spread
    order_a = [grid.rel("x", g % 2) * 2 + grid.rel("y", g // 2) for g in range(G)]
    order_b = [grid.rel("y", g // 2) * 2 + grid.rel("x", g % 2) for g in range(G)]
    order_z = [grid.rel("z", z) for z in range(Z)]
    tab = jnp.stack([at["c"]] + order_a + order_b + order_z).astype(jnp.int32)
    docs = lax.dynamic_slice_in_dim(doc_ids, lax.axis_index("gy"), 1, 0)
    dq, dk = docs.reshape(L, 1), docs

    mix = mixing.reshape(2, HR, KB)
    wts = jnp.concatenate([lane_pad(value_w, mix_gain), lane_pad(output_w.T, ffn_gain)], axis=0)
    down_t = down_w.T
    ffn = [
        jnp.concatenate([m[:, i * LN : (i + 1) * LN] for m in (up_w, down_t)], axis=0)
        for i in range(FB // LN)
    ]

    def cross(p, q, *deps):
        p, q = after((p, q), *deps)
        p, q = spread(p, "x"), spread(q, "y")
        return spread(p, "y").reshape(U_SHAPE), spread(q, "x").reshape(U_SHAPE)

    def both(val, *deps):
        return val, fetch(after(val, *deps), "c", 1)

    def tail_to(vals, *deps):
        return list(after(tuple(vals), *deps))

    c1 = spread(jnp.stack([mix[0], wts]), "z")
    b = spread(spread(mix[1], "x"), "y").reshape(G, HR, KB)
    start = window(at["z"])
    order = jnp.stack(order_b)
    b = jnp.stack([lax.dynamic_index_in_dim(b, order[start + i], 0, False) for i in range(WIN)])
    a, w = cross(c1[:, 0], c1[:, 1])
    b = spread(after(b, c1), "z")
    w = both(w)
    a = both(a)
    low, vals, gain = run_values(tab, layer_in, w)
    f1 = spread(after(ffn[0], b), "z")
    b = both(b)
    f1 = spread(after(f1, a[0], w[0]), "y")
    mixed_a = run_mixer(tab, 0, layer_in, gain, dq, dk, vals, a)[0]
    f23 = spread(after(jnp.stack([ffn[1], ffn[2]]), f1, low), "z")
    f1 = spread(f1, "x").reshape(U_SHAPE)
    f2, f3 = cross(f23[:, 0], f23[:, 1], mixed_a)
    mixed_b, mid, n_two = run_mixer(tab, 1, layer_in, gain, dq, dk, vals, b, mixed_a, w)
    f1 = both(f1)
    f2, f3 = both(f2, n_two), both(f3, n_two)

    def split(*pair):
        return [v.reshape((2, 2) + v.shape[1:]) for v in pair]

    k1, s1, *acc = run_ffn(tab, tab_a, n_two, cot, f1)
    r1 = fetch(s1, "c", 1)
    k2, s2, *acc = run_ffn(tab, tab_b, n_two, cot, f2, acc)
    g1 = grid.reduce(tail_to(split(k1, r1), s2), "x")
    r2 = fetch(s2, "c", 1)
    k3, s3, _, n_grad, layer_out = run_ffn(tab, tab_a, after(n_two, r1), cot, f3, acc, mid)
    n_grad = after(n_grad, g1, r2)
    g1 = grid.reduce(tail_to(g1, s3), "y")
    g2 = grid.reduce(tail_to(split(k2, r2), s3), "y")
    r3 = fetch(s3, "c", 1)
    mid_grad, grad, ko, so = run_branch(tab, n_grad, mid, cot, gain, mixed_a, mixed_b, w)
    ro = fetch(so, "c", 1)
    g3 = grid.reduce(tail_to(split(k3, r3), so), "x")
    kb, sb, vgb = run_mixer_back(tab, True, after(grad, g1, r3), dq, dk, vals, b)
    rb = fetch(sb, "c", 1)
    g2 = grid.reduce(tail_to(g2, sb), "x")
    go = grid.reduce(tail_to(split(ko, ro), sb), "x")
    ka, sa, vga = run_mixer_back(tab, False, after(grad, g2[:-1], ro), dq, dk, vals, a)
    ra = fetch(sa, "c", 1)
    gb = grid.reduce(tail_to((kb, rb), sa), "z")
    g3 = grid.reduce(tail_to(g3, sa), "y")
    go = grid.reduce(tail_to(go, sa), "y")
    low = after(low, g3[:-1], rb, g2, go[:-1])
    grad_in, kv, sv = run_last(tab, layer_in, gain, low, vga, vgb, w, mid_grad)
    rv = fetch(sv, "c", 1)
    ga = grid.reduce(split(ka, ra), "y")
    gf = [jnp.stack(v, axis=1) for v in zip(g1, g2, g3)]
    gf = add_up(grid.reduce(tail_to(gf, gb), "z"))
    wide = []
    for v in gb:
        blocks = []
        for k in range(G):
            spot = (at["y"] - k // 2) % 2 * 2 + (at["x"] - k % 2) % 2 - start
            blk = lax.dynamic_index_in_dim(v, jnp.clip(spot, 0, WIN - 1), 0, False)
            ok = jnp.logical_and(spot >= 0, spot < WIN)
            blocks.append(jnp.where(ok, blk, jnp.zeros_like(blk)))
        wide.append(jnp.stack(blocks).reshape(2, 2, HR, KB))
    gv = grid.reduce(split(kv, rv), "x")
    gb = add_up(grid.reduce(grid.reduce(wide, "y"), "x"))
    ga = grid.reduce(ga, "x")
    gv = grid.reduce(gv, "y")
    gm = [jnp.concatenate(v, axis=1) for v in zip(ga, go, gv)]
    gm = add_up(grid.reduce(gm, "z"))

    go, gv = gm[HR : HR + DB], gm[HR + DB :]
    grad_mixing = jnp.concatenate([gm[:HR], gb], axis=0).reshape(H, QB, KB)
    grad_up = jnp.concatenate([gf[i, :DB] for i in range(FB // LN)], axis=1)
    grad_down = jnp.concatenate([gf[i, DB:] for i in range(FB // LN)], axis=1)
    return (
        layer_out, grad_in, gv[0, CB : CB + GN], gv[:, :CB], grad_mixing, go[:, :CB].T,
        go[0, CB : CB + GN], grad_up, grad_down.T,
    )


def compute(tab, x, docs, cot, a, b, w, ffn):
    dq, dk = docs.reshape(L, 1), docs
    low, vals, gain = run_values(tab, x, w)
    mixed_a = run_mixer(tab, 0, x, gain, dq, dk, vals, a)[0]
    mixed_b, mid, n_two = run_mixer(tab, 1, x, gain, dq, dk, vals, b, mixed_a, w)
    k1, s1, *acc = run_ffn(tab, tab_a, n_two, cot, ffn[0])
    k2, s2, *acc = run_ffn(tab, tab_a, n_two, cot, ffn[1], acc)
    k3, s3, _, n_grad, layer_out = run_ffn(tab, tab_a, n_two, cot, ffn[2], acc, mid)
    mid_grad, grad, *go = run_branch(tab, n_grad, mid, cot, gain, mixed_a, mixed_b, w)
    *gb, vgb = run_mixer_back(tab, True, grad, dq, dk, vals, b)
    *ga, vga = run_mixer_back(tab, False, grad, dq, dk, vals, a)
    grad_in, *gv = run_last(tab, x, gain, low, vga, vgb, w, mid_grad)
    return layer_out, grad_in, ((k1, s1), (k2, s2), (k3, s3)), ga, gb, go, gv


def cols_in(v, o, gains):
    def blocks(mat, gain):
        mat = mat.reshape(G, DB, Z, 2, CB).transpose(3, 0, 2, 1, 4)
        gain = gain.reshape(G, Z, 2, 1, GN).transpose(2, 0, 1, 3, 4)
        gain = jnp.pad(gain, ((0, 0),) * 3 + ((0, DB - 1), (0, LN - CB - GN)))
        return jnp.concatenate([mat, gain], axis=-1)

    return jnp.concatenate([blocks(v, gains[0]), blocks(o, gains[1])], axis=3)


def cols_out(keep, send):
    mat = jnp.stack([keep, send])
    dg = mat[:, :, :, 0, CB : CB + GN].transpose(1, 2, 0, 3).reshape(D)
    return mat[..., :CB].transpose(1, 3, 2, 0, 4).reshape(D, D), dg


def any_shards(layer_in, doc_ids, mix_gain, value_w, mixing, output_w, ffn_gain, up_w, down_w, cot):
    ax = ("gx", "gy")
    seqs = layer_in.shape[0] // L
    me = lax.axis_index("gy") * seqs

    def gather(arr, d0, d1):
        arr = lax.all_gather(arr, "gx", axis=d0, tiled=True)
        return lax.all_gather(arr, "gy", axis=d1, tiled=True)

    def scatter(arr, d0, d1):
        arr = lax.psum_scatter(arr, "gx", scatter_dimension=d0, tiled=True)
        return lax.psum_scatter(arr, "gy", scatter_dimension=d1, tiled=True).astype(F32)

    gains = lax.all_gather(jnp.stack([mix_gain, ffn_gain]), ax, axis=1, tiled=True)
    w = cols_in(gather(value_w, 0, 1), gather(output_w.T, 0, 1), gains)
    mix_full = gather(mixing, 2, 1).reshape(2, HA, Z, 2, QB, G, KB).transpose(0, 3, 5, 2, 1, 4, 6)
    a, b = mix_full.reshape((2, 2) + U_SHAPE)
    starts = [min(max(m - 1, 0), G - WIN) for m in range(Z)]
    b = jnp.stack([b[:, s : s + WIN, m] for m, s in enumerate(starts)], axis=1)
    ffn = jnp.stack([gather(up_w, 0, 1), gather(down_w.T, 0, 1)])
    ffn = ffn.reshape(2, G, DB, Z, 2, FB // LN, LN).transpose(5, 4, 1, 3, 0, 2, 6)
    ffn = ffn.reshape((FB // LN, 2) + U_SHAPE)
    tab = jnp.array([0] + [0, 1, 2, 3] * 3, jnp.int32)

    rows_out, grads = [], None
    for s in range(seqs):
        docs = lax.dynamic_slice_in_dim(doc_ids, me + s, 1, 0)
        part = slice(s * L, (s + 1) * L)
        out, g_in, *rest = compute(tab, layer_in[part], docs, cot[part], a, b, w, ffn)
        rows_out.append((out, g_in))
        rest = jax.tree.map(lambda v: v.astype(F32), rest) if seqs > 1 else rest
        grads = rest if grads is None else jax.tree.map(jnp.add, grads, rest)
    layer_out = jnp.concatenate([r[0] for r in rows_out], axis=0)
    grad_in = jnp.concatenate([r[1] for r in rows_out], axis=0)
    gf, ga, gb, go, gv = jax.tree.map(lambda v: v.astype(BF16), grads)
    value_full, dg_one = cols_out(*gv)
    output_full, dg_two = cols_out(*go)
    gb = jnp.stack(gb)
    gb = jnp.stack(
        [
            jnp.pad(gb[:, m], ((0, 0), (s, G - WIN - s), (0, 0), (0, 0)))
            for m, s in enumerate(starts)
        ],
        axis=2,
    )
    gm = jnp.stack([jnp.stack(ga), gb]).reshape(2, 2, G, Z, HA, QB, KB)
    gm = gm.transpose(0, 4, 3, 1, 5, 2, 6)
    gf = jnp.stack([jnp.stack(pair) for pair in gf]).reshape(FB // LN, 2, G, Z, 2, DB, LN)
    grad_up, grad_down = gf.transpose(4, 2, 5, 3, 1, 0, 6).reshape(2, D, FF)
    dgs = jnp.stack([dg_one, dg_two]).astype(F32)
    dgs = lax.psum_scatter(dgs, ax, scatter_dimension=1, tiled=True)
    return (
        layer_out, grad_in, dgs[0], scatter(value_full, 0, 1), scatter(gm.reshape(H, L, L), 2, 1),
        scatter(output_full, 0, 1).T, dgs[1], scatter(grad_up, 0, 1), scatter(grad_down, 0, 1).T,
    )


def solution(mesh):
    tok = P(("gx", "gy"), None)
    vec = P(("gx", "gy"))
    wgt = P("gx", "gy")
    twg = P("gy", "gx")
    mix = P(None, "gy", "gx")
    in_specs = (tok, P("gx", None), vec, wgt, mix, twg, vec, wgt, twg, tok)
    out_specs = (tok, tok, vec, wgt, mix, twg, vec, wgt, twg)

    def run(*args):
        small = (mesh.shape["gx"], mesh.shape["gy"], args[0].shape[0]) == (G, 2 * Z, L)
        return (small_shards if small else any_shards)(*args)

    return jax.shard_map(run, mesh=mesh, in_specs=in_specs, out_specs=out_specs, check_vma=False)
```

```python
import functools

import jax
import jax.numpy as jnp
from jax import lax
from jax.experimental import pallas as pl
from jax.experimental.pallas import tpu as pltpu
from jax.sharding import PartitionSpec as P

D = 768
H = 12
HS = 64
FF = 3072
L = 512
EPS = 1e-05
G = 4
Z = 4
DB = D // G
CB = D // (2 * Z)
FB = FF // (2 * Z)
QB = L // (2 * Z)
KB = L // G
LN = 128
GW = 2 * LN
GN = CB // 4
HA = H // 2
HR = HA * QB
TM = 128
WIN = 3
HZ = H // Z
GC = 0.7978845608
GA = 0.044715
VMEM_LIMIT = 52 * 1024 * 1024
COST = 1 << 38

F32 = jnp.float32
BF16 = jnp.bfloat16


def dot(a, b, ca, cb):
    return lax.dot_general(a, b, (((ca,), (cb,)), ((), ())), preferred_element_type=F32)


def call(body, grid, in_specs, out_specs, out_shape, scratch=(), flops=0, nbytes=0):
    return pl.pallas_call(
        body,
        grid_spec=pltpu.PrefetchScalarGridSpec(
            num_scalar_prefetch=1,
            grid=grid,
            in_specs=in_specs,
            out_specs=out_specs,
            scratch_shapes=list(scratch),
        ),
        out_shape=out_shape,
        compiler_params=pltpu.CompilerParams(
            dimension_semantics=("arbitrary",) * len(grid), vmem_limit_bytes=VMEM_LIMIT
        ),
        cost_estimate=pl.CostEstimate(flops=COST, bytes_accessed=nbytes, transcendentals=0),
    )


def whole(shape):
    zeros = (0,) * len(shape)
    return pl.BlockSpec(shape, lambda i, t: zeros, pipeline_mode=pl.Buffered(1))


def rows(width):
    return pl.BlockSpec((TM, width), lambda i, t: (i, 0))


def out_whole(shape):
    zeros = (0,) * len(shape)
    return pl.BlockSpec(shape, lambda i, t: zeros)


def tab_a(t, g):
    return t[1 + g]


def tab_b(t, g):
    return t[1 + G + g]


def tab_z(t, z):
    return t[1 + 2 * G + z]


def norm_stats(x):
    mean = jnp.mean(x, axis=-1, keepdims=True)
    cen = x - mean
    rstd = lax.rsqrt(jnp.mean(cen * cen, axis=-1, keepdims=True) + EPS)
    return cen, rstd


def weight_z(own, oth, t, z, base):
    parts = [
        jnp.concatenate(
            [ref[tab_a(t, g), tab_z(t, z), base : base + DB, :] for g in range(G)], axis=0
        )
        for ref in (own, oth)
    ]
    return jnp.concatenate(parts, axis=1)


def head_masks(core, nrows):
    lane = lax.broadcasted_iota(jnp.int32, (nrows, GW), 1)
    tile = lane // LN
    place = lane - tile * LN
    side = jnp.where(core == 0, tile, 1 - tile)
    col = jnp.where(place < CB, side * CB + place, -1)
    return [jnp.logical_and(col >= HS * i, col < HS * (i + 1)) for i in range(HZ)]


def halves(ref, core, lead=None):
    lo = pl.multiple_of(core * QB, QB)
    hi = pl.multiple_of((1 - core) * QB, QB)
    if lead is None:
        return jnp.concatenate([ref[pl.ds(lo, QB), :], ref[pl.ds(hi, QB), :]], axis=0)
    return jnp.concatenate([ref[lead, pl.ds(lo, QB), :], ref[lead, pl.ds(hi, QB), :]], axis=0)


def put_halves(ref, core, val, lead=None):
    lo = pl.multiple_of(core * QB, QB)
    hi = pl.multiple_of((1 - core) * QB, QB)
    if lead is None:
        ref[pl.ds(lo, QB), :] = val[:QB]
        ref[pl.ds(hi, QB), :] = val[QB:]
    else:
        ref[lead, pl.ds(lo, QB), :] = val[:QB]
        ref[lead, pl.ds(hi, QB), :] = val[QB:]


def window(m):
    return jnp.clip(m - 1, 0, G - WIN)


def exp_scores(a_own, a_oth, b_own, b_oth, t, m, head, mask):
    parts = []
    for i in range(WIN):
        both = []
        for a, b in ((a_own, b_own), (a_oth, b_oth)):
            if head < HA:
                both.append(a[tab_b(t, window(m) + i), tab_z(t, m), head * QB : (head + 1) * QB, :])
            else:
                h = head - HA
                both.append(b[tab_z(t, m), i, h * QB : (h + 1) * QB, :])
        parts.append(jnp.concatenate(both, axis=0))
    scores = jnp.concatenate(parts, axis=1).astype(F32)
    return jnp.where(mask, jnp.exp(scores), 0.0)


def gain_spots():
    for g in range(G):
        for z in range(Z):
            for c in range(2):
                yield g, z, c, DB * g + (2 * GN) * z + GN * c


def pick(core, c, own, oth):
    return jnp.where(core == c, own, oth)


def gains_row(own, oth, t, base):
    lane = lax.broadcasted_iota(jnp.int32, (1, LN), 1)
    tiles = [jnp.zeros((1, LN), F32) for _ in range(D // LN)]
    for g, z, c, at in gain_spots():
        a, b = (r[tab_a(t, g), tab_z(t, z), base : base + 16, :].astype(F32)[:1] for r in (own, oth))
        row = pick(t[0], c, a, b)
        tile, off = at // LN, at % LN
        row = pltpu.roll(row, (off - CB) % LN, 1)
        tiles[tile] = jnp.where(jnp.logical_and(lane >= off, lane < off + GN), row, tiles[tile])
        if off + GN > LN:
            tiles[tile + 1] = jnp.where(lane < off + GN - LN, row, tiles[tile + 1])
    return jnp.concatenate(tiles, axis=1)


def put_weight_grads(acc, dg, t, keep, send):
    lane = lax.broadcasted_iota(jnp.int32, (1, LN), 1)
    top = lax.broadcasted_iota(jnp.int32, (16, LN), 0) == 0
    spot = jnp.logical_and(top, jnp.logical_and(lane >= CB, lane < CB + GN))
    rows_of = {}
    for g, z, c, at in gain_spots():
        tile, off = at // LN, at % LN
        row = dg[:, tile * LN : (tile + 1) * LN]
        if off + GN > LN:
            row = jnp.where(lane < off, dg[:, (tile + 1) * LN : (tile + 2) * LN], row)
        rows_of[g, z, c] = pltpu.roll(row, (CB - off) % LN, 1)
    for g in range(G):
        for z in range(Z):
            for p, ref in ((0, keep), (1, send)):
                blk = acc[z, g * DB : (g + 1) * DB, p * LN : (p + 1) * LN]
                row = pick(t[0], p, rows_of[g, z, 0], rows_of[g, z, 1])
                ref[tab_a(t, g), tab_z(t, z)] = blk.astype(BF16)
                ref[tab_a(t, g), tab_z(t, z), 0:16, :] = jnp.where(spot, row, blk[:16]).astype(BF16)


def values_body(t, x_ref, own_ref, oth_ref, n_ref, val_ref, gain_ref):
    @pl.when(pl.program_id(0) == 0)
    def _():
        gain_ref[0:1, :] = gains_row(own_ref, oth_ref, t, 0)
        gain_ref[1:2, :] = gains_row(own_ref, oth_ref, t, DB)

    cen, rstd = norm_stats(x_ref[...].astype(F32))
    low = (cen * rstd * gain_ref[0:1, :]).astype(BF16)
    n_ref[...] = low
    for z in range(Z):
        val_ref[z] = dot(low, weight_z(own_ref, oth_ref, t, z, 0), 1, 0).astype(BF16)


def mixer_body(
    t, x_ref, gain_ref, dq_ref, dk_ref, val_ref, a_own, a_oth, b_own, b_oth, w_own, w_oth,
    mix_ref, mid_ref, n_ref,
):
    m = pl.program_id(0)
    core = t[0]
    k0 = pl.multiple_of(window(m) * KB, KB)
    mask = halves(dq_ref, core) == dk_ref[:, pl.ds(k0, WIN * KB)]
    heads = head_masks(core, TM)
    acc = halves(x_ref, core).astype(F32)
    for z in range(Z):
        win = val_ref[z, pl.ds(k0, WIN * KB), :]
        out = jnp.zeros((TM, GW), F32)
        for i in range(HZ):
            e = exp_scores(a_own, a_oth, b_own, b_oth, t, m, HZ * z + i, mask)
            inv = 1.0 / jnp.sum(e, axis=-1, keepdims=True)
            part = dot((e * inv).astype(BF16), win, 1, 0)
            out = jnp.where(heads[i], part, out)
        low = out.astype(BF16)
        put_halves(mix_ref, core, low, z)
        acc = acc + dot(low, weight_z(w_own, w_oth, t, z, DB), 1, 1)
    put_halves(mid_ref, core, acc)
    cen, rstd = norm_stats(acc)
    put_halves(n_ref, core, (cen * rstd * gain_ref[1:2, :]).astype(BF16))


def ffn_body(first, last, t, n_ref, c_ref, u_ref, d_ref, *refs):
    refs = list(refs)
    if not first:
        ia_ref, ib_ref = refs[:2]
        refs = refs[2:]
    if last:
        mid_ref = refs[0]
        refs = refs[1:]
    gu_ref, gd_ref, b_ref, a_ref = refs[:4]
    j = pl.program_id(0)
    n = n_ref[...]
    cot = c_ref[...]
    up_w = jnp.concatenate([u_ref[tab_b(t, g), 0] for g in range(G)], axis=0)
    dn_w = jnp.concatenate([d_ref[tab_a(t, g), 0] for g in range(G)], axis=0)

    @pl.when(j == 0)
    def _():
        if first:
            a_ref[...] = jnp.zeros_like(a_ref)
            b_ref[...] = jnp.zeros_like(b_ref)
        else:
            a_ref[...] = ia_ref[...]
            b_ref[...] = ib_ref[...]

    up = dot(n, up_w, 1, 0)
    sq = up * up
    th = jnp.tanh(GC * up * (1.0 + GA * sq))
    half = 0.5 + 0.5 * th
    act = (up * half).astype(BF16)
    slope = half + (0.5 * GC) * up * (1.0 - th * th) * (1.0 + (3.0 * GA) * sq)
    a_ref[...] += dot(act, dn_w, 1, 1)
    gd = dot(cot, act, 0, 0).astype(BF16)
    up_g = (dot(cot, dn_w, 1, 0) * slope).astype(BF16)
    gu = dot(n, up_g, 0, 0).astype(BF16)
    b_ref[...] += dot(up_g, up_w, 1, 1)
    for g in range(G):
        gu_ref[tab_b(t, g), 0] = gu[g * DB : (g + 1) * DB]
        gd_ref[tab_a(t, g), 0] = gd[g * DB : (g + 1) * DB]
    if last:
        lo_ref = refs[4]

        @pl.when(j == Z - 1)
        def _():
            lo_ref[...] = (mid_ref[...] + a_ref[...]).astype(BF16)


def norm_back(cen, rstd, gain, dn):
    xhat = cen * rstd
    e = dn * gain
    dv = (
        e
        - jnp.mean(e, axis=-1, keepdims=True)
        - xhat * jnp.mean(e * xhat, axis=-1, keepdims=True)
    ) * rstd
    return dv, jnp.sum(dn * xhat, axis=0, keepdims=True)


def mixer_back_body(
    t, dn_ref, mid_ref, c_ref, gain_ref, dq_ref, dk_ref, mix_ref, val_ref,
    a_own, a_oth, b_own, b_oth, w_own, w_oth,
    mg_ref, ka_ref, sa_ref, kb_ref, sb_ref, ko_ref, so_ref, vg_ref, dg_acc, go_acc, vg_acc,
):
    m = pl.program_id(0)
    core = t[0]
    start = window(m)
    k0 = pl.multiple_of(start * KB, KB)

    @pl.when(m == 0)
    def _():
        go_acc[...] = jnp.zeros_like(go_acc)
        vg_acc[...] = jnp.zeros_like(vg_acc)
        dg_acc[...] = jnp.zeros_like(dg_acc)

    cen, rstd = norm_stats(halves(mid_ref, core))
    dv, dg = norm_back(cen, rstd, gain_ref[1:2, :], halves(dn_ref, core))
    dg_acc[0:1, :] += dg
    mid_grad = halves(c_ref, core).astype(F32) + dv
    put_halves(mg_ref, core, mid_grad)
    branch = mid_grad.astype(BF16)
    mask = halves(dq_ref, core) == dk_ref[:, pl.ds(k0, WIN * KB)]
    heads = head_masks(core, TM)
    rest = tab_b(t, jnp.where(start == 0, G - 1, 0))
    ka_ref[rest, 0] = jnp.zeros((HR, KB), BF16)
    sa_ref[rest, 0] = jnp.zeros((HR, KB), BF16)
    for z in range(Z):
        go_acc[z] += dot(branch, halves(mix_ref, core, z), 0, 0)
        grad = dot(branch, weight_z(w_own, w_oth, t, z, DB), 1, 0)
        grad = grad.astype(BF16).astype(F32)
        win = val_ref[z, pl.ds(k0, WIN * KB), :]
        total = jnp.zeros((WIN * KB, GW), F32)
        for i in range(HZ):
            head = HZ * z + i
            e = exp_scores(a_own, a_oth, b_own, b_oth, t, m, head, mask)
            inv = 1.0 / jnp.sum(e, axis=-1, keepdims=True)
            prob = e * inv
            mine = jnp.where(heads[i], grad, 0.0).astype(BF16)
            total = total + dot(prob.astype(BF16), mine, 0, 0)
            dp = dot(mine, win, 1, 1)
            pd = prob * dp
            ds = (pd - prob * jnp.sum(pd, axis=-1, keepdims=True)).astype(BF16)
            for k in range(WIN):
                for p, (ra, rb) in enumerate(((ka_ref, kb_ref), (sa_ref, sb_ref))):
                    blk = ds[p * QB : (p + 1) * QB, k * KB : (k + 1) * KB]
                    if head < HA:
                        ra[tab_b(t, start + k), 0, head * QB : (head + 1) * QB, :] = blk
                    else:
                        h = head - HA
                        rb[0, k, h * QB : (h + 1) * QB, :] = blk
        vg_acc[z, pl.ds(k0, WIN * KB), :] += total

    @pl.when(m == Z - 1)
    def _():
        vg_ref[...] = vg_acc[...].astype(BF16)
        put_weight_grads(go_acc, dg_acc[0:1, :], t, ko_ref, so_ref)


def last_body(
    t, x_ref, gain_ref, n_ref, vg_ref, w_own, w_oth, mg_ref, gi_ref, kv_ref, sv_ref, dg_acc, gv_acc
):
    m = pl.program_id(0)

    @pl.when(m == 0)
    def _():
        gv_acc[...] = jnp.zeros_like(gv_acc)
        dg_acc[...] = jnp.zeros_like(dg_acc)

    low = n_ref[...]
    dn = jnp.zeros((TM, D), F32)
    for z in range(Z):
        vg = vg_ref[z]
        gv_acc[z] += dot(low, vg, 0, 0)
        dn = dn + dot(vg, weight_z(w_own, w_oth, t, z, 0), 1, 1)
    cen, rstd = norm_stats(x_ref[...].astype(F32))
    dv, dg = norm_back(cen, rstd, gain_ref[0:1, :], dn)
    dg_acc[0:1, :] += dg
    gi_ref[...] = mg_ref[...] + dv

    @pl.when(m == Z - 1)
    def _():
        put_weight_grads(gv_acc, dg_acc[0:1, :], t, kv_ref, sv_ref)


def sds(shape, dtype):
    return jax.ShapeDtypeStruct(shape, dtype)


W_SHAPE = (G, Z, 2 * DB, LN)
V_SHAPE = (G, Z, DB, LN)
A_SHAPE = (G, Z, HR, KB)
B_SHAPE = (Z, WIN, HR, KB)
F_SHAPE = (G, Z, DB, FB)
Z_ROWS = pl.BlockSpec((Z, TM, GW), lambda i, t: (0, i, 0))


def run_values(tab, x, w):
    return call(
        values_body,
        (L // TM,),
        [rows(D), whole(W_SHAPE), whole(W_SHAPE)],
        [rows(D), Z_ROWS, out_whole((8, D))],
        [sds((L, D), BF16), sds((Z, L, GW), BF16), sds((8, D), F32)],
        flops=2 * L * D * Z * GW,
        nbytes=6 << 20,
    )(tab, x, *w)


def run_mixer(tab, x, gain, dq, dk, vals, a, b, w):
    return call(
        mixer_body,
        (L // TM,),
        [
            rows(D), whole((8, D)), rows(1), whole((1, L)), whole((Z, L, GW)),
            whole(A_SHAPE), whole(A_SHAPE), whole(B_SHAPE), whole(B_SHAPE),
            whole(W_SHAPE), whole(W_SHAPE),
        ],
        [Z_ROWS, rows(D), rows(D)],
        [sds((Z, L, GW), BF16), sds((L, D), F32), sds((L, D), BF16)],
        flops=2 * L * D * Z * GW + 2 * H * L * WIN * KB * GW,
        nbytes=14 << 20,
    )(tab, x, gain, dq, dk, vals, *a, *b, *w)

def run_ffn(tab, n, cot, u_w, d_w, acc=None, mid=None):
    first, last = acc is None, mid is not None
    blk = pl.BlockSpec((G, 1, DB, FB), lambda i, t: (0, i, 0, 0))
    in_specs = [whole((L, D)), whole((L, D)), blk, blk]
    args = [tab, n, cot, u_w, d_w]
    if not first:
        in_specs += [whole((L, D)), whole((L, D))]
        args += list(acc)
    if last:
        in_specs += [whole((L, D))]
        args += [mid]
    out_specs = [blk, blk, out_whole((L, D))]
    outs = [sds(F_SHAPE, BF16), sds(F_SHAPE, BF16), sds((L, D), F32)]
    scratch = ()
    if last:
        scratch = (pltpu.VMEM((L, D), F32),)
        out_specs += [out_whole((L, D))]
        outs += [sds((L, D), BF16)]
    else:
        out_specs += [out_whole((L, D))]
        outs += [sds((L, D), F32)]

    def body(t, *refs):
        if last:
            refs = list(refs)
            refs = refs[:-2] + [refs[-1], refs[-2]]
        ffn_body(first, last, t, *refs)

    return call(
        body, (Z,), in_specs, out_specs, outs, scratch, flops=6 * L * D * FF, nbytes=20 << 20
    )(*args)


def run_mixer_back(tab, dn, mid, cot, gain, dq, dk, mixed, vals, a, b, w):
    blk_a = pl.BlockSpec((G, 1, HR, KB), lambda i, t: (0, tab_z(t, i), 0, 0))
    blk_b = pl.BlockSpec((1, WIN, HR, KB), lambda i, t: (tab_z(t, i), 0, 0, 0))
    return call(
        mixer_back_body,
        (L // TM,),
        [
            rows(D), rows(D), rows(D), whole((8, D)), rows(1), whole((1, L)), Z_ROWS,
            whole((Z, L, GW)), whole(A_SHAPE), whole(A_SHAPE), whole(B_SHAPE), whole(B_SHAPE),
            whole(W_SHAPE), whole(W_SHAPE),
        ],
        [rows(D), blk_a, blk_a, blk_b, blk_b, out_whole(V_SHAPE), out_whole(V_SHAPE), out_whole((Z, L, GW))],
        [
            sds((L, D), F32), sds(A_SHAPE, BF16), sds(A_SHAPE, BF16), sds(B_SHAPE, BF16),
            sds(B_SHAPE, BF16), sds(V_SHAPE, BF16), sds(V_SHAPE, BF16), sds((Z, L, GW), BF16),
        ],
        scratch=(pltpu.VMEM((8, D), F32), pltpu.VMEM((Z, D, GW), F32), pltpu.VMEM((Z, L, GW), F32)),
        flops=4 * L * D * Z * GW + 6 * H * L * WIN * KB * GW,
        nbytes=28 << 20,
    )(tab, dn, mid, cot, gain, dq, dk, mixed, vals, *a, *b, *w)


def run_last(tab, x, gain, low, vg, w, mid_grad):
    return call(
        last_body,
        (L // TM,),
        [rows(D), whole((8, D)), rows(D), Z_ROWS, whole(W_SHAPE), whole(W_SHAPE), rows(D)],
        [rows(D), out_whole(V_SHAPE), out_whole(V_SHAPE)],
        [sds((L, D), F32), sds(V_SHAPE, BF16), sds(V_SHAPE, BF16)],
        scratch=(pltpu.VMEM((8, D), F32), pltpu.VMEM((Z, D, GW), F32)),
        flops=4 * L * D * Z * GW,
        nbytes=12 << 20,
    )(tab, x, gain, low, vg, *w, mid_grad)


def add_up(terms):
    total = terms[0].astype(F32)
    for term in terms[1:]:
        total = total + term.astype(F32)
    return total


def after(val, *deps):
    return lax.optimization_barrier((val, deps))[0]


class Grid:
    def __init__(self, gx, gy):
        self.gy = gy
        self.size = {"y": gx // 2, "x": 2, "z": gy // 2, "c": 2}
        i, j = lax.axis_index("gx"), lax.axis_index("gy")
        self.at = {"y": i // 2, "x": i % 2, "z": j // 2, "c": j % 2}

    def fetch(self, val, axis, k):
        sizes = self.size
        pairs = []
        for y in range(sizes["y"]):
            for x in range(sizes["x"]):
                for z in range(sizes["z"]):
                    for c in range(sizes["c"]):
                        src = {"y": y, "x": x, "z": z, "c": c}
                        dst = dict(src)
                        dst[axis] = (src[axis] + k) % sizes[axis]
                        pairs.append(tuple((p["y"] * 2 + p["x"]) * self.gy + p["z"] * 2 + p["c"] for p in (src, dst)))
        return lax.ppermute(val, ("gx", "gy"), pairs)

    def rel(self, axis, v):
        return (self.at[axis] - v) % self.size[axis]

    def spread(self, val, axis):
        return jnp.stack([val] + [self.fetch(val, axis, k) for k in range(1, self.size[axis])])

    def reduce(self, terms, stage, axis, *deps):
        if deps:
            terms = terms[:-1] + [(after(terms[-1][0], *deps), terms[-1][1])]
        got = []
        for k in range(1, self.size[axis]):
            part = add_up([v[(0,) * (stage - born) + (k,)] for v, born in terms]).astype(BF16)
            got.append((self.fetch(part, axis, -k), stage + 1))
        return terms + got

    def total(self, terms, stage):
        return add_up([v[(0,) * (stage - born)] for v, born in terms])

    def reduce_joined(self, groups, axis, *deps):
        groups = list(groups)
        if deps:
            groups[-1] = groups[-1][:-1] + [(after(groups[-1][-1][0], *deps), groups[-1][-1][1])]
        got = []
        for k in range(1, self.size[axis]):
            parts = [
                add_up([v[(0,) * (2 - born) + (k,)] for v, born in terms]).astype(BF16)
                for terms in groups
            ]
            got.append(self.fetch(jnp.concatenate(parts, axis=0), axis, -k))
        out, at_row = [], 0
        for terms in groups:
            n = terms[0][0].shape[-2]
            own = [v[(0,) * (3 - born)] for v, born in terms]
            out.append(add_up(own + [v[at_row : at_row + n] for v in got]))
            at_row += n
        return out


def compute(tab, x, docs, cot, a, b, w, u, d):
    dq, dk = docs.reshape(L, 1), docs
    low, vals, gain = run_values(tab, x, w)
    mixed, mid, n_two = run_mixer(tab, x, gain, dq, dk, vals, a, b, w)
    gu0, gd0, acc_b, acc_a = run_ffn(tab, n_two, cot, u[0], d[0])
    gu1, gd1, n_grad, layer_out = run_ffn(tab, n_two, cot, u[1], d[1], (acc_a, acc_b), mid)
    mid_grad, ka, sa, kb, sb, ko, so, vg = run_mixer_back(
        tab, n_grad, mid, cot, gain, dq, dk, mixed, vals, a, b, w
    )
    grad_in, kv, sv = run_last(tab, x, gain, low, vg, w, mid_grad)
    return layer_out, grad_in, (gu0, gu1), (gd0, gd1), (ka, sa), (kb, sb), (ko, so), (kv, sv)


def lane_pad(mat, gains):
    row = jnp.pad(gains.reshape(1, GN), ((0, DB - 1), (0, LN - CB - GN)))
    return jnp.concatenate([mat, row], axis=1)


def small_shards(layer_in, doc_ids, mix_gain, value_w, mixing, output_w, ffn_gain, up_w, down_w, cot):
    grid = Grid(G, 2 * Z)
    at = grid.at
    order_a = [grid.rel("x", g % 2) * 2 + grid.rel("y", g // 2) for g in range(G)]
    order_b = [grid.rel("y", g // 2) * 2 + grid.rel("x", g % 2) for g in range(G)]
    order_z = [grid.rel("z", z) for z in range(Z)]
    tab = jnp.stack([at["c"]] + order_a + order_b + order_z).astype(jnp.int32)
    docs = lax.dynamic_slice_in_dim(doc_ids, lax.axis_index("gy"), 1, 0)

    dq, dk = docs.reshape(L, 1), docs
    mix = mixing.reshape(2, HR, KB)
    fetch, spread = grid.fetch, grid.spread
    wts = jnp.concatenate([lane_pad(value_w, mix_gain), lane_pad(output_w.T, ffn_gain)], axis=0)

    def both(val, *deps):
        return val, fetch(after(val, *deps) if deps else val, "c", 1)

    def along_z(val):
        return [val] + [fetch(val, "z", k) for k in range(1, Z)]

    c1 = along_z(jnp.concatenate([mix[0], wts], axis=0))
    b = spread(spread(mix[1], "x"), "y").reshape(G, HR, KB)
    start = window(at["z"])
    order = jnp.stack(order_b)
    b = jnp.stack([lax.dynamic_index_in_dim(b, order[start + i], 0, False) for i in range(WIN)])
    a, w = (jnp.stack([v[i * HR : (i + 1) * HR] for v in c1]) for i in range(2))
    ffn = along_z(after(jnp.stack([up_w, down_w.T]), c1[1:]))
    a, w = spread(a, "x"), spread(w, "y")
    a, w = spread(a, "y").reshape(A_SHAPE), spread(w, "x").reshape(W_SHAPE)
    b = spread(after(b, ffn[1:]), "z")
    ffn[1:] = after(ffn[1:], a, w)
    u, d = (jnp.stack([v[i] for v in ffn]) for i in range(2))
    w, a = both(w), both(a)
    low, vals, gain = run_values(tab, layer_in, w)
    u, d = spread(u, "x"), spread(d, "y")
    b = both(b)
    u, d = after((u, d), low)
    u, d = spread(u, "y").reshape(F_SHAPE), spread(d, "x").reshape(F_SHAPE)
    mixed, mid, n_two = run_mixer(tab, layer_in, gain, dq, dk, vals, a, b, w)
    u, d = both(u, n_two), both(d, n_two)

    def begin(keep, send):
        got = fetch(send, "c", 1)
        return [(v.reshape((2, 2) + v.shape[1:]), 0) for v in (keep, got)]

    def last(*groups):
        return [terms[-1][0] for terms in groups]

    su, sd, acc_b, acc_a = run_ffn(tab, n_two, cot, u[1], d[1])
    ku, kd, n_grad, layer_out = run_ffn(tab, n_two, cot, u[0], d[0], (acc_a, acc_b), mid)
    gu, gd = begin(ku, su), begin(kd, sd)
    n_grad = after(n_grad, last(gu, gd))
    gu, gd = grid.reduce(gu, 0, "y"), grid.reduce(gd, 0, "x")
    mid_grad, ka, sa, kb, sb, ko, so, vg = run_mixer_back(
        tab, n_grad, mid, cot, gain, dq, dk, mixed, vals, a, b, w
    )
    vg = after(vg, last(gu, gd))
    ga, go, rb = begin(ka, sa), begin(ko, so), fetch(sb, "c", 1)
    gu, gd = grid.reduce(gu, 1, "x", sa), grid.reduce(gd, 1, "y", sa)
    gb = grid.reduce([(kb, 2), (rb, 2)], 2, "z")
    grad_in, kv, sv = run_last(tab, layer_in, gain, low, vg, w, mid_grad)
    gv = begin(kv, sv)
    ga = grid.reduce(ga, 0, "y", sv)
    go = grid.reduce(go, 0, "x", sv)
    gu, gd = grid.reduce_joined((gu, gd), "z", last(gb))
    gv = grid.reduce(gv, 0, "x")
    wide = grid.total(gb, 3)
    blocks = []
    for k in range(G):
        spot = (at["y"] - k // 2) % 2 * 2 + (at["x"] - k % 2) % 2 - start
        blk = lax.dynamic_index_in_dim(wide, jnp.clip(spot, 0, WIN - 1), 0, False)
        ok = jnp.logical_and(spot >= 0, spot < WIN)
        blocks.append(jnp.where(ok, blk, jnp.zeros_like(blk)))
    gb = [(jnp.stack(blocks).reshape(2, 2, HR, KB), 0)]
    gb = grid.total(grid.reduce(grid.reduce(gb, 0, "y"), 1, "x"), 2)
    ga, go = grid.reduce(ga, 1, "x"), grid.reduce(go, 1, "y")
    gv = grid.reduce(gv, 1, "y")
    ga, go, gv = grid.reduce_joined((ga, go, gv), "z")

    grad_mixing = jnp.concatenate([ga, gb], axis=0).reshape(H, QB, KB)
    return (
        layer_out, grad_in, gv[0, CB : CB + GN], gv[:, :CB], grad_mixing, go[:, :CB].T,
        go[0, CB : CB + GN], gu, gd.T,
    )


def cols_in(v, o, gains):
    def blocks(mat, gain):
        mat = mat.reshape(G, DB, Z, 2, CB).transpose(3, 0, 2, 1, 4)
        gain = gain.reshape(G, Z, 2, 1, GN).transpose(2, 0, 1, 3, 4)
        gain = jnp.pad(gain, ((0, 0),) * 3 + ((0, DB - 1), (0, LN - CB - GN)))
        return jnp.concatenate([mat, gain], axis=-1)

    return jnp.concatenate([blocks(v, gains[0]), blocks(o, gains[1])], axis=3)


def cols_out(keep, send):
    mat = jnp.stack([keep, send])
    dg = mat[:, :, :, 0, CB : CB + GN].transpose(1, 2, 0, 3).reshape(D)
    return mat[..., :CB].transpose(1, 3, 2, 0, 4).reshape(D, D), dg


def any_shards(layer_in, doc_ids, mix_gain, value_w, mixing, output_w, ffn_gain, up_w, down_w, cot):
    ax = ("gx", "gy")
    seqs = layer_in.shape[0] // L
    me = lax.axis_index("gy") * seqs

    def gather(arr, d0, d1):
        arr = lax.all_gather(arr, "gx", axis=d0, tiled=True)
        return lax.all_gather(arr, "gy", axis=d1, tiled=True)

    def scatter(arr, d0, d1):
        arr = lax.psum_scatter(arr, "gx", scatter_dimension=d0, tiled=True)
        return lax.psum_scatter(arr, "gy", scatter_dimension=d1, tiled=True).astype(F32)

    gains = lax.all_gather(jnp.stack([mix_gain, ffn_gain]), ax, axis=1, tiled=True)
    w = cols_in(gather(value_w, 0, 1), gather(output_w.T, 0, 1), gains)
    mix_full = gather(mixing, 2, 1).reshape(2, HA, Z, 2, QB, G, KB).transpose(0, 3, 5, 2, 1, 4, 6)
    mix_full = mix_full.reshape(2, 2, G, Z, HR, KB)
    a = mix_full[0]
    starts = [min(max(m - 1, 0), G - WIN) for m in range(Z)]
    b = jnp.stack([mix_full[1][:, s : s + WIN, m] for m, s in enumerate(starts)], axis=1)
    u = gather(up_w, 0, 1).reshape(G, DB, Z, 2, FB).transpose(3, 0, 2, 1, 4)
    d = gather(down_w.T, 0, 1).reshape(G, DB, Z, 2, FB).transpose(3, 0, 2, 1, 4)
    tab = jnp.array([0] + [0, 1, 2, 3] * 3, jnp.int32)

    rows_out, grads = [], None
    for s in range(seqs):
        docs = lax.dynamic_slice_in_dim(doc_ids, me + s, 1, 0)
        part = slice(s * L, (s + 1) * L)
        out, g_in, *rest = compute(tab, layer_in[part], docs, cot[part], a, b, w, u, d)
        rows_out.append((out, g_in))
        rest = jax.tree.map(lambda v: v.astype(F32), rest) if seqs > 1 else rest
        grads = rest if grads is None else jax.tree.map(jnp.add, grads, rest)
    layer_out = jnp.concatenate([r[0] for r in rows_out], axis=0)
    grad_in = jnp.concatenate([r[1] for r in rows_out], axis=0)
    gu, gd, ga, gb, go, gv = jax.tree.map(lambda v: v.astype(BF16), grads)

    def ffn_out(pair):
        return jnp.stack(pair).transpose(1, 3, 2, 0, 4).reshape(D, FF)

    value_full, dg_one = cols_out(*gv)
    output_full, dg_two = cols_out(*go)
    ga, gb = jnp.stack(ga), jnp.stack(gb)
    gb = jnp.stack(
        [
            jnp.pad(gb[:, m], ((0, 0), (s, G - WIN - s), (0, 0), (0, 0)))
            for m, s in enumerate(starts)
        ],
        axis=2,
    )
    gm = jnp.stack([ga, gb]).reshape(2, 2, G, Z, HA, QB, KB).transpose(0, 4, 3, 1, 5, 2, 6)
    dgs = jnp.stack([dg_one, dg_two]).astype(F32)
    dgs = lax.psum_scatter(dgs, ax, scatter_dimension=1, tiled=True)
    return (
        layer_out, grad_in, dgs[0], scatter(value_full, 0, 1), scatter(gm.reshape(H, L, L), 2, 1),
        scatter(output_full, 0, 1).T, dgs[1], scatter(ffn_out(gu), 0, 1), scatter(ffn_out(gd), 0, 1).T,
    )


def solution(mesh):
    tok = P(("gx", "gy"), None)
    vec = P(("gx", "gy"))
    wgt = P("gx", "gy")
    twg = P("gy", "gx")
    mix = P(None, "gy", "gx")
    in_specs = (tok, P("gx", None), vec, wgt, mix, twg, vec, wgt, twg, tok)
    out_specs = (tok, tok, vec, wgt, mix, twg, vec, wgt, twg)

    def run(*args):
        small = (mesh.shape["gx"], mesh.shape["gy"], args[0].shape[0]) == (G, 2 * Z, L)
        return (small_shards if small else any_shards)(*args)

    return jax.shard_map(run, mesh=mesh, in_specs=in_specs, out_specs=out_specs, check_vma=False)
```

```python
import functools

import jax
import jax.numpy as jnp
from jax import lax
from jax.experimental import pallas as pl
from jax.experimental.pallas import tpu as pltpu
from jax.sharding import PartitionSpec as P

D = 768
H = 12
HS = 64
FF = 3072
L = 512
EPS = 1e-05
G = 4
Z = 4
DB = D // G
CB = D // (2 * Z)
FB = FF // (2 * Z)
QB = L // (2 * Z)
KB = L // G
LN = 128
GW = 2 * LN
GN = CB // 4
HA = H // 2
ZS = 2
HR = HA * QB
TM = 128
WIN = 3
HZ = H // Z
GC = 0.7978845608
GA = 0.044715
VMEM_LIMIT = 32 * 1024 * 1024
COST = 1 << 38

F32 = jnp.float32
BF16 = jnp.bfloat16


def dot(a, b, ca, cb):
    return lax.dot_general(a, b, (((ca,), (cb,)), ((), ())), preferred_element_type=F32)


def call(body, grid, in_specs, out_specs, out_shape, scratch=(), flops=0, nbytes=0):
    return pl.pallas_call(
        body,
        grid_spec=pltpu.PrefetchScalarGridSpec(
            num_scalar_prefetch=1,
            grid=grid,
            in_specs=in_specs,
            out_specs=out_specs,
            scratch_shapes=list(scratch),
        ),
        out_shape=out_shape,
        compiler_params=pltpu.CompilerParams(
            dimension_semantics=("arbitrary",) * len(grid), vmem_limit_bytes=VMEM_LIMIT
        ),
        cost_estimate=pl.CostEstimate(flops=COST, bytes_accessed=nbytes, transcendentals=0),
    )


def whole(shape):
    return pl.BlockSpec(memory_space=pltpu.VMEM)


def rows(width):
    return pl.BlockSpec((TM, width), lambda i, t: (i, 0))


def out_whole(shape):
    return pl.BlockSpec(memory_space=pltpu.VMEM)


def tab_a(t, g):
    return t[1 + g]


def tab_b(t, g):
    return t[1 + G + g]


def tab_z(t, z):
    return t[1 + 2 * G + z]


def norm_stats(x):
    mean = jnp.mean(x, axis=-1, keepdims=True)
    cen = x - mean
    rstd = lax.rsqrt(jnp.mean(cen * cen, axis=-1, keepdims=True) + EPS)
    return cen, rstd


def weight_z(own, oth, t, z, base):
    parts = [
        jnp.concatenate(
            [ref[tab_a(t, g), tab_z(t, z), base : base + DB, :] for g in range(G)], axis=0
        )
        for ref in (own, oth)
    ]
    return jnp.concatenate(parts, axis=1)


def head_masks(core, nrows):
    lane = lax.broadcasted_iota(jnp.int32, (nrows, GW), 1)
    tile = lane // LN
    place = lane - tile * LN
    side = jnp.where(core == 0, tile, 1 - tile)
    col = jnp.where(place < CB, side * CB + place, -1)
    return [jnp.logical_and(col >= HS * i, col < HS * (i + 1)) for i in range(HZ)]


def halves(ref, core, lead=None, base=0):
    lo = pl.multiple_of(base + core * QB, QB)
    hi = pl.multiple_of(base + (1 - core) * QB, QB)
    if lead is None:
        return jnp.concatenate([ref[pl.ds(lo, QB), :], ref[pl.ds(hi, QB), :]], axis=0)
    return jnp.concatenate([ref[lead, pl.ds(lo, QB), :], ref[lead, pl.ds(hi, QB), :]], axis=0)


def put_halves(ref, core, val, lead=None, base=0):
    lo = pl.multiple_of(base + core * QB, QB)
    hi = pl.multiple_of(base + (1 - core) * QB, QB)
    if lead is None:
        ref[pl.ds(lo, QB), :] = val[:QB]
        ref[pl.ds(hi, QB), :] = val[QB:]
    else:
        ref[lead, pl.ds(lo, QB), :] = val[:QB]
        ref[lead, pl.ds(hi, QB), :] = val[QB:]


def window(m):
    return jnp.clip(m - 1, 0, G - WIN)


def exp_scores(a_own, a_oth, b_own, b_oth, t, m, head, mask):
    parts = []
    for i in range(WIN):
        both = []
        for a, b in ((a_own, b_own), (a_oth, b_oth)):
            if head < HA:
                both.append(a[tab_b(t, window(m) + i), tab_z(t, m), head * QB : (head + 1) * QB, :])
            else:
                h = head - HA
                both.append(b[tab_z(t, m), i, h * QB : (h + 1) * QB, :])
        parts.append(jnp.concatenate(both, axis=0))
    scores = jnp.concatenate(parts, axis=1).astype(F32)
    return jnp.where(mask, jnp.exp(scores), 0.0)


def gain_spots():
    for g in range(G):
        for z in range(Z):
            for c in range(2):
                yield g, z, c, DB * g + (2 * GN) * z + GN * c


def pick(core, c, own, oth):
    return jnp.where(core == c, own, oth)


def gains_row(own, oth, t, base):
    lane = lax.broadcasted_iota(jnp.int32, (1, LN), 1)
    tiles = [jnp.zeros((1, LN), F32) for _ in range(D // LN)]
    for g, z, c, at in gain_spots():
        a, b = (r[tab_a(t, g), tab_z(t, z), base : base + 16, :].astype(F32)[:1] for r in (own, oth))
        row = pick(t[0], c, a, b)
        tile, off = at // LN, at % LN
        row = pltpu.roll(row, (off - CB) % LN, 1)
        tiles[tile] = jnp.where(jnp.logical_and(lane >= off, lane < off + GN), row, tiles[tile])
        if off + GN > LN:
            tiles[tile + 1] = jnp.where(lane < off + GN - LN, row, tiles[tile + 1])
    return jnp.concatenate(tiles, axis=1)


def put_weight_grads(acc, dg, t, keep, send):
    lane = lax.broadcasted_iota(jnp.int32, (1, LN), 1)
    top = lax.broadcasted_iota(jnp.int32, (16, LN), 0) == 0
    spot = jnp.logical_and(top, jnp.logical_and(lane >= CB, lane < CB + GN))
    rows_of = {}
    for g, z, c, at in gain_spots():
        tile, off = at // LN, at % LN
        row = dg[:, tile * LN : (tile + 1) * LN]
        if off + GN > LN:
            row = jnp.where(lane < off, dg[:, (tile + 1) * LN : (tile + 2) * LN], row)
        rows_of[g, z, c] = pltpu.roll(row, (CB - off) % LN, 1)
    for z in range(Z):
        full = acc(z)
        for g in range(G):
            for p, ref in ((0, keep), (1, send)):
                blk = full[g * DB : (g + 1) * DB, p * LN : (p + 1) * LN]
                row = pick(t[0], p, rows_of[g, z, 0], rows_of[g, z, 1])
                ref[tab_a(t, g), tab_z(t, z)] = blk.astype(BF16)
                ref[tab_a(t, g), tab_z(t, z), 0:16, :] = jnp.where(spot, row, blk[:16]).astype(BF16)


def by_rows(body):
    def step(i, carry):
        body(pl.ds(pl.multiple_of(i * TM, TM), TM))
        return carry

    lax.fori_loop(0, L // TM, step, 0)


def values_body(t, x_ref, own_ref, oth_ref, n_ref, val_ref, gain_ref):
    gain_ref[0:1, :] = gains_row(own_ref, oth_ref, t, 0)
    gain_ref[1:2, :] = gains_row(own_ref, oth_ref, t, DB)

    def norm(at):
        cen, rstd = norm_stats(x_ref[at, :].astype(F32))
        n_ref[at, :] = (cen * rstd * gain_ref[0:1, :]).astype(BF16)

    by_rows(norm)
    for z in range(Z):
        val_ref[z] = dot(n_ref[...], weight_z(own_ref, oth_ref, t, z, 0), 1, 0).astype(BF16)


def probs_of(units, t, m, z, mask):
    parts = []
    for i in range(HZ):
        e = exp_scores(*units, t, m, HZ * z + i, mask)
        inv = 1.0 / jnp.sum(e, axis=-1, keepdims=True)
        parts.append(e * inv)
    return parts


def mixer_body(
    t, x_ref, gain_ref, dq_ref, dk_ref, val_ref, a_own, a_oth, b_own, b_oth, w_own, w_oth,
    mix_ref, mid_ref, n_ref,
):
    m = pl.program_id(0)
    core = t[0]
    base = m * TM
    k0 = pl.multiple_of(window(m) * KB, KB)
    mask = halves(dq_ref, core) == dk_ref[:, pl.ds(k0, WIN * KB)]
    heads = head_masks(core, TM)
    for z in range(Z):
        win = val_ref[z, pl.ds(k0, WIN * KB), :]
        prob = probs_of((a_own, a_oth, b_own, b_oth), t, m, z, mask)
        part = dot(jnp.concatenate([p.astype(BF16) for p in prob], axis=0), win, 1, 0)
        out = jnp.zeros((TM, GW), F32)
        for i in range(HZ):
            out = jnp.where(heads[i], part[i * TM : (i + 1) * TM], out)
        put_halves(mix_ref, core, out.astype(BF16), z, base)

    @pl.when(m == Z - 1)
    def _():
        acc = dot(mix_ref[0], weight_z(w_own, w_oth, t, 0, DB), 1, 1)
        for z in range(1, Z):
            acc = acc + dot(mix_ref[z], weight_z(w_own, w_oth, t, z, DB), 1, 1)
        mid_ref[...] = acc

        def norm(at):
            mid = x_ref[at, :].astype(F32) + mid_ref[at, :]
            mid_ref[at, :] = mid
            cen, rstd = norm_stats(mid)
            n_ref[at, :] = (cen * rstd * gain_ref[1:2, :]).astype(BF16)

        by_rows(norm)


def ffn_body(first, last, t, n_ref, c_ref, u_ref, d_ref, *refs):
    refs = list(refs)
    if not first:
        ia_ref, ib_ref = refs[:2]
        refs = refs[2:]
    if last:
        mid_ref = refs[0]
        refs = refs[1:]
    gu_ref, gd_ref, b_ref, a_ref = refs[:4]
    j = pl.program_id(0)
    n = n_ref[...]
    cot = c_ref[...]
    up_w = jnp.concatenate(
        [jnp.concatenate([u_ref[tab_b(t, g), i] for g in range(G)], axis=0) for i in range(ZS)], axis=1
    )
    dn_w = jnp.concatenate(
        [jnp.concatenate([d_ref[tab_a(t, g), i] for g in range(G)], axis=0) for i in range(ZS)], axis=1
    )

    @pl.when(j == 0)
    def _():
        if first:
            a_ref[...] = jnp.zeros_like(a_ref)
            b_ref[...] = jnp.zeros_like(b_ref)
        else:
            a_ref[...] = ia_ref[...]
            b_ref[...] = ib_ref[...]

    up = dot(n, up_w, 1, 0)
    sq = up * up
    th = jnp.tanh(GC * up * (1.0 + GA * sq))
    half = 0.5 + 0.5 * th
    act = (up * half).astype(BF16)
    slope = half + (0.5 * GC) * up * (1.0 - th * th) * (1.0 + (3.0 * GA) * sq)
    a_ref[...] += dot(act, dn_w, 1, 1)
    gd = dot(cot, act, 0, 0).astype(BF16)
    up_g = (dot(cot, dn_w, 1, 0) * slope).astype(BF16)
    gu = dot(n, up_g, 0, 0).astype(BF16)
    b_ref[...] += dot(up_g, up_w, 1, 1)
    for g in range(G):
        for i in range(ZS):
            part = slice(g * DB, (g + 1) * DB), slice(i * FB, (i + 1) * FB)
            gu_ref[tab_b(t, g), i] = gu[part]
            gd_ref[tab_a(t, g), i] = gd[part]
    if last:
        lo_ref = refs[4]

        @pl.when(j == Z // ZS - 1)
        def _():
            lo_ref[...] = (mid_ref[...] + a_ref[...]).astype(BF16)


def norm_back(cen, rstd, gain, dn):
    xhat = cen * rstd
    e = dn * gain
    dv = (
        e
        - jnp.mean(e, axis=-1, keepdims=True)
        - xhat * jnp.mean(e * xhat, axis=-1, keepdims=True)
    ) * rstd
    return dv, jnp.sum(dn * xhat, axis=0, keepdims=True)


def mixer_back_body(
    t, dn_ref, mid_ref, c_ref, gain_ref, dq_ref, dk_ref, mix_ref, val_ref,
    a_own, a_oth, b_own, b_oth, w_own, w_oth,
    mg_ref, ka_ref, sa_ref, kb_ref, sb_ref, ko_ref, so_ref, vg_ref, dg_acc, br_ref, grad_ref, vg_acc,
):
    m = pl.program_id(0)
    core = t[0]
    base = m * TM
    start = window(m)
    k0 = pl.multiple_of(start * KB, KB)

    @pl.when(m == 0)
    def _():
        vg_acc[...] = jnp.zeros_like(vg_acc)
        dg_acc[...] = jnp.zeros_like(dg_acc)

        def norm(at):
            cen, rstd = norm_stats(mid_ref[at, :])
            dv, dg = norm_back(cen, rstd, gain_ref[1:2, :], dn_ref[at, :])
            dg_acc[0:1, :] += dg
            mid_grad = c_ref[at, :].astype(F32) + dv
            mg_ref[at, :] = mid_grad
            br_ref[at, :] = mid_grad.astype(BF16)

        by_rows(norm)
        branch = br_ref[...]
        for z in range(Z):
            grad_ref[z] = dot(branch, weight_z(w_own, w_oth, t, z, DB), 1, 0).astype(BF16)
        put_weight_grads(
            lambda z: dot(branch, mix_ref[z], 0, 0), dg_acc[0:1, :], t, ko_ref, so_ref
        )

    mask = halves(dq_ref, core) == dk_ref[:, pl.ds(k0, WIN * KB)]
    heads = head_masks(core, TM)
    rest = tab_b(t, jnp.where(start == 0, G - 1, 0))
    ka_ref[rest, 0] = jnp.zeros((HR, KB), BF16)
    sa_ref[rest, 0] = jnp.zeros((HR, KB), BF16)
    for z in range(Z):
        grad = halves(grad_ref, core, z, base)
        mine = jnp.concatenate(
            [jnp.where(heads[i], grad, jnp.zeros_like(grad)) for i in range(HZ)], axis=0
        )
        win = val_ref[z, pl.ds(k0, WIN * KB), :]
        prob = probs_of((a_own, a_oth, b_own, b_oth), t, m, z, mask)
        dp = dot(mine, win, 1, 1)
        low = jnp.concatenate([p.astype(BF16) for p in prob], axis=0)
        vg_acc[z, pl.ds(k0, WIN * KB), :] += dot(low, mine, 0, 0)
        for i in range(HZ):
            head = HZ * z + i
            pd = prob[i] * dp[i * TM : (i + 1) * TM]
            ds = (pd - prob[i] * jnp.sum(pd, axis=-1, keepdims=True)).astype(BF16)
            for k in range(WIN):
                for p, (ra, rb) in enumerate(((ka_ref, kb_ref), (sa_ref, sb_ref))):
                    blk = ds[p * QB : (p + 1) * QB, k * KB : (k + 1) * KB]
                    if head < HA:
                        ra[tab_b(t, start + k), 0, head * QB : (head + 1) * QB, :] = blk
                    else:
                        h = head - HA
                        rb[0, k, h * QB : (h + 1) * QB, :] = blk

    @pl.when(m == Z - 1)
    def _():
        vg_ref[...] = vg_acc[...].astype(BF16)


def last_body(
    t, x_ref, gain_ref, n_ref, vg_ref, w_own, w_oth, mg_ref, gi_ref, kv_ref, sv_ref, dg_acc, dn_ref
):
    dg_acc[...] = jnp.zeros_like(dg_acc)
    acc = dot(vg_ref[0], weight_z(w_own, w_oth, t, 0, 0), 1, 1)
    for z in range(1, Z):
        acc = acc + dot(vg_ref[z], weight_z(w_own, w_oth, t, z, 0), 1, 1)
    dn_ref[...] = acc

    def norm(at):
        cen, rstd = norm_stats(x_ref[at, :].astype(F32))
        dv, dg = norm_back(cen, rstd, gain_ref[0:1, :], dn_ref[at, :])
        dg_acc[0:1, :] += dg
        gi_ref[at, :] = mg_ref[at, :] + dv

    by_rows(norm)
    low = n_ref[...]
    put_weight_grads(lambda z: dot(low, vg_ref[z], 0, 0), dg_acc[0:1, :], t, kv_ref, sv_ref)


def sds(shape, dtype):
    return jax.ShapeDtypeStruct(shape, dtype)


W_SHAPE = (G, Z, 2 * DB, LN)
V_SHAPE = (G, Z, DB, LN)
A_SHAPE = (G, Z, HR, KB)
B_SHAPE = (Z, WIN, HR, KB)
F_SHAPE = (G, Z, DB, FB)
Z_ROWS = pl.BlockSpec((Z, TM, GW), lambda i, t: (0, i, 0))


def run_values(tab, x, w):
    return call(
        values_body,
        (1,),
        [whole((L, D)), whole(W_SHAPE), whole(W_SHAPE)],
        [out_whole((L, D)), out_whole((Z, L, GW)), out_whole((8, D))],
        [sds((L, D), BF16), sds((Z, L, GW), BF16), sds((8, D), F32)],
        flops=2 * L * D * Z * GW,
        nbytes=6 << 20,
    )(tab, x, *w)


def run_mixer(tab, x, gain, dq, dk, vals, a, b, w):
    return call(
        mixer_body,
        (L // TM,),
        [
            whole((L, D)), whole((8, D)), rows(1), whole((1, L)), whole((Z, L, GW)),
            whole(A_SHAPE), whole(A_SHAPE), whole(B_SHAPE), whole(B_SHAPE),
            whole(W_SHAPE), whole(W_SHAPE),
        ],
        [out_whole((Z, L, GW)), out_whole((L, D)), out_whole((L, D))],
        [sds((Z, L, GW), BF16), sds((L, D), F32), sds((L, D), BF16)],
        flops=2 * L * D * Z * GW + 2 * H * L * WIN * KB * GW,
        nbytes=14 << 20,
    )(tab, x, gain, dq, dk, vals, *a, *b, *w)


def run_ffn(tab, n, cot, u_w, d_w, acc=None, mid=None):
    first, last = acc is None, mid is not None
    blk = pl.BlockSpec((G, ZS, DB, FB), lambda i, t: (0, i, 0, 0))
    in_specs = [whole((L, D)), whole((L, D)), blk, blk]
    args = [tab, n, cot, u_w, d_w]
    if not first:
        in_specs += [whole((L, D)), whole((L, D))]
        args += list(acc)
    if last:
        in_specs += [whole((L, D))]
        args += [mid]
    out_specs = [blk, blk, out_whole((L, D))]
    outs = [sds(F_SHAPE, BF16), sds(F_SHAPE, BF16), sds((L, D), F32)]
    scratch = ()
    if last:
        scratch = (pltpu.VMEM((L, D), F32),)
        out_specs += [out_whole((L, D))]
        outs += [sds((L, D), BF16)]
    else:
        out_specs += [out_whole((L, D))]
        outs += [sds((L, D), F32)]

    def body(t, *refs):
        if last:
            refs = list(refs)
            refs = refs[:-2] + [refs[-1], refs[-2]]
        ffn_body(first, last, t, *refs)

    return call(
        body, (Z // ZS,), in_specs, out_specs, outs, scratch, flops=6 * L * D * FF, nbytes=20 << 20
    )(*args)


def run_mixer_back(tab, dn, mid, cot, gain, dq, dk, mixed, vals, a, b, w):
    blk_a = pl.BlockSpec((G, 1, HR, KB), lambda i, t: (0, tab_z(t, i), 0, 0))
    blk_b = pl.BlockSpec((1, WIN, HR, KB), lambda i, t: (tab_z(t, i), 0, 0, 0))
    return call(
        mixer_back_body,
        (L // TM,),
        [
            whole((L, D)), whole((L, D)), whole((L, D)), whole((8, D)), rows(1), whole((1, L)),
            whole((Z, L, GW)), whole((Z, L, GW)), whole(A_SHAPE), whole(A_SHAPE), whole(B_SHAPE), whole(B_SHAPE),
            whole(W_SHAPE), whole(W_SHAPE),
        ],
        [out_whole((L, D)), blk_a, blk_a, blk_b, blk_b, out_whole(V_SHAPE), out_whole(V_SHAPE), out_whole((Z, L, GW))],
        [
            sds((L, D), F32), sds(A_SHAPE, BF16), sds(A_SHAPE, BF16), sds(B_SHAPE, BF16),
            sds(B_SHAPE, BF16), sds(V_SHAPE, BF16), sds(V_SHAPE, BF16), sds((Z, L, GW), BF16),
        ],
        scratch=(
            pltpu.VMEM((8, D), F32), pltpu.VMEM((L, D), BF16), pltpu.VMEM((Z, L, GW), BF16),
            pltpu.VMEM((Z, L, GW), F32),
        ),
        flops=4 * L * D * Z * GW + 6 * H * L * WIN * KB * GW,
        nbytes=28 << 20,
    )(tab, dn, mid, cot, gain, dq, dk, mixed, vals, *a, *b, *w)


def run_last(tab, x, gain, low, vg, w, mid_grad):
    return call(
        last_body,
        (1,),
        [
            whole((L, D)), whole((8, D)), whole((L, D)), whole((Z, L, GW)), whole(W_SHAPE),
            whole(W_SHAPE), whole((L, D)),
        ],
        [out_whole((L, D)), out_whole(V_SHAPE), out_whole(V_SHAPE)],
        [sds((L, D), F32), sds(V_SHAPE, BF16), sds(V_SHAPE, BF16)],
        scratch=(pltpu.VMEM((8, D), F32), pltpu.VMEM((L, D), F32)),
        flops=4 * L * D * Z * GW,
        nbytes=12 << 20,
    )(tab, x, gain, low, vg, *w, mid_grad)


def add_up(terms):
    total = terms[0].astype(F32)
    for term in terms[1:]:
        total = total + term.astype(F32)
    return total


def after(val, *deps):
    return lax.optimization_barrier((val, deps))[0]


class Grid:
    def __init__(self, gx, gy):
        self.gy = gy
        self.size = {"y": gx // 2, "x": 2, "z": gy // 2, "c": 2}
        i, j = lax.axis_index("gx"), lax.axis_index("gy")
        self.at = {"y": i // 2, "x": i % 2, "z": j // 2, "c": j % 2}

    def fetch(self, val, axis, k):
        sizes = self.size
        pairs = []
        for y in range(sizes["y"]):
            for x in range(sizes["x"]):
                for z in range(sizes["z"]):
                    for c in range(sizes["c"]):
                        src = {"y": y, "x": x, "z": z, "c": c}
                        dst = dict(src)
                        dst[axis] = src[axis] ^ k
                        pairs.append(tuple((p["y"] * 2 + p["x"]) * self.gy + p["z"] * 2 + p["c"] for p in (src, dst)))
        return lax.ppermute(val, ("gx", "gy"), pairs)

    def rel(self, axis, v):
        return self.at[axis] ^ v

    def spread(self, val, axis):
        return jnp.stack([val] + [self.fetch(val, axis, k) for k in range(1, self.size[axis])])

    def reduce(self, terms, stage, axis, *deps):
        if deps:
            terms = terms[:-1] + [(after(terms[-1][0], *deps), terms[-1][1])]
        got = []
        for k in range(1, self.size[axis]):
            part = add_up([v[(0,) * (stage - born) + (k,)] for v, born in terms]).astype(BF16)
            got.append((self.fetch(part, axis, k), stage + 1))
        return terms + got

    def total(self, terms, stage):
        return add_up([v[(0,) * (stage - born)] for v, born in terms])

    def reduce_joined(self, groups, axis, *deps):
        groups = list(groups)
        if deps:
            groups[-1] = groups[-1][:-1] + [(after(groups[-1][-1][0], *deps), groups[-1][-1][1])]
        got = []
        for k in range(1, self.size[axis]):
            parts = [
                add_up([v[(0,) * (2 - born) + (k,)] for v, born in terms]).astype(BF16)
                for terms in groups
            ]
            got.append(self.fetch(jnp.concatenate(parts, axis=0), axis, k))
        out, at_row = [], 0
        for terms in groups:
            n = terms[0][0].shape[-2]
            own = [v[(0,) * (3 - born)] for v, born in terms]
            out.append(add_up(own + [v[at_row : at_row + n] for v in got]))
            at_row += n
        return out


def compute(tab, x, docs, cot, a, b, w, u, d):
    dq, dk = docs.reshape(L, 1), docs
    low, vals, gain = run_values(tab, x, w)
    mixed, mid, n_two = run_mixer(tab, x, gain, dq, dk, vals, a, b, w)
    gu0, gd0, acc_b, acc_a = run_ffn(tab, n_two, cot, u[0], d[0])
    gu1, gd1, n_grad, layer_out = run_ffn(tab, n_two, cot, u[1], d[1], (acc_a, acc_b), mid)
    mid_grad, ka, sa, kb, sb, ko, so, vg = run_mixer_back(
        tab, n_grad, mid, cot, gain, dq, dk, mixed, vals, a, b, w
    )
    grad_in, kv, sv = run_last(tab, x, gain, low, vg, w, mid_grad)
    return layer_out, grad_in, (gu0, gu1), (gd0, gd1), (ka, sa), (kb, sb), (ko, so), (kv, sv)


def lane_pad(mat, gains):
    row = jnp.pad(gains.reshape(1, GN), ((0, DB - 1), (0, LN - CB - GN)))
    return jnp.concatenate([mat, row], axis=1)


def small_shards(layer_in, doc_ids, mix_gain, value_w, mixing, output_w, ffn_gain, up_w, down_w, cot):
    grid = Grid(G, 2 * Z)
    at = grid.at
    order_a = [grid.rel("x", g % 2) * 2 + grid.rel("y", g // 2) for g in range(G)]
    order_b = [grid.rel("y", g // 2) * 2 + grid.rel("x", g % 2) for g in range(G)]
    order_z = [grid.rel("z", z) for z in range(Z)]
    tab = jnp.stack([at["c"]] + order_a + order_b + order_z).astype(jnp.int32)
    docs = lax.dynamic_slice_in_dim(doc_ids, lax.axis_index("gy"), 1, 0)

    dq, dk = docs.reshape(L, 1), docs
    mix = mixing.reshape(2, HR, KB)
    fetch, spread = grid.fetch, grid.spread
    wts = jnp.concatenate([lane_pad(value_w, mix_gain), lane_pad(output_w.T, ffn_gain)], axis=0)

    def both(val, *deps):
        return val, fetch(after(val, *deps) if deps else val, "c", 1)

    def along_z(val):
        return [val] + [fetch(val, "z", k) for k in range(1, Z)]

    c1 = along_z(jnp.concatenate([mix[0], wts], axis=0))
    b = spread(spread(mix[1], "x"), "y").reshape(G, HR, KB)
    start = window(at["z"])
    order = jnp.stack(order_b)
    b = jnp.stack([lax.dynamic_index_in_dim(b, order[start + i], 0, False) for i in range(WIN)])
    a, w = (jnp.stack([v[i * HR : (i + 1) * HR] for v in c1]) for i in range(2))
    ffn = along_z(after(jnp.stack([up_w, down_w.T]), c1[1:]))
    a, w = after((a, w), b)
    a, w = spread(a, "x"), spread(w, "y")
    a, w = after((a, w), ffn[1])
    a, w = spread(a, "y").reshape(A_SHAPE), spread(w, "x").reshape(W_SHAPE)
    a, w = after((a, w), ffn[2:])
    b = spread(after(b, ffn[1:]), "z")
    u, d = (jnp.stack([v[i] for v in ffn]) for i in range(2))
    w, a = both(w), both(a)
    low, vals, gain = run_values(tab, layer_in, w)
    u, d = spread(u, "x"), spread(d, "y")
    b = both(b, u, d)
    u, d = spread(u, "y").reshape(F_SHAPE), spread(d, "x").reshape(F_SHAPE)
    mixed, mid, n_two = run_mixer(tab, layer_in, after(gain, u, d), dq, dk, vals, a, b, w)
    u, d = both(u), both(d)

    def begin(keep, send):
        got = fetch(send, "c", 1)
        return [(v.reshape((2, 2) + v.shape[1:]), 0) for v in (keep, got)]

    def last(*groups):
        return [terms[-1][0] for terms in groups]

    su, sd, acc_b, acc_a = run_ffn(tab, n_two, cot, u[1], d[1])
    ku, kd, n_grad, layer_out = run_ffn(tab, n_two, cot, u[0], d[0], (acc_a, acc_b), mid)
    gu, gd = begin(ku, su), begin(kd, sd)
    n_grad = after(n_grad, last(gu, gd))
    gu, gd = grid.reduce(gu, 0, "y"), grid.reduce(gd, 0, "x")
    mid_grad, ka, sa, kb, sb, ko, so, vg = run_mixer_back(
        tab, n_grad, mid, cot, gain, dq, dk, mixed, vals, a, b, w
    )
    vg = after(vg, last(gu, gd))
    gu, gd = grid.reduce(gu, 1, "x", sa), grid.reduce(gd, 1, "y", sa)
    grad_in, kv, sv = run_last(tab, layer_in, gain, low, vg, w, mid_grad)
    sa, sb, so = after((sa, sb, so), sv)
    gv, ga, go, rb = begin(kv, sv), begin(ka, sa), begin(ko, so), fetch(sb, "c", 1)
    gb = grid.reduce([(kb, 2), (rb, 2)], 2, "z")
    ga = grid.reduce(ga, 0, "y")
    go = grid.reduce(go, 0, "x")
    gu, gd = grid.reduce_joined((gu, gd), "z", last(gb))
    gv = grid.reduce(gv, 0, "x")
    wide = grid.total(gb, 3)
    blocks = []
    for k in range(G):
        spot = (at["y"] - k // 2) % 2 * 2 + (at["x"] - k % 2) % 2 - start
        blk = lax.dynamic_index_in_dim(wide, jnp.clip(spot, 0, WIN - 1), 0, False)
        ok = jnp.logical_and(spot >= 0, spot < WIN)
        blocks.append(jnp.where(ok, blk, jnp.zeros_like(blk)))
    gb = [(jnp.stack(blocks).reshape(2, 2, HR, KB), 0)]
    gb = grid.total(grid.reduce(grid.reduce(gb, 0, "y"), 1, "x"), 2)
    ga, go = grid.reduce(ga, 1, "x"), grid.reduce(go, 1, "y")
    gv = grid.reduce(gv, 1, "y")
    ga, go, gv = grid.reduce_joined((ga, go, gv), "z")

    grad_mixing = jnp.concatenate([ga, gb], axis=0).reshape(H, QB, KB)
    return (
        layer_out, grad_in, gv[0, CB : CB + GN], gv[:, :CB], grad_mixing, go[:, :CB].T,
        go[0, CB : CB + GN], gu, gd.T,
    )


def cols_in(v, o, gains):
    def blocks(mat, gain):
        mat = mat.reshape(G, DB, Z, 2, CB).transpose(3, 0, 2, 1, 4)
        gain = gain.reshape(G, Z, 2, 1, GN).transpose(2, 0, 1, 3, 4)
        gain = jnp.pad(gain, ((0, 0),) * 3 + ((0, DB - 1), (0, LN - CB - GN)))
        return jnp.concatenate([mat, gain], axis=-1)

    return jnp.concatenate([blocks(v, gains[0]), blocks(o, gains[1])], axis=3)


def cols_out(keep, send):
    mat = jnp.stack([keep, send])
    dg = mat[:, :, :, 0, CB : CB + GN].transpose(1, 2, 0, 3).reshape(D)
    return mat[..., :CB].transpose(1, 3, 2, 0, 4).reshape(D, D), dg


def any_shards(layer_in, doc_ids, mix_gain, value_w, mixing, output_w, ffn_gain, up_w, down_w, cot):
    ax = ("gx", "gy")
    seqs = layer_in.shape[0] // L
    me = lax.axis_index("gy") * seqs

    def gather(arr, d0, d1):
        arr = lax.all_gather(arr, "gx", axis=d0, tiled=True)
        return lax.all_gather(arr, "gy", axis=d1, tiled=True)

    def scatter(arr, d0, d1):
        arr = lax.psum_scatter(arr, "gx", scatter_dimension=d0, tiled=True)
        return lax.psum_scatter(arr, "gy", scatter_dimension=d1, tiled=True).astype(F32)

    gains = lax.all_gather(jnp.stack([mix_gain, ffn_gain]), ax, axis=1, tiled=True)
    w = cols_in(gather(value_w, 0, 1), gather(output_w.T, 0, 1), gains)
    mix_full = gather(mixing, 2, 1).reshape(2, HA, Z, 2, QB, G, KB).transpose(0, 3, 5, 2, 1, 4, 6)
    mix_full = mix_full.reshape(2, 2, G, Z, HR, KB)
    a = mix_full[0]
    starts = [min(max(m - 1, 0), G - WIN) for m in range(Z)]
    b = jnp.stack([mix_full[1][:, s : s + WIN, m] for m, s in enumerate(starts)], axis=1)
    u = gather(up_w, 0, 1).reshape(G, DB, Z, 2, FB).transpose(3, 0, 2, 1, 4)
    d = gather(down_w.T, 0, 1).reshape(G, DB, Z, 2, FB).transpose(3, 0, 2, 1, 4)
    tab = jnp.array([0] + [0, 1, 2, 3] * 3, jnp.int32)

    rows_out, grads = [], None
    for s in range(seqs):
        docs = lax.dynamic_slice_in_dim(doc_ids, me + s, 1, 0)
        part = slice(s * L, (s + 1) * L)
        out, g_in, *rest = compute(tab, layer_in[part], docs, cot[part], a, b, w, u, d)
        rows_out.append((out, g_in))
        rest = jax.tree.map(lambda v: v.astype(F32), rest) if seqs > 1 else rest
        grads = rest if grads is None else jax.tree.map(jnp.add, grads, rest)
    layer_out = jnp.concatenate([r[0] for r in rows_out], axis=0)
    grad_in = jnp.concatenate([r[1] for r in rows_out], axis=0)
    gu, gd, ga, gb, go, gv = jax.tree.map(lambda v: v.astype(BF16), grads)

    def ffn_out(pair):
        return jnp.stack(pair).transpose(1, 3, 2, 0, 4).reshape(D, FF)

    value_full, dg_one = cols_out(*gv)
    output_full, dg_two = cols_out(*go)
    ga, gb = jnp.stack(ga), jnp.stack(gb)
    gb = jnp.stack(
        [
            jnp.pad(gb[:, m], ((0, 0), (s, G - WIN - s), (0, 0), (0, 0)))
            for m, s in enumerate(starts)
        ],
        axis=2,
    )
    gm = jnp.stack([ga, gb]).reshape(2, 2, G, Z, HA, QB, KB).transpose(0, 4, 3, 1, 5, 2, 6)
    dgs = jnp.stack([dg_one, dg_two]).astype(F32)
    dgs = lax.psum_scatter(dgs, ax, scatter_dimension=1, tiled=True)
    return (
        layer_out, grad_in, dgs[0], scatter(value_full, 0, 1), scatter(gm.reshape(H, L, L), 2, 1),
        scatter(output_full, 0, 1).T, dgs[1], scatter(ffn_out(gu), 0, 1), scatter(ffn_out(gd), 0, 1).T,
    )


def solution(mesh):
    tok = P(("gx", "gy"), None)
    vec = P(("gx", "gy"))
    wgt = P("gx", "gy")
    twg = P("gy", "gx")
    mix = P(None, "gy", "gx")
    in_specs = (tok, P("gx", None), vec, wgt, mix, twg, vec, wgt, twg, tok)
    out_specs = (tok, tok, vec, wgt, mix, twg, vec, wgt, twg)

    def run(*args):
        small = (mesh.shape["gx"], mesh.shape["gy"], args[0].shape[0]) == (G, 2 * Z, L)
        return (small_shards if small else any_shards)(*args)

    return jax.shard_map(run, mesh=mesh, in_specs=in_specs, out_specs=out_specs, check_vma=False)
```

```python
import functools

import jax
import jax.numpy as jnp
from jax import lax
from jax.experimental import pallas as pl
from jax.experimental.pallas import tpu as pltpu
from jax.sharding import PartitionSpec as P

D = 768
H = 12
HS = 64
FF = 3072
L = 512
EPS = 1e-05
G = 4
Z = 4
DB = D // G
CB = D // (2 * Z)
FB = FF // (2 * Z)
QB = L // (2 * Z)
KB = L // G
LN = 128
GW = 2 * LN
GN = CB // 4
HA = H // 2
ZS = 2
HR = HA * QB
TM = 128
WIN = 3
HZ = H // Z
GC = 0.7978845608
GA = 0.044715
VMEM_LIMIT = 40 * 1024 * 1024
COST = 1 << 38

F32 = jnp.float32
BF16 = jnp.bfloat16


def dot(a, b, ca, cb):
    return lax.dot_general(a, b, (((ca,), (cb,)), ((), ())), preferred_element_type=F32)


def call(body, grid, in_specs, out_specs, out_shape, scratch=(), flops=0, nbytes=0, vmem=VMEM_LIMIT):
    return pl.pallas_call(
        body,
        grid_spec=pltpu.PrefetchScalarGridSpec(
            num_scalar_prefetch=1,
            grid=grid,
            in_specs=in_specs,
            out_specs=out_specs,
            scratch_shapes=list(scratch),
        ),
        out_shape=out_shape,
        compiler_params=pltpu.CompilerParams(
            dimension_semantics=("arbitrary",) * len(grid), vmem_limit_bytes=vmem
        ),
        cost_estimate=pl.CostEstimate(flops=COST, bytes_accessed=nbytes, transcendentals=0),
    )


def whole(shape):
    return pl.BlockSpec(memory_space=pltpu.VMEM)


def rows(width):
    return pl.BlockSpec((TM, width), lambda i, t: (i, 0))


def out_whole(shape):
    return pl.BlockSpec(memory_space=pltpu.VMEM)


def tab_a(t, g):
    return t[1 + g]


def tab_b(t, g):
    return t[1 + G + g]


def tab_z(t, z):
    return t[1 + 2 * G + z]


def g_of(t, r, order_b):
    return t[1 + 2 * G + Z] ^ (r if order_b else (r % 2) * 2 + r // 2)


def norm_stats(x):
    mean = jnp.mean(x, axis=-1, keepdims=True)
    cen = x - mean
    rstd = lax.rsqrt(jnp.mean(cen * cen, axis=-1, keepdims=True) + EPS)
    return cen, rstd


def weight_z(own, oth, t, z, base):
    parts = [
        jnp.concatenate(
            [ref[tab_a(t, g), tab_z(t, z), base : base + DB, :] for g in range(G)], axis=0
        )
        for ref in (own, oth)
    ]
    return jnp.concatenate(parts, axis=1)


def head_masks(core, nrows):
    lane = lax.broadcasted_iota(jnp.int32, (nrows, GW), 1)
    tile = lane // LN
    place = lane - tile * LN
    side = jnp.where(core == 0, tile, 1 - tile)
    col = jnp.where(place < CB, side * CB + place, -1)
    return [jnp.logical_and(col >= HS * i, col < HS * (i + 1)) for i in range(HZ)]


def halves(ref, core, lead=None, base=0):
    lo = pl.multiple_of(base + core * QB, QB)
    hi = pl.multiple_of(base + (1 - core) * QB, QB)
    if lead is None:
        return jnp.concatenate([ref[pl.ds(lo, QB), :], ref[pl.ds(hi, QB), :]], axis=0)
    return jnp.concatenate([ref[lead, pl.ds(lo, QB), :], ref[lead, pl.ds(hi, QB), :]], axis=0)


def put_halves(ref, core, val, lead=None, base=0):
    lo = pl.multiple_of(base + core * QB, QB)
    hi = pl.multiple_of(base + (1 - core) * QB, QB)
    if lead is None:
        ref[pl.ds(lo, QB), :] = val[:QB]
        ref[pl.ds(hi, QB), :] = val[QB:]
    else:
        ref[lead, pl.ds(lo, QB), :] = val[:QB]
        ref[lead, pl.ds(hi, QB), :] = val[QB:]


def window(m):
    return jnp.clip(m - 1, 0, G - WIN)


def exp_scores(a_own, a_oth, b_own, b_oth, t, m, head, mask):
    parts = []
    for i in range(WIN):
        both = []
        for a, b in ((a_own, b_own), (a_oth, b_oth)):
            if head < HA:
                both.append(a[tab_b(t, window(m) + i), tab_z(t, m), head * QB : (head + 1) * QB, :])
            else:
                h = head - HA
                both.append(b[tab_z(t, m), i, h * QB : (h + 1) * QB, :])
        parts.append(jnp.concatenate(both, axis=0))
    scores = jnp.concatenate(parts, axis=1).astype(F32)
    return jnp.where(mask, jnp.exp(scores), 0.0)


def gain_spots():
    for g in range(G):
        for z in range(Z):
            for c in range(2):
                yield g, z, c, DB * g + (2 * GN) * z + GN * c


def pick(core, c, own, oth):
    return jnp.where(core == c, own, oth)


def gains_row(own, oth, t, base):
    lane = lax.broadcasted_iota(jnp.int32, (1, LN), 1)
    tiles = [jnp.zeros((1, LN), F32) for _ in range(D // LN)]
    for g, z, c, at in gain_spots():
        a, b = (r[tab_a(t, g), tab_z(t, z), base : base + 16, :].astype(F32)[:1] for r in (own, oth))
        row = pick(t[0], c, a, b)
        tile, off = at // LN, at % LN
        row = pltpu.roll(row, (off - CB) % LN, 1)
        tiles[tile] = jnp.where(jnp.logical_and(lane >= off, lane < off + GN), row, tiles[tile])
        if off + GN > LN:
            tiles[tile + 1] = jnp.where(lane < off + GN - LN, row, tiles[tile + 1])
    return jnp.concatenate(tiles, axis=1)


def with_gains(full, dg, t):
    lane = lax.broadcasted_iota(jnp.int32, (1, LN), 1)
    top = lax.broadcasted_iota(jnp.int32, (16, LN), 0) == 0
    spot = jnp.logical_and(top, jnp.logical_and(lane >= CB, lane < CB + GN))
    rows_of = {}
    for g, z, c, at in gain_spots():
        tile, off = at // LN, at % LN
        row = dg[:, tile * LN : (tile + 1) * LN]
        if off + GN > LN:
            row = jnp.where(lane < off, dg[:, (tile + 1) * LN : (tile + 2) * LN], row)
        rows_of[g, z, c] = pltpu.roll(row, (CB - off) % LN, 1)
    for z in range(Z):
        for g in range(G):
            for p in range(2):
                row = pick(t[0], p, rows_of[g, z, 0], rows_of[g, z, 1])
                at = z, slice(g * DB, g * DB + 16), slice(p * LN, (p + 1) * LN)
                full[at] = jnp.where(spot, row, full[at].astype(F32)).astype(BF16)


def by_rows(body):
    def step(i, carry):
        body(pl.ds(pl.multiple_of(i * TM, TM), TM))
        return carry

    lax.fori_loop(0, L // TM, step, 0)


def values_body(t, x_ref, own_ref, oth_ref, n_ref, val_ref, gain_ref):
    gain_ref[0:1, :] = gains_row(own_ref, oth_ref, t, 0)
    gain_ref[1:2, :] = gains_row(own_ref, oth_ref, t, DB)

    def norm(at):
        cen, rstd = norm_stats(x_ref[at, :].astype(F32))
        n_ref[at, :] = (cen * rstd * gain_ref[0:1, :]).astype(BF16)

    by_rows(norm)
    for z in range(Z):
        val_ref[z] = dot(n_ref[...], weight_z(own_ref, oth_ref, t, z, 0), 1, 0).astype(BF16)


def probs_of(units, t, m, z, mask):
    parts = []
    for i in range(HZ):
        e = exp_scores(*units, t, m, HZ * z + i, mask)
        inv = 1.0 / jnp.sum(e, axis=-1, keepdims=True)
        parts.append(e * inv)
    return parts


def mixer_body(
    t, x_ref, gain_ref, dq_ref, dk_ref, val_ref, a_own, a_oth, b_own, b_oth, w_own, w_oth,
    mix_ref, mid_ref, n_ref,
):
    m = pl.program_id(0)
    core = t[0]
    base = m * TM
    k0 = pl.multiple_of(window(m) * KB, KB)
    mask = halves(dq_ref, core) == dk_ref[:, pl.ds(k0, WIN * KB)]
    heads = head_masks(core, TM)
    for z in range(Z):
        win = val_ref[z, pl.ds(k0, WIN * KB), :]
        prob = probs_of((a_own, a_oth, b_own, b_oth), t, m, z, mask)
        part = dot(jnp.concatenate([p.astype(BF16) for p in prob], axis=0), win, 1, 0)
        out = jnp.zeros((TM, GW), F32)
        for i in range(HZ):
            out = jnp.where(heads[i], part[i * TM : (i + 1) * TM], out)
        put_halves(mix_ref, core, out.astype(BF16), z, base)

    @pl.when(m == Z - 1)
    def _():
        acc = dot(mix_ref[0], weight_z(w_own, w_oth, t, 0, DB), 1, 1)
        for z in range(1, Z):
            acc = acc + dot(mix_ref[z], weight_z(w_own, w_oth, t, z, DB), 1, 1)
        mid_ref[...] = acc

        def norm(at):
            mid = x_ref[at, :].astype(F32) + mid_ref[at, :]
            mid_ref[at, :] = mid
            cen, rstd = norm_stats(mid)
            n_ref[at, :] = (cen * rstd * gain_ref[1:2, :]).astype(BF16)

        by_rows(norm)


def ffn_body(pair, t, *refs):
    refs = list(refs)
    n_refs, refs = refs[: 1 + pair], refs[1 + pair :]
    c_refs, refs = refs[: 1 + pair], refs[1 + pair :]
    u_refs, d_refs = refs[:2], refs[2:4]
    ku, su, kd, sd = refs[4:8]
    out_refs = refs[8:]
    n_all, c_all, a_acc, b_acc, gu_all, gd_all = out_refs[2 + 2 * pair :]
    out_refs = out_refs[: 2 + 2 * pair]
    j = pl.program_id(0)

    @pl.when(j == 0)
    def _():
        for i in range(1 + pair):
            n_all[i * L : (i + 1) * L] = n_refs[i][...]
            c_all[i * L : (i + 1) * L] = c_refs[i][...]
        a_acc[...] = jnp.zeros_like(a_acc)
        b_acc[...] = jnp.zeros_like(b_acc)

    n, cot = n_all[...], c_all[...]
    def weights(parts, tab):
        cols = []
        for i in range(ZS):
            blocks = []
            for g in range(G):
                at = tab(t, g)
                one, two = (r[at % 2, i] for r in parts)
                blocks.append(jnp.where(at < 2, one, two))
            cols.append(jnp.concatenate(blocks, axis=0))
        return jnp.concatenate(cols, axis=1)

    up_w, dn_w = weights(u_refs, tab_b), weights(d_refs, tab_a)
    up = dot(n, up_w, 1, 0)
    sq = up * up
    th = jnp.tanh(GC * up * (1.0 + GA * sq))
    half = 0.5 + 0.5 * th
    act = (up * half).astype(BF16)
    slope = half + (0.5 * GC) * up * (1.0 - th * th) * (1.0 + (3.0 * GA) * sq)
    a_acc[...] += dot(act, dn_w, 1, 1)
    gd_all[...] = dot(cot, act, 0, 0).astype(BF16)
    up_g = (dot(cot, dn_w, 1, 0) * slope).astype(BF16)
    gu_all[...] = dot(n, up_g, 0, 0).astype(BF16)
    b_acc[...] += dot(up_g, up_w, 1, 1)
    for src, order_b, keep, send in ((gu_all, True, ku, su), (gd_all, False, kd, sd)):
        for r in range(G):
            at = pl.ds(pl.multiple_of(g_of(t, r, order_b) * DB, DB), DB)
            for i in range(ZS):
                (keep, send)[r // 2][r % 2, i] = src[at, i * FB : (i + 1) * FB]

    @pl.when(j == Z // ZS - 1)
    def _():
        for i in range(1 + pair):
            part = slice(i * L, (i + 1) * L)
            out_refs[i][...] = a_acc[part].astype(out_refs[i].dtype)
            out_refs[1 + pair + i][...] = b_acc[part].astype(out_refs[1 + pair + i].dtype)


def norm_back(cen, rstd, gain, dn):
    xhat = cen * rstd
    e = dn * gain
    dv = (
        e
        - jnp.mean(e, axis=-1, keepdims=True)
        - xhat * jnp.mean(e * xhat, axis=-1, keepdims=True)
    ) * rstd
    return dv, jnp.sum(dn * xhat, axis=0, keepdims=True)


def mixer_back_body(
    t, dna_ref, dnb_ref, mid_ref, c_ref, gain_ref, dq_ref, dk_ref, mix_ref, val_ref,
    a_own, a_oth, b_own, b_oth, w_own, w_oth,
    mg_ref, ka_ref, sa_ref, kb_ref, sb_ref, vg_ref, dg_acc, br_ref, grad_ref, vg_acc, go_ref,
):
    m = pl.program_id(0)
    core = t[0]
    base = m * TM
    start = window(m)
    k0 = pl.multiple_of(start * KB, KB)

    @pl.when(m == 0)
    def _():
        vg_acc[...] = jnp.zeros_like(vg_acc)
        dg_acc[...] = jnp.zeros_like(dg_acc)

        def norm(at):
            cen, rstd = norm_stats(mid_ref[at, :])
            dn = dna_ref[at, :] + dnb_ref[at, :].astype(F32)
            dv, dg = norm_back(cen, rstd, gain_ref[1:2, :], dn)
            dg_acc[0:1, :] += dg
            mid_grad = c_ref[at, :].astype(F32) + dv
            mg_ref[at, :] = mid_grad
            br_ref[at, :] = mid_grad.astype(BF16)

        by_rows(norm)
        branch = br_ref[...]
        for z in range(Z):
            grad_ref[z] = dot(branch, weight_z(w_own, w_oth, t, z, DB), 1, 0).astype(BF16)
            go_ref[z] = dot(branch, mix_ref[z], 0, 0).astype(BF16)
        with_gains(go_ref, dg_acc[0:1, :], t)

    mask = halves(dq_ref, core) == dk_ref[:, pl.ds(k0, WIN * KB)]
    heads = head_masks(core, TM)
    for g in range(G):
        for p, ref in ((0, ka_ref), (1, sa_ref)):
            ref[tab_b(t, g), 0, HR:, :] = go_ref[m, g * DB : (g + 1) * DB, p * LN : (p + 1) * LN]
    rest = jnp.where(start == 0, G - 1, 0)
    for ref, tab in ((ka_ref, tab_b), (sa_ref, tab_b), (kb_ref, tab_a), (sb_ref, tab_a)):
        ref[tab(t, rest), 0, 0:HR, :] = jnp.zeros((HR, KB), BF16)
    for z in range(Z):
        grad = halves(grad_ref, core, z, base)
        mine = jnp.concatenate(
            [jnp.where(heads[i], grad, jnp.zeros_like(grad)) for i in range(HZ)], axis=0
        )
        win = val_ref[z, pl.ds(k0, WIN * KB), :]
        prob = probs_of((a_own, a_oth, b_own, b_oth), t, m, z, mask)
        dp = dot(mine, win, 1, 1)
        low = jnp.concatenate([p.astype(BF16) for p in prob], axis=0)
        vg_acc[z, pl.ds(k0, WIN * KB), :] += dot(low, mine, 0, 0)
        for i in range(HZ):
            head = HZ * z + i
            pd = prob[i] * dp[i * TM : (i + 1) * TM]
            ds = (pd - prob[i] * jnp.sum(pd, axis=-1, keepdims=True)).astype(BF16)
            low_half = head < HA
            row = (head if low_half else head - HA) * QB
            tab = tab_b if low_half else tab_a
            for k in range(WIN):
                for p, ref in enumerate((ka_ref, sa_ref) if low_half else (kb_ref, sb_ref)):
                    ref[tab(t, start + k), 0, row : row + QB, :] = ds[
                        p * QB : (p + 1) * QB, k * KB : (k + 1) * KB
                    ]

    @pl.when(m == Z - 1)
    def _():
        vg_ref[...] = vg_acc[...].astype(BF16)


def last_body(
    t, x_ref, gain_ref, n_ref, vg_ref, w_own, w_oth, mg_ref, gi_ref, kv_ref, sv_ref, dg_acc, dn_ref,
    gv_ref,
):
    dg_acc[...] = jnp.zeros_like(dg_acc)
    acc = dot(vg_ref[0], weight_z(w_own, w_oth, t, 0, 0), 1, 1)
    for z in range(1, Z):
        acc = acc + dot(vg_ref[z], weight_z(w_own, w_oth, t, z, 0), 1, 1)
    dn_ref[...] = acc

    def norm(at):
        cen, rstd = norm_stats(x_ref[at, :].astype(F32))
        dv, dg = norm_back(cen, rstd, gain_ref[0:1, :], dn_ref[at, :])
        dg_acc[0:1, :] += dg
        gi_ref[at, :] = mg_ref[at, :] + dv

    by_rows(norm)
    low = n_ref[...]
    for z in range(Z):
        gv_ref[z] = dot(low, vg_ref[z], 0, 0).astype(BF16)
    with_gains(gv_ref, dg_acc[0:1, :], t)
    for z in range(Z):
        for g in range(G):
            for p, ref in ((0, kv_ref), (1, sv_ref)):
                blk = gv_ref[z, g * DB : (g + 1) * DB, p * LN : (p + 1) * LN]
                ref[tab_a(t, g), tab_z(t, z)] = blk


def sds(shape, dtype):
    return jax.ShapeDtypeStruct(shape, dtype)


W_SHAPE = (G, Z, 2 * DB, LN)
V_SHAPE = (G, Z, DB, LN)
A_SHAPE = (G, Z, HR, KB)
AO_SHAPE = (G, Z, HR + DB, KB)
B_SHAPE = (Z, WIN, HR, KB)
F_SHAPE = (G, Z, DB, FB)
Z_ROWS = pl.BlockSpec((Z, TM, GW), lambda i, t: (0, i, 0))


def run_values(tab, x, w):
    return call(
        values_body,
        (1,),
        [whole((L, D)), whole(W_SHAPE), whole(W_SHAPE)],
        [out_whole((L, D)), out_whole((Z, L, GW)), out_whole((8, D))],
        [sds((L, D), BF16), sds((Z, L, GW), BF16), sds((8, D), F32)],
        flops=2 * L * D * Z * GW,
        nbytes=6 << 20,
    )(tab, x, *w)


def run_mixer(tab, x, gain, dq, dk, vals, a, b, w):
    return call(
        mixer_body,
        (L // TM,),
        [
            whole((L, D)), whole((8, D)), rows(1), whole((1, L)), whole((Z, L, GW)),
            whole(A_SHAPE), whole(A_SHAPE), whole(B_SHAPE), whole(B_SHAPE),
            whole(W_SHAPE), whole(W_SHAPE),
        ],
        [out_whole((Z, L, GW)), out_whole((L, D)), out_whole((L, D))],
        [sds((Z, L, GW), BF16), sds((L, D), F32), sds((L, D), BF16)],
        flops=2 * L * D * Z * GW + 2 * H * L * WIN * KB * GW,
        nbytes=14 << 20,
    )(tab, x, gain, dq, dk, vals, *a, *b, *w)


def run_ffn(tab, ns, cots, u_w, d_w):
    n = len(ns)
    out = pl.BlockSpec((2, ZS, DB, FB), lambda i, t: (0, i, 0, 0))
    types = [F32, BF16][:n] * 2
    return call(
        functools.partial(ffn_body, n - 1),
        (Z // ZS,),
        [whole((L, D))] * (2 * n) + [out] * 4,
        [out] * 4 + [out_whole((L, D))] * (2 * n),
        [sds((2, Z, DB, FB), BF16)] * 4 + [sds((L, D), k) for k in types],
        scratch=(
            pltpu.VMEM((n * L, D), BF16), pltpu.VMEM((n * L, D), BF16), pltpu.VMEM((n * L, D), F32),
            pltpu.VMEM((n * L, D), F32), pltpu.VMEM((D, ZS * FB), BF16), pltpu.VMEM((D, ZS * FB), BF16),
        ),
        flops=6 * L * D * FF,
        nbytes=20 << 20,
        vmem=54 << 20,
    )(tab, *ns, *cots, *u_w, *d_w)


def run_mixer_back(tab, dn, mid, cot, gain, dq, dk, mixed, vals, a, b, w):
    blk_a = pl.BlockSpec((G, 1, HR + DB, KB), lambda i, t: (0, tab_z(t, i), 0, 0))
    blk_b = pl.BlockSpec((G, 1, HR, KB), lambda i, t: (0, tab_z(t, i), 0, 0))
    return call(
        mixer_back_body,
        (L // TM,),
        [
            whole((L, D)), whole((L, D)), whole((L, D)), whole((L, D)), whole((8, D)), rows(1),
            whole((1, L)), whole((Z, L, GW)), whole((Z, L, GW)),
            whole(A_SHAPE), whole(A_SHAPE), whole(B_SHAPE), whole(B_SHAPE),
            whole(W_SHAPE), whole(W_SHAPE),
        ],
        [out_whole((L, D)), blk_a, blk_a, blk_b, blk_b, out_whole((Z, L, GW))],
        [
            sds((L, D), F32), sds(AO_SHAPE, BF16), sds(AO_SHAPE, BF16), sds(A_SHAPE, BF16),
            sds(A_SHAPE, BF16), sds((Z, L, GW), BF16),
        ],
        scratch=(
            pltpu.VMEM((8, D), F32), pltpu.VMEM((L, D), BF16), pltpu.VMEM((Z, L, GW), BF16),
            pltpu.VMEM((Z, L, GW), F32), pltpu.VMEM((Z, D, GW), BF16),
        ),
        flops=4 * L * D * Z * GW + 6 * H * L * WIN * KB * GW,
        nbytes=28 << 20,
    )(tab, *dn, mid, cot, gain, dq, dk, mixed, vals, *a, *b, *w)


def run_last(tab, x, gain, low, vg, w, mid_grad):
    return call(
        last_body,
        (1,),
        [
            whole((L, D)), whole((8, D)), whole((L, D)), whole((Z, L, GW)), whole(W_SHAPE),
            whole(W_SHAPE), whole((L, D)),
        ],
        [out_whole((L, D)), out_whole(V_SHAPE), out_whole(V_SHAPE)],
        [sds((L, D), F32), sds(V_SHAPE, BF16), sds(V_SHAPE, BF16)],
        scratch=(pltpu.VMEM((8, D), F32), pltpu.VMEM((L, D), F32), pltpu.VMEM((Z, D, GW), BF16)),
        flops=4 * L * D * Z * GW,
        nbytes=12 << 20,
    )(tab, x, gain, low, vg, *w, mid_grad)


def add_up(terms):
    total = terms[0].astype(F32)
    for term in terms[1:]:
        total = total + term.astype(F32)
    return total


def after(val, *deps):
    return lax.optimization_barrier((val, deps))[0]


class Grid:
    def __init__(self, gx, gy):
        self.gy = gy
        self.size = {"y": gx // 2, "x": 2, "z": gy // 2, "c": 2}
        i, j = lax.axis_index("gx"), lax.axis_index("gy")
        self.at = {"y": i // 2, "x": i % 2, "z": j // 2, "c": j % 2}

    def fetch(self, val, axis, k):
        sizes = self.size
        pairs = []
        for y in range(sizes["y"]):
            for x in range(sizes["x"]):
                for z in range(sizes["z"]):
                    for c in range(sizes["c"]):
                        src = {"y": y, "x": x, "z": z, "c": c}
                        dst = dict(src)
                        dst[axis] = src[axis] ^ k
                        pairs.append(tuple((p["y"] * 2 + p["x"]) * self.gy + p["z"] * 2 + p["c"] for p in (src, dst)))
        return lax.ppermute(val, ("gx", "gy"), pairs)

    def rel(self, axis, v):
        return self.at[axis] ^ v

    def spread(self, val, axis):
        return jnp.stack([val] + [self.fetch(val, axis, k) for k in range(1, self.size[axis])])

    def reduce(self, terms, stage, axis, *deps):
        if deps:
            terms = terms[:-1] + [(after(terms[-1][0], *deps), terms[-1][1])]
        got = []
        for k in range(1, self.size[axis]):
            part = add_up([v[(0,) * (stage - born) + (k,)] for v, born in terms]).astype(BF16)
            got.append((self.fetch(part, axis, k), stage + 1))
        return terms + got

    def total(self, terms, stage):
        return add_up([v[(0,) * (stage - born)] for v, born in terms])

    def reduce_pair(self, p, q, stage, axis, *deps):
        if deps:
            p = p[:-1] + [(after(p[-1][0], *deps), p[-1][1])]
        parts = [
            add_up([v[(0,) * (stage - born) + (1,)] for v, born in terms]).astype(BF16) for terms in (p, q)
        ]
        rows_p = parts[0].shape[-2]
        got = self.fetch(jnp.concatenate(parts, axis=-2), axis, 1)
        return p + [(got[..., :rows_p, :], stage + 1)], q + [(got[..., rows_p:, :], stage + 1)]

    def reduce_joined(self, groups, axis, *deps):
        groups = list(groups)
        if deps:
            groups[-1] = groups[-1][:-1] + [(after(groups[-1][-1][0], *deps), groups[-1][-1][1])]
        got = []
        for k in range(1, self.size[axis]):
            parts = [
                add_up([v[(0,) * (2 - born) + (k,)] for v, born in terms]).astype(BF16)
                for terms in groups
            ]
            got.append(self.fetch(jnp.concatenate(parts, axis=0), axis, k))
        out, at_row = [], 0
        for terms in groups:
            n = terms[0][0].shape[-2]
            own = [v[(0,) * (3 - born)] for v, born in terms]
            out.append(add_up(own + [v[at_row : at_row + n] for v in got]))
            at_row += n
        return out


def compute(tab, x, docs, cot, a, b, w, u, d):
    dq, dk = docs.reshape(L, 1), docs
    low, vals, gain = run_values(tab, x, w)
    mixed, mid, n_two = run_mixer(tab, x, gain, dq, dk, vals, a, b, w)
    sides = [
        run_ffn(tab, [n_two], [cot], (u[p, :2], u[p, 2:]), (d[p, :2], d[p, 2:])) for p in range(2)
    ]
    gu, gd = ([jnp.concatenate(v[i : i + 2], axis=0) for v in sides] for i in (0, 2))
    layer_out = (mid + sides[0][4] + sides[1][4]).astype(BF16)
    mid_grad, *ga, vg = run_mixer_back(
        tab, (sides[0][5], sides[1][5]), mid, cot, gain, dq, dk, mixed, vals, a, b, w
    )
    grad_in, *gv = run_last(tab, x, gain, low, vg, w, mid_grad)
    return layer_out, grad_in, gu, gd, ga[:2], ga[2:], gv


def lane_pad(mat, gains):
    row = jnp.pad(gains.reshape(1, GN), ((0, DB - 1), (0, LN - CB - GN)))
    return jnp.concatenate([mat, row], axis=1)


def small_shards(layer_in, doc_ids, mix_gain, value_w, mixing, output_w, ffn_gain, up_w, down_w, cot):
    grid = Grid(G, 2 * Z)
    at = grid.at
    order_a = [grid.rel("x", g % 2) * 2 + grid.rel("y", g // 2) for g in range(G)]
    order_b = [grid.rel("y", g // 2) * 2 + grid.rel("x", g % 2) for g in range(G)]
    order_z = [grid.rel("z", z) for z in range(Z)]
    own = [at["y"] * 2 + at["x"]]
    tab = jnp.stack([at["c"]] + order_a + order_b + order_z + own).astype(jnp.int32)
    docs = lax.dynamic_slice_in_dim(doc_ids, lax.axis_index("gy"), 1, 0)

    dq, dk = docs.reshape(L, 1), docs
    mix = mixing.reshape(2, HR, KB)
    fetch, spread = grid.fetch, grid.spread
    wts = jnp.concatenate([lane_pad(value_w, mix_gain), lane_pad(output_w.T, ffn_gain)], axis=0)

    def both(val, *deps):
        return val, fetch(after(val, *deps) if deps else val, "c", 1)

    def along_z(val):
        return [val] + [fetch(val, "z", k) for k in range(1, Z)]

    c1 = along_z(jnp.concatenate([mix[0], wts], axis=0))
    cots = [cot, fetch(cot, "c", 1)]
    b = spread(spread(mix[1], "x"), "y").reshape(G, HR, KB)
    start = window(at["z"])
    order = jnp.stack(order_b)
    b = jnp.stack([lax.dynamic_index_in_dim(b, order[start + i], 0, False) for i in range(WIN)])
    a, w = (jnp.stack([v[i * HR : (i + 1) * HR] for v in c1]) for i in range(2))
    ffn = along_z(after(jnp.stack([up_w, down_w.T]), c1[1:]))
    a, w = after((a, w), b)
    a, w = spread(a, "x"), spread(w, "y")
    a, w = after((a, w), ffn[1])
    a, w = spread(a, "y").reshape(A_SHAPE), spread(w, "x").reshape(W_SHAPE)
    b = along_z(after(b, ffn[1:]))
    u, d = (jnp.stack([v[i] for v in ffn]) for i in range(2))
    u, d = spread(u, "x"), spread(d, "y")
    w, a = both(w, b[1:], u, d), both(a, b[1:], u, d)
    u, d = after((u, d), a[0], w[0])
    u, d = [u, fetch(u, "y", 1)], [d, fetch(d, "x", 1)]
    b = both(jnp.stack(b))
    low, vals, gain = run_values(tab, after(layer_in, a[1], b[1]), w)
    mixed, mid, n_two = run_mixer(tab, layer_in, gain, dq, dk, vals, a, b, w)

    def begin(keep, send):
        got = fetch(send, "c", 1)
        return [(v.reshape((2, 2) + v.shape[1:]), 0) for v in (keep, got)]

    def last(*groups):
        return [terms[-1][0] for terms in groups]

    ku, su, kd, sd, out_a, out_b, ng_a, ng_b = run_ffn(
        tab, [n_two, fetch(n_two, "c", 1)], cots, u, d
    )
    ng_b = fetch(ng_b, "c", 1)
    gu = [(ku, 1), (fetch(su, "y", 1), 1)]
    gd = [(kd, 1), (fetch(sd, "x", 1), 1)]
    out_b = fetch(out_b, "c", 1)
    layer_out = (mid + out_a + out_b.astype(F32)).astype(BF16)
    mid_grad, ka, sa, kb, sb, vg = run_mixer_back(
        tab, (ng_a, ng_b), mid, cot, gain, dq, dk, mixed, vals, a, b, w
    )
    vg = after(vg, last(gu, gd))
    gu, gd = grid.reduce(gu, 1, "x", sa), grid.reduce(gd, 1, "y", sa)
    grad_in, kv, sv = run_last(tab, layer_in, gain, low, vg, w, mid_grad)
    ga, gb = begin(ka, sa), begin(kb, sb)
    gv = begin(kv, after(sv, last(gu, gd, ga, gb)))
    ga = grid.reduce(ga, 0, "y")
    bv = grid.reduce_pair(gb, gv, 0, "x")
    gu, gd = grid.reduce_joined((gu, gd), "z")
    ga = grid.reduce(ga, 1, "x")
    bv = grid.reduce_pair(*bv, 1, "y")
    ga, gb, gv = grid.reduce_joined((ga, *bv), "z")

    go = ga[HR:]
    grad_mixing = jnp.concatenate([ga[:HR], gb], axis=0).reshape(H, QB, KB)
    return (
        layer_out, grad_in, gv[0, CB : CB + GN], gv[:, :CB], grad_mixing, go[:, :CB].T,
        go[0, CB : CB + GN], gu, gd.T,
    )


def cols_in(v, o, gains):
    def blocks(mat, gain):
        mat = mat.reshape(G, DB, Z, 2, CB).transpose(3, 0, 2, 1, 4)
        gain = gain.reshape(G, Z, 2, 1, GN).transpose(2, 0, 1, 3, 4)
        gain = jnp.pad(gain, ((0, 0),) * 3 + ((0, DB - 1), (0, LN - CB - GN)))
        return jnp.concatenate([mat, gain], axis=-1)

    return jnp.concatenate([blocks(v, gains[0]), blocks(o, gains[1])], axis=3)


def cols_out(keep, send):
    mat = jnp.stack([keep, send])
    dg = mat[:, :, :, 0, CB : CB + GN].transpose(1, 2, 0, 3).reshape(D)
    return mat[..., :CB].transpose(1, 3, 2, 0, 4).reshape(D, D), dg


def any_shards(layer_in, doc_ids, mix_gain, value_w, mixing, output_w, ffn_gain, up_w, down_w, cot):
    ax = ("gx", "gy")
    seqs = layer_in.shape[0] // L
    me = lax.axis_index("gy") * seqs

    def gather(arr, d0, d1):
        arr = lax.all_gather(arr, "gx", axis=d0, tiled=True)
        return lax.all_gather(arr, "gy", axis=d1, tiled=True)

    def scatter(arr, d0, d1):
        arr = lax.psum_scatter(arr, "gx", scatter_dimension=d0, tiled=True)
        return lax.psum_scatter(arr, "gy", scatter_dimension=d1, tiled=True).astype(F32)

    gains = lax.all_gather(jnp.stack([mix_gain, ffn_gain]), ax, axis=1, tiled=True)
    w = cols_in(gather(value_w, 0, 1), gather(output_w.T, 0, 1), gains)
    mix_full = gather(mixing, 2, 1).reshape(2, HA, Z, 2, QB, G, KB).transpose(0, 3, 5, 2, 1, 4, 6)
    mix_full = mix_full.reshape(2, 2, G, Z, HR, KB)
    a = mix_full[0]
    starts = [min(max(m - 1, 0), G - WIN) for m in range(Z)]
    b = jnp.stack([mix_full[1][:, s : s + WIN, m] for m, s in enumerate(starts)], axis=1)
    u = gather(up_w, 0, 1).reshape(G, DB, Z, 2, FB).transpose(3, 0, 2, 1, 4)
    d = gather(down_w.T, 0, 1).reshape(G, DB, Z, 2, FB).transpose(3, 0, 2, 1, 4)
    w = w.reshape((2, 2, 2) + w.shape[2:]).swapaxes(1, 2).reshape(w.shape)
    d = d.reshape((2, 2, 2) + d.shape[2:]).swapaxes(1, 2).reshape(d.shape)
    tab = jnp.array([0, 0, 2, 1, 3] + [0, 1, 2, 3] * 2 + [0], jnp.int32)

    rows_out, grads = [], None
    for s in range(seqs):
        docs = lax.dynamic_slice_in_dim(doc_ids, me + s, 1, 0)
        part = slice(s * L, (s + 1) * L)
        out, g_in, *rest = compute(tab, layer_in[part], docs, cot[part], a, b, w, u, d)
        rows_out.append((out, g_in))
        rest = jax.tree.map(lambda v: v.astype(F32), rest) if seqs > 1 else rest
        grads = rest if grads is None else jax.tree.map(jnp.add, grads, rest)
    layer_out = jnp.concatenate([r[0] for r in rows_out], axis=0)
    grad_in = jnp.concatenate([r[1] for r in rows_out], axis=0)
    gu, gd, ga, gb, gv = jax.tree.map(lambda v: v.astype(BF16), grads)

    def by_a(v):
        return v.reshape((2, 2) + v.shape[1:]).swapaxes(0, 1).reshape(v.shape)

    def ffn_out(pair):
        return jnp.stack(pair).transpose(1, 3, 2, 0, 4).reshape(D, FF)

    value_full, dg_one = cols_out(*[by_a(v) for v in gv])
    output_full, dg_two = cols_out(*[v[:, :, HR:] for v in ga])
    gm = jnp.stack([jnp.stack([v[:, :, :HR] for v in ga]), jnp.stack([by_a(v) for v in gb])])
    gm = gm.reshape(2, 2, G, Z, HA, QB, KB).transpose(0, 4, 3, 1, 5, 2, 6)
    gd = [by_a(v) for v in gd]
    dgs = jnp.stack([dg_one, dg_two]).astype(F32)
    dgs = lax.psum_scatter(dgs, ax, scatter_dimension=1, tiled=True)
    return (
        layer_out, grad_in, dgs[0], scatter(value_full, 0, 1), scatter(gm.reshape(H, L, L), 2, 1),
        scatter(output_full, 0, 1).T, dgs[1], scatter(ffn_out(gu), 0, 1), scatter(ffn_out(gd), 0, 1).T,
    )


def solution(mesh):
    tok = P(("gx", "gy"), None)
    vec = P(("gx", "gy"))
    wgt = P("gx", "gy")
    twg = P("gy", "gx")
    mix = P(None, "gy", "gx")
    in_specs = (tok, P("gx", None), vec, wgt, mix, twg, vec, wgt, twg, tok)
    out_specs = (tok, tok, vec, wgt, mix, twg, vec, wgt, twg)

    def run(*args):
        small = (mesh.shape["gx"], mesh.shape["gy"], args[0].shape[0]) == (G, 2 * Z, L)
        return (small_shards if small else any_shards)(*args)

    return jax.shard_map(run, mesh=mesh, in_specs=in_specs, out_specs=out_specs, check_vma=False)
```

```python
import functools

import jax
import jax.numpy as jnp
from jax import lax
from jax.experimental import pallas as pl
from jax.experimental.pallas import tpu as pltpu
from jax.sharding import PartitionSpec as P

D = 768
H = 12
HS = 64
FF = 3072
L = 512
EPS = 1e-05
G = 4
Z = 4
DB = D // G
CB = D // (2 * Z)
FB = FF // (2 * Z)
QB = L // (2 * Z)
KB = L // G
LN = 128
GW = 2 * LN
GN = CB // 4
HA = H // 2
ZS = 2
HR = HA * QB
TM = 128
WIN = 3
HZ = H // Z
GC = 0.7978845608
GA = 0.044715
VMEM_LIMIT = 40 * 1024 * 1024
COST = 1 << 38
CFG = {
    "fz": ("c1",),
    "aw1": ("bxy",),
    "aw2": ("fz1",),
    "bz": ("c1",),
    "f1": ("aw1",),
    "wc": ("f1",),
    "ac": ("bz", "f1"),
    "k1": ("ac", "bc"),
    "f2r": ("sa",),
    "k5": ("f1r", "ca", "co"),
    "cv": ("f2r", "ca", "co", "cb"),
    "fzr": ("wide",),
}

F32 = jnp.float32
BF16 = jnp.bfloat16


def dot(a, b, ca, cb):
    return lax.dot_general(a, b, (((ca,), (cb,)), ((), ())), preferred_element_type=F32)


def call(body, grid, in_specs, out_specs, out_shape, scratch=(), flops=0, nbytes=0, vmem=VMEM_LIMIT):
    return pl.pallas_call(
        body,
        grid_spec=pltpu.PrefetchScalarGridSpec(
            num_scalar_prefetch=1,
            grid=grid,
            in_specs=in_specs,
            out_specs=out_specs,
            scratch_shapes=list(scratch),
        ),
        out_shape=out_shape,
        compiler_params=pltpu.CompilerParams(
            dimension_semantics=("arbitrary",) * len(grid), vmem_limit_bytes=vmem
        ),
        cost_estimate=pl.CostEstimate(flops=COST, bytes_accessed=nbytes, transcendentals=0),
    )


def whole(shape):
    return pl.BlockSpec(memory_space=pltpu.VMEM)


def rows(width):
    return pl.BlockSpec((TM, width), lambda i, t: (i, 0))


def out_whole(shape):
    return pl.BlockSpec(memory_space=pltpu.VMEM)


def tab_a(t, g):
    return t[1 + g]


def tab_b(t, g):
    return t[1 + G + g]


def tab_z(t, z):
    return t[1 + 2 * G + z]


def g_of(t, r, order_b):
    return t[1 + 2 * G + Z] ^ (r if order_b else (r % 2) * 2 + r // 2)


def norm_stats(x):
    mean = jnp.mean(x, axis=-1, keepdims=True)
    cen = x - mean
    rstd = lax.rsqrt(jnp.mean(cen * cen, axis=-1, keepdims=True) + EPS)
    return cen, rstd


def weight_z(own, oth, t, z, base):
    parts = [
        jnp.concatenate(
            [ref[tab_a(t, g), tab_z(t, z), base : base + DB, :] for g in range(G)], axis=0
        )
        for ref in (own, oth)
    ]
    return jnp.concatenate(parts, axis=1)


def head_masks(core, nrows):
    lane = lax.broadcasted_iota(jnp.int32, (nrows, GW), 1)
    tile = lane // LN
    place = lane - tile * LN
    side = jnp.where(core == 0, tile, 1 - tile)
    col = jnp.where(place < CB, side * CB + place, -1)
    return [jnp.logical_and(col >= HS * i, col < HS * (i + 1)) for i in range(HZ)]


def halves(ref, core, lead=None, base=0):
    lo = pl.multiple_of(base + core * QB, QB)
    hi = pl.multiple_of(base + (1 - core) * QB, QB)
    if lead is None:
        return jnp.concatenate([ref[pl.ds(lo, QB), :], ref[pl.ds(hi, QB), :]], axis=0)
    return jnp.concatenate([ref[lead, pl.ds(lo, QB), :], ref[lead, pl.ds(hi, QB), :]], axis=0)


def put_halves(ref, core, val, lead=None, base=0):
    lo = pl.multiple_of(base + core * QB, QB)
    hi = pl.multiple_of(base + (1 - core) * QB, QB)
    if lead is None:
        ref[pl.ds(lo, QB), :] = val[:QB]
        ref[pl.ds(hi, QB), :] = val[QB:]
    else:
        ref[lead, pl.ds(lo, QB), :] = val[:QB]
        ref[lead, pl.ds(hi, QB), :] = val[QB:]


def window(m):
    return jnp.clip(m - 1, 0, G - WIN)


def exp_scores(a_own, a_oth, b_own, b_oth, t, m, head, mask):
    parts = []
    for i in range(WIN):
        both = []
        for a, b in ((a_own, b_own), (a_oth, b_oth)):
            if head < HA:
                both.append(a[tab_b(t, window(m) + i), tab_z(t, m), head * QB : (head + 1) * QB, :])
            else:
                h = head - HA
                both.append(b[tab_z(t, m), i, h * QB : (h + 1) * QB, :])
        parts.append(jnp.concatenate(both, axis=0))
    scores = jnp.concatenate(parts, axis=1).astype(F32)
    return jnp.where(mask, jnp.exp(scores), 0.0)


def gain_spots():
    for g in range(G):
        for z in range(Z):
            for c in range(2):
                yield g, z, c, DB * g + (2 * GN) * z + GN * c


def pick(core, c, own, oth):
    return jnp.where(core == c, own, oth)


def gains_row(own, oth, t, base):
    lane = lax.broadcasted_iota(jnp.int32, (1, LN), 1)
    tiles = [jnp.zeros((1, LN), F32) for _ in range(D // LN)]
    for g, z, c, at in gain_spots():
        a, b = (r[tab_a(t, g), tab_z(t, z), base : base + 16, :].astype(F32)[:1] for r in (own, oth))
        row = pick(t[0], c, a, b)
        tile, off = at // LN, at % LN
        row = pltpu.roll(row, (off - CB) % LN, 1)
        tiles[tile] = jnp.where(jnp.logical_and(lane >= off, lane < off + GN), row, tiles[tile])
        if off + GN > LN:
            tiles[tile + 1] = jnp.where(lane < off + GN - LN, row, tiles[tile + 1])
    return jnp.concatenate(tiles, axis=1)


def with_gains(full, dg, t):
    lane = lax.broadcasted_iota(jnp.int32, (1, LN), 1)
    top = lax.broadcasted_iota(jnp.int32, (16, LN), 0) == 0
    spot = jnp.logical_and(top, jnp.logical_and(lane >= CB, lane < CB + GN))
    rows_of = {}
    for g, z, c, at in gain_spots():
        tile, off = at // LN, at % LN
        row = dg[:, tile * LN : (tile + 1) * LN]
        if off + GN > LN:
            row = jnp.where(lane < off, dg[:, (tile + 1) * LN : (tile + 2) * LN], row)
        rows_of[g, z, c] = pltpu.roll(row, (CB - off) % LN, 1)
    for z in range(Z):
        for g in range(G):
            for p in range(2):
                row = pick(t[0], p, rows_of[g, z, 0], rows_of[g, z, 1])
                at = z, slice(g * DB, g * DB + 16), slice(p * LN, (p + 1) * LN)
                full[at] = jnp.where(spot, row, full[at].astype(F32)).astype(BF16)


def by_rows(body):
    def step(i, carry):
        body(pl.ds(pl.multiple_of(i * TM, TM), TM))
        return carry

    lax.fori_loop(0, L // TM, step, 0)


def values_body(t, x_ref, own_ref, oth_ref, n_ref, val_ref, gain_ref):
    gain_ref[0:1, :] = gains_row(own_ref, oth_ref, t, 0)
    gain_ref[1:2, :] = gains_row(own_ref, oth_ref, t, DB)

    def norm(at):
        cen, rstd = norm_stats(x_ref[at, :].astype(F32))
        n_ref[at, :] = (cen * rstd * gain_ref[0:1, :]).astype(BF16)

    by_rows(norm)
    for z in range(Z):
        val_ref[z] = dot(n_ref[...], weight_z(own_ref, oth_ref, t, z, 0), 1, 0).astype(BF16)


def probs_of(units, t, m, z, mask):
    parts = []
    for i in range(HZ):
        e = exp_scores(*units, t, m, HZ * z + i, mask)
        inv = 1.0 / jnp.sum(e, axis=-1, keepdims=True)
        parts.append(e * inv)
    return parts


def mixer_body(
    t, x_ref, gain_ref, dq_ref, dk_ref, val_ref, a_own, a_oth, b_own, b_oth, w_own, w_oth,
    mix_ref, mid_ref, n_ref,
):
    m = pl.program_id(0)
    core = t[0]
    base = m * TM
    k0 = pl.multiple_of(window(m) * KB, KB)
    mask = halves(dq_ref, core) == dk_ref[:, pl.ds(k0, WIN * KB)]
    heads = head_masks(core, TM)
    for z in range(Z):
        win = val_ref[z, pl.ds(k0, WIN * KB), :]
        prob = probs_of((a_own, a_oth, b_own, b_oth), t, m, z, mask)
        part = dot(jnp.concatenate([p.astype(BF16) for p in prob], axis=0), win, 1, 0)
        out = jnp.zeros((TM, GW), F32)
        for i in range(HZ):
            out = jnp.where(heads[i], part[i * TM : (i + 1) * TM], out)
        put_halves(mix_ref, core, out.astype(BF16), z, base)

    @pl.when(m == Z - 1)
    def _():
        acc = dot(mix_ref[0], weight_z(w_own, w_oth, t, 0, DB), 1, 1)
        for z in range(1, Z):
            acc = acc + dot(mix_ref[z], weight_z(w_own, w_oth, t, z, DB), 1, 1)
        mid_ref[...] = acc

        def norm(at):
            mid = x_ref[at, :].astype(F32) + mid_ref[at, :]
            mid_ref[at, :] = mid
            cen, rstd = norm_stats(mid)
            n_ref[at, :] = (cen * rstd * gain_ref[1:2, :]).astype(BF16)

        by_rows(norm)


def ffn_body(pair, t, *refs):
    refs = list(refs)
    n_refs, refs = refs[: 1 + pair], refs[1 + pair :]
    c_refs, refs = refs[: 1 + pair], refs[1 + pair :]
    u_refs, d_refs = refs[:2], refs[2:4]
    ku, su, kd, sd = refs[4:8]
    out_refs = refs[8:]
    n_all, c_all, a_acc, b_acc, gu_all, gd_all = out_refs[2 + 2 * pair :]
    out_refs = out_refs[: 2 + 2 * pair]
    j = pl.program_id(0)

    @pl.when(j == 0)
    def _():
        for i in range(1 + pair):
            n_all[i * L : (i + 1) * L] = n_refs[i][...]
            c_all[i * L : (i + 1) * L] = c_refs[i][...]
        a_acc[...] = jnp.zeros_like(a_acc)
        b_acc[...] = jnp.zeros_like(b_acc)

    n, cot = n_all[...], c_all[...]
    def weights(parts, tab):
        cols = []
        for i in range(ZS):
            blocks = []
            for g in range(G):
                at = tab(t, g)
                one, two = (r[at % 2, i] for r in parts)
                blocks.append(jnp.where(at < 2, one, two))
            cols.append(jnp.concatenate(blocks, axis=0))
        return jnp.concatenate(cols, axis=1)

    up_w, dn_w = weights(u_refs, tab_b), weights(d_refs, tab_a)
    up = dot(n, up_w, 1, 0)
    sq = up * up
    th = jnp.tanh(GC * up * (1.0 + GA * sq))
    half = 0.5 + 0.5 * th
    act = (up * half).astype(BF16)
    slope = half + (0.5 * GC) * up * (1.0 - th * th) * (1.0 + (3.0 * GA) * sq)
    a_acc[...] += dot(act, dn_w, 1, 1)
    gd_all[...] = dot(cot, act, 0, 0).astype(BF16)
    up_g = (dot(cot, dn_w, 1, 0) * slope).astype(BF16)
    gu_all[...] = dot(n, up_g, 0, 0).astype(BF16)
    b_acc[...] += dot(up_g, up_w, 1, 1)
    for src, order_b, keep, send in ((gu_all, True, ku, su), (gd_all, False, kd, sd)):
        for r in range(G):
            at = pl.ds(pl.multiple_of(g_of(t, r, order_b) * DB, DB), DB)
            for i in range(ZS):
                (keep, send)[r // 2][r % 2, i] = src[at, i * FB : (i + 1) * FB]

    @pl.when(j == Z // ZS - 1)
    def _():
        for i in range(1 + pair):
            part = slice(i * L, (i + 1) * L)
            out_refs[i][...] = a_acc[part].astype(out_refs[i].dtype)
            out_refs[1 + pair + i][...] = b_acc[part].astype(out_refs[1 + pair + i].dtype)


def norm_back(cen, rstd, gain, dn):
    xhat = cen * rstd
    e = dn * gain
    dv = (
        e
        - jnp.mean(e, axis=-1, keepdims=True)
        - xhat * jnp.mean(e * xhat, axis=-1, keepdims=True)
    ) * rstd
    return dv, jnp.sum(dn * xhat, axis=0, keepdims=True)


def mixer_back_body(
    t, dna_ref, dnb_ref, mid_ref, c_ref, gain_ref, dq_ref, dk_ref, mix_ref, val_ref,
    a_own, a_oth, b_own, b_oth, w_own, w_oth,
    mg_ref, ka_ref, sa_ref, kb_ref, sb_ref, ko_ref, so_ref, vg_ref, dg_acc, br_ref, grad_ref, vg_acc,
    go_ref,
):
    m = pl.program_id(0)
    core = t[0]
    base = m * TM
    start = window(m)
    k0 = pl.multiple_of(start * KB, KB)

    @pl.when(m == 0)
    def _():
        vg_acc[...] = jnp.zeros_like(vg_acc)
        dg_acc[...] = jnp.zeros_like(dg_acc)

        def norm(at):
            cen, rstd = norm_stats(mid_ref[at, :])
            dn = dna_ref[at, :] + dnb_ref[at, :].astype(F32)
            dv, dg = norm_back(cen, rstd, gain_ref[1:2, :], dn)
            dg_acc[0:1, :] += dg
            mid_grad = c_ref[at, :].astype(F32) + dv
            mg_ref[at, :] = mid_grad
            br_ref[at, :] = mid_grad.astype(BF16)

        by_rows(norm)
        branch = br_ref[...]
        for z in range(Z):
            grad_ref[z] = dot(branch, weight_z(w_own, w_oth, t, z, DB), 1, 0).astype(BF16)
            go_ref[z] = dot(branch, mix_ref[z], 0, 0).astype(BF16)
        with_gains(go_ref, dg_acc[0:1, :], t)

    mask = halves(dq_ref, core) == dk_ref[:, pl.ds(k0, WIN * KB)]
    heads = head_masks(core, TM)
    for g in range(G):
        for p, ref in ((0, ko_ref), (1, so_ref)):
            ref[tab_a(t, g), 0] = go_ref[m, g * DB : (g + 1) * DB, p * LN : (p + 1) * LN]
    rest = tab_b(t, jnp.where(start == 0, G - 1, 0))
    for ref in (ka_ref, sa_ref):
        ref[rest, 0] = jnp.zeros((HR, KB), BF16)
    for z in range(Z):
        grad = halves(grad_ref, core, z, base)
        mine = jnp.concatenate(
            [jnp.where(heads[i], grad, jnp.zeros_like(grad)) for i in range(HZ)], axis=0
        )
        win = val_ref[z, pl.ds(k0, WIN * KB), :]
        prob = probs_of((a_own, a_oth, b_own, b_oth), t, m, z, mask)
        dp = dot(mine, win, 1, 1)
        low = jnp.concatenate([p.astype(BF16) for p in prob], axis=0)
        vg_acc[z, pl.ds(k0, WIN * KB), :] += dot(low, mine, 0, 0)
        for i in range(HZ):
            head = HZ * z + i
            pd = prob[i] * dp[i * TM : (i + 1) * TM]
            ds = (pd - prob[i] * jnp.sum(pd, axis=-1, keepdims=True)).astype(BF16)
            for k in range(WIN):
                for p, (ra, rb) in enumerate(((ka_ref, kb_ref), (sa_ref, sb_ref))):
                    blk = ds[p * QB : (p + 1) * QB, k * KB : (k + 1) * KB]
                    if head < HA:
                        ra[tab_b(t, start + k), 0, head * QB : (head + 1) * QB, :] = blk
                    else:
                        h = head - HA
                        rb[0, k, h * QB : (h + 1) * QB, :] = blk

    @pl.when(m == Z - 1)
    def _():
        vg_ref[...] = vg_acc[...].astype(BF16)


def last_body(
    t, x_ref, gain_ref, n_ref, vg_ref, w_own, w_oth, mg_ref, gi_ref, kv_ref, sv_ref, dg_acc, dn_ref,
    gv_ref,
):
    dg_acc[...] = jnp.zeros_like(dg_acc)
    acc = dot(vg_ref[0], weight_z(w_own, w_oth, t, 0, 0), 1, 1)
    for z in range(1, Z):
        acc = acc + dot(vg_ref[z], weight_z(w_own, w_oth, t, z, 0), 1, 1)
    dn_ref[...] = acc

    def norm(at):
        cen, rstd = norm_stats(x_ref[at, :].astype(F32))
        dv, dg = norm_back(cen, rstd, gain_ref[0:1, :], dn_ref[at, :])
        dg_acc[0:1, :] += dg
        gi_ref[at, :] = mg_ref[at, :] + dv

    by_rows(norm)
    low = n_ref[...]
    for z in range(Z):
        gv_ref[z] = dot(low, vg_ref[z], 0, 0).astype(BF16)
    with_gains(gv_ref, dg_acc[0:1, :], t)
    for z in range(Z):
        for g in range(G):
            for p, ref in ((0, kv_ref), (1, sv_ref)):
                blk = gv_ref[z, g * DB : (g + 1) * DB, p * LN : (p + 1) * LN]
                ref[tab_a(t, g), tab_z(t, z)] = blk


def sds(shape, dtype):
    return jax.ShapeDtypeStruct(shape, dtype)


W_SHAPE = (G, Z, 2 * DB, LN)
V_SHAPE = (G, Z, DB, LN)
A_SHAPE = (G, Z, HR, KB)
B_SHAPE = (Z, WIN, HR, KB)
F_SHAPE = (G, Z, DB, FB)
Z_ROWS = pl.BlockSpec((Z, TM, GW), lambda i, t: (0, i, 0))


def run_values(tab, x, w):
    return call(
        values_body,
        (1,),
        [whole((L, D)), whole(W_SHAPE), whole(W_SHAPE)],
        [out_whole((L, D)), out_whole((Z, L, GW)), out_whole((8, D))],
        [sds((L, D), BF16), sds((Z, L, GW), BF16), sds((8, D), F32)],
        flops=2 * L * D * Z * GW,
        nbytes=6 << 20,
    )(tab, x, *w)


def run_mixer(tab, x, gain, dq, dk, vals, a, b, w):
    return call(
        mixer_body,
        (L // TM,),
        [
            whole((L, D)), whole((8, D)), rows(1), whole((1, L)), whole((Z, L, GW)),
            whole(A_SHAPE), whole(A_SHAPE), whole(B_SHAPE), whole(B_SHAPE),
            whole(W_SHAPE), whole(W_SHAPE),
        ],
        [out_whole((Z, L, GW)), out_whole((L, D)), out_whole((L, D))],
        [sds((Z, L, GW), BF16), sds((L, D), F32), sds((L, D), BF16)],
        flops=2 * L * D * Z * GW + 2 * H * L * WIN * KB * GW,
        nbytes=14 << 20,
    )(tab, x, gain, dq, dk, vals, *a, *b, *w)


def run_ffn(tab, ns, cots, u_w, d_w):
    n = len(ns)
    out = pl.BlockSpec((2, ZS, DB, FB), lambda i, t: (0, i, 0, 0))
    types = [F32, BF16][:n] * 2
    return call(
        functools.partial(ffn_body, n - 1),
        (Z // ZS,),
        [whole((L, D))] * (2 * n) + [out] * 4,
        [out] * 4 + [out_whole((L, D))] * (2 * n),
        [sds((2, Z, DB, FB), BF16)] * 4 + [sds((L, D), k) for k in types],
        scratch=(
            pltpu.VMEM((n * L, D), BF16), pltpu.VMEM((n * L, D), BF16), pltpu.VMEM((n * L, D), F32),
            pltpu.VMEM((n * L, D), F32), pltpu.VMEM((D, ZS * FB), BF16), pltpu.VMEM((D, ZS * FB), BF16),
        ),
        flops=6 * L * D * FF,
        nbytes=20 << 20,
        vmem=54 << 20,
    )(tab, *ns, *cots, *u_w, *d_w)


def run_mixer_back(tab, dn, mid, cot, gain, dq, dk, mixed, vals, a, b, w):
    blk_a = pl.BlockSpec((G, 1, HR, KB), lambda i, t: (0, tab_z(t, i), 0, 0))
    blk_b = pl.BlockSpec((1, WIN, HR, KB), lambda i, t: (tab_z(t, i), 0, 0, 0))
    blk_o = pl.BlockSpec((G, 1, DB, LN), lambda i, t: (0, tab_z(t, i), 0, 0))
    return call(
        mixer_back_body,
        (L // TM,),
        [
            whole((L, D)), whole((L, D)), whole((L, D)), whole((L, D)), whole((8, D)), rows(1),
            whole((1, L)), whole((Z, L, GW)), whole((Z, L, GW)),
            whole(A_SHAPE), whole(A_SHAPE), whole(B_SHAPE), whole(B_SHAPE),
            whole(W_SHAPE), whole(W_SHAPE),
        ],
        [out_whole((L, D)), blk_a, blk_a, blk_b, blk_b, blk_o, blk_o, out_whole((Z, L, GW))],
        [
            sds((L, D), F32), sds(A_SHAPE, BF16), sds(A_SHAPE, BF16), sds(B_SHAPE, BF16),
            sds(B_SHAPE, BF16), sds(V_SHAPE, BF16), sds(V_SHAPE, BF16), sds((Z, L, GW), BF16),
        ],
        scratch=(
            pltpu.VMEM((8, D), F32), pltpu.VMEM((L, D), BF16), pltpu.VMEM((Z, L, GW), BF16),
            pltpu.VMEM((Z, L, GW), F32), pltpu.VMEM((Z, D, GW), BF16),
        ),
        flops=4 * L * D * Z * GW + 6 * H * L * WIN * KB * GW,
        nbytes=28 << 20,
    )(tab, *dn, mid, cot, gain, dq, dk, mixed, vals, *a, *b, *w)


def run_last(tab, x, gain, low, vg, w, mid_grad):
    return call(
        last_body,
        (1,),
        [
            whole((L, D)), whole((8, D)), whole((L, D)), whole((Z, L, GW)), whole(W_SHAPE),
            whole(W_SHAPE), whole((L, D)),
        ],
        [out_whole((L, D)), out_whole(V_SHAPE), out_whole(V_SHAPE)],
        [sds((L, D), F32), sds(V_SHAPE, BF16), sds(V_SHAPE, BF16)],
        scratch=(pltpu.VMEM((8, D), F32), pltpu.VMEM((L, D), F32), pltpu.VMEM((Z, D, GW), BF16)),
        flops=4 * L * D * Z * GW,
        nbytes=12 << 20,
    )(tab, x, gain, low, vg, *w, mid_grad)


def add_up(terms):
    total = terms[0].astype(F32)
    for term in terms[1:]:
        total = total + term.astype(F32)
    return total


def after(val, *deps):
    return lax.optimization_barrier((val, deps))[0]


class Grid:
    def __init__(self, gx, gy):
        self.gy = gy
        self.size = {"y": gx // 2, "x": 2, "z": gy // 2, "c": 2}
        i, j = lax.axis_index("gx"), lax.axis_index("gy")
        self.at = {"y": i // 2, "x": i % 2, "z": j // 2, "c": j % 2}

    def fetch(self, val, axis, k):
        sizes = self.size
        pairs = []
        for y in range(sizes["y"]):
            for x in range(sizes["x"]):
                for z in range(sizes["z"]):
                    for c in range(sizes["c"]):
                        src = {"y": y, "x": x, "z": z, "c": c}
                        dst = dict(src)
                        dst[axis] = src[axis] ^ k
                        pairs.append(tuple((p["y"] * 2 + p["x"]) * self.gy + p["z"] * 2 + p["c"] for p in (src, dst)))
        return lax.ppermute(val, ("gx", "gy"), pairs)

    def rel(self, axis, v):
        return self.at[axis] ^ v

    def spread(self, val, axis):
        return jnp.stack([val] + [self.fetch(val, axis, k) for k in range(1, self.size[axis])])

    def reduce(self, terms, stage, axis, *deps):
        if deps:
            terms = terms[:-1] + [(after(terms[-1][0], *deps), terms[-1][1])]
        got = []
        for k in range(1, self.size[axis]):
            part = add_up([v[(0,) * (stage - born) + (k,)] for v, born in terms]).astype(BF16)
            got.append((self.fetch(part, axis, k), stage + 1))
        return terms + got

    def total(self, terms, stage):
        return add_up([v[(0,) * (stage - born)] for v, born in terms])

    def reduce_pair(self, p, q, stage, axis, *deps):
        if deps:
            p = p[:-1] + [(after(p[-1][0], *deps), p[-1][1])]
        parts = [
            add_up([v[(0,) * (stage - born) + (1,)] for v, born in terms]).astype(BF16) for terms in (p, q)
        ]
        rows_p = parts[0].shape[-2]
        got = self.fetch(jnp.concatenate(parts, axis=-2), axis, 1)
        return p + [(got[..., :rows_p, :], stage + 1)], q + [(got[..., rows_p:, :], stage + 1)]

    def reduce_joined(self, groups, axis, *deps):
        groups = list(groups)
        if deps:
            groups[-1] = groups[-1][:-1] + [(after(groups[-1][-1][0], *deps), groups[-1][-1][1])]
        got = []
        for k in range(1, self.size[axis]):
            parts = [
                add_up([v[(0,) * (2 - born) + (k,)] for v, born in terms]).astype(BF16)
                for terms in groups
            ]
            got.append(self.fetch(jnp.concatenate(parts, axis=0), axis, k))
        out, at_row = [], 0
        for terms in groups:
            n = terms[0][0].shape[-2]
            own = [v[(0,) * (3 - born)] for v, born in terms]
            out.append(add_up(own + [v[at_row : at_row + n] for v in got]))
            at_row += n
        return out


def compute(tab, x, docs, cot, a, b, w, u, d):
    dq, dk = docs.reshape(L, 1), docs
    low, vals, gain = run_values(tab, x, w)
    mixed, mid, n_two = run_mixer(tab, x, gain, dq, dk, vals, a, b, w)
    sides = [
        run_ffn(tab, [n_two], [cot], (u[p, :2], u[p, 2:]), (d[p, :2], d[p, 2:])) for p in range(2)
    ]
    gu, gd = ([jnp.concatenate(v[i : i + 2], axis=0) for v in sides] for i in (0, 2))
    layer_out = (mid + sides[0][4] + sides[1][4]).astype(BF16)
    mid_grad, *ga, vg = run_mixer_back(
        tab, (sides[0][5], sides[1][5]), mid, cot, gain, dq, dk, mixed, vals, a, b, w
    )
    grad_in, *gv = run_last(tab, x, gain, low, vg, w, mid_grad)
    return layer_out, grad_in, gu, gd, ga[:2], ga[2:4], ga[4:], gv


def lane_pad(mat, gains):
    row = jnp.pad(gains.reshape(1, GN), ((0, DB - 1), (0, LN - CB - GN)))
    return jnp.concatenate([mat, row], axis=1)


def small_shards(layer_in, doc_ids, mix_gain, value_w, mixing, output_w, ffn_gain, up_w, down_w, cot):
    grid = Grid(G, 2 * Z)
    at = grid.at
    order_a = [grid.rel("x", g % 2) * 2 + grid.rel("y", g // 2) for g in range(G)]
    order_b = [grid.rel("y", g // 2) * 2 + grid.rel("x", g % 2) for g in range(G)]
    order_z = [grid.rel("z", z) for z in range(Z)]
    own = [at["y"] * 2 + at["x"]]
    tab = jnp.stack([at["c"]] + order_a + order_b + order_z + own).astype(jnp.int32)
    docs = lax.dynamic_slice_in_dim(doc_ids, lax.axis_index("gy"), 1, 0)

    dq, dk = docs.reshape(L, 1), docs
    mix = mixing.reshape(2, HR, KB)
    fetch, spread = grid.fetch, grid.spread
    wts = jnp.concatenate([lane_pad(value_w, mix_gain), lane_pad(output_w.T, ffn_gain)], axis=0)

    def both(val, *deps):
        return val, fetch(after(val, *deps) if deps else val, "c", 1)

    def along_z(val):
        return [val] + [fetch(val, "z", k) for k in range(1, Z)]

    events = {}

    def mark(name, *vals):
        events[name] = vals

    def hook(name, val):
        deps = [events[d] for d in CFG.get(name, ())]
        return after(val, *deps) if deps else val

    c1 = along_z(jnp.concatenate([mix[0], wts], axis=0))
    mark("c1", c1[1:])
    cots = [cot, fetch(cot, "c", 1)]
    b = spread(spread(mix[1], "x"), "y").reshape(G, HR, KB)
    mark("bxy", b)
    start = window(at["z"])
    order = jnp.stack(order_b)
    b = jnp.stack([lax.dynamic_index_in_dim(b, order[start + i], 0, False) for i in range(WIN)])
    a, w = (jnp.stack([v[i * HR : (i + 1) * HR] for v in c1]) for i in range(2))
    ffn = along_z(hook("fz", jnp.stack([up_w, down_w.T])))
    for i in range(1, Z):
        mark("fz%d" % i, ffn[i])
    mark("fz", ffn[1:])
    a, w = hook("aw1", (a, w))
    ra, rw = fetch(a, "x", 1), fetch(w, "y", 1)
    mark("aw1", ra, rw)
    a, w = hook("aw2", (jnp.stack([a, ra]), jnp.stack([w, rw])))
    ra, rw = fetch(a, "y", 1), fetch(w, "x", 1)
    mark("aw2", ra, rw)
    mark("w2", rw)
    a, w = jnp.stack([a, ra]).reshape(A_SHAPE), jnp.stack([w, rw]).reshape(W_SHAPE)
    b = along_z(hook("bz", b))
    mark("bz1", b[1])
    mark("bz", b[1:])
    u, d = hook("f1", tuple(jnp.stack([v[i] for v in ffn]) for i in range(2)))
    ru, rd = fetch(u, "x", 1), fetch(d, "y", 1)
    mark("f1", ru, rd)
    w = both(hook("wc", w))
    mark("wc", w[1])
    a = both(hook("ac", a))
    mark("ac", a[1])
    u, d = hook("f2", (jnp.stack([u, ru]), jnp.stack([d, rd])))
    u, d = [u, fetch(u, "y", 1)], [d, fetch(d, "x", 1)]
    mark("f2", u[1], d[1])
    if CFG.get("bc") == ("k1",):
        low, vals, gain = run_values(tab, hook("k1", layer_in), w)
        mark("k1", low)
        b = both(hook("bc", jnp.stack(b)))
        mark("bc", b[1])
    else:
        b = both(hook("bc", jnp.stack(b)))
        mark("bc", b[1])
        low, vals, gain = run_values(tab, hook("k1", layer_in), w)
    mixed, mid, n_two = run_mixer(tab, layer_in, hook("k2", gain), dq, dk, vals, a, b, w)

    def begin(keep, send):
        got = fetch(send, "c", 1)
        return [(v.reshape((2, 2) + v.shape[1:]), 0) for v in (keep, got)]

    def last(*groups):
        return [terms[-1][0] for terms in groups]

    ku, su, kd, sd, out_a, out_b, ng_a, ng_b = run_ffn(
        tab, [n_two, fetch(n_two, "c", 1)], cots, u, d
    )
    ng_b = fetch(ng_b, "c", 1)
    gu = [(ku, 1), (fetch(su, "y", 1), 1)]
    gd = [(kd, 1), (fetch(sd, "x", 1), 1)]
    out_b = fetch(out_b, "c", 1)
    layer_out = (mid + out_a + out_b.astype(F32)).astype(BF16)
    mid_grad, ka, sa, kb, sb, ko, so, vg = run_mixer_back(
        tab, (ng_a, ng_b), mid, cot, gain, dq, dk, mixed, vals, a, b, w
    )
    mark("f1r", last(gu, gd))
    mark("sa", sa)
    gu, gd = gu[:-1] + [(hook("f2r", gu[-1][0]), 1)], gd[:-1] + [(hook("f2r", gd[-1][0]), 1)]
    gu, gd = grid.reduce(gu, 1, "x"), grid.reduce(gd, 1, "y")
    mark("f2r", last(gu, gd))

    def cores():
        rb = fetch(hook("cab", sb), "c", 1)
        mark("cb", rb)
        ga, go = begin(ka, hook("cab", sa)), begin(ko, hook("cab", so))
        mark("ca", last(ga))
        mark("co", last(go))
        return ga, go, [(kb, 2), (rb, 2)]

    if CFG.get("cab") != ("sv",):
        ga, go, gb = cores()
        gb[-1] = (hook("bzr", gb[-1][0]), 2)
        gb = grid.reduce(gb, 2, "z")
        mark("bzr1", last(gb[:-2]))
        mark("bzr", last(gb))
    grad_in, kv, sv = run_last(tab, layer_in, gain, low, hook("k5", vg), w, mid_grad)
    mark("sv", sv)
    if CFG.get("cab") == ("sv",):
        ga, go, gb = cores()
        gb = grid.reduce(gb, 2, "z")
        mark("bzr", last(gb))
    gv = begin(kv, hook("cv", sv))
    mark("cv", last(gv))
    ga[-1] = (hook("m1a", ga[-1][0]), 0)
    ga = grid.reduce(ga, 0, "y")
    mark("m1a", last(ga))
    go[-1] = (hook("m1b", go[-1][0]), 0)
    go, gv = grid.reduce_pair(go, gv, 0, "x")
    mark("m1b", last(go))
    gb[-1] = (hook("by", gb[-1][0]), 3)
    wide = grid.total(gb, 3)
    mark("wide", wide)
    blocks = []
    for k in range(G):
        spot = (at["y"] ^ (k // 2)) * 2 + (at["x"] ^ (k % 2)) - start
        blk = lax.dynamic_index_in_dim(wide, jnp.clip(spot, 0, WIN - 1), 0, False)
        ok = jnp.logical_and(spot >= 0, spot < WIN)
        blocks.append(jnp.where(ok, blk, jnp.zeros_like(blk)))
    gb = [(jnp.stack(blocks).reshape(2, 2, HR, KB), 0)]
    gu[-1] = (hook("fzr", gu[-1][0]), 2)
    gu, gd = grid.reduce_joined((gu, gd), "z")
    mark("fzr", gu)
    ga = grid.reduce(ga, 1, "x")
    mark("m2a", last(ga))
    go, gv = grid.reduce_pair(go, gv, 1, "y")
    mark("m2", last(ga, go))
    gb = grid.reduce(gb, 0, "y")
    gb = grid.total(grid.reduce(gb, 1, "x"), 2)
    ga, go, gv = grid.reduce_joined((ga, go, gv), "z")

    grad_mixing = jnp.concatenate([ga, gb], axis=0).reshape(H, QB, KB)
    return (
        layer_out, grad_in, gv[0, CB : CB + GN], gv[:, :CB], grad_mixing, go[:, :CB].T,
        go[0, CB : CB + GN], gu, gd.T,
    )


def cols_in(v, o, gains):
    def blocks(mat, gain):
        mat = mat.reshape(G, DB, Z, 2, CB).transpose(3, 0, 2, 1, 4)
        gain = gain.reshape(G, Z, 2, 1, GN).transpose(2, 0, 1, 3, 4)
        gain = jnp.pad(gain, ((0, 0),) * 3 + ((0, DB - 1), (0, LN - CB - GN)))
        return jnp.concatenate([mat, gain], axis=-1)

    return jnp.concatenate([blocks(v, gains[0]), blocks(o, gains[1])], axis=3)


def cols_out(keep, send):
    mat = jnp.stack([keep, send])
    dg = mat[:, :, :, 0, CB : CB + GN].transpose(1, 2, 0, 3).reshape(D)
    return mat[..., :CB].transpose(1, 3, 2, 0, 4).reshape(D, D), dg


def any_shards(layer_in, doc_ids, mix_gain, value_w, mixing, output_w, ffn_gain, up_w, down_w, cot):
    ax = ("gx", "gy")
    seqs = layer_in.shape[0] // L
    me = lax.axis_index("gy") * seqs

    def gather(arr, d0, d1):
        arr = lax.all_gather(arr, "gx", axis=d0, tiled=True)
        return lax.all_gather(arr, "gy", axis=d1, tiled=True)

    def scatter(arr, d0, d1):
        arr = lax.psum_scatter(arr, "gx", scatter_dimension=d0, tiled=True)
        return lax.psum_scatter(arr, "gy", scatter_dimension=d1, tiled=True).astype(F32)

    gains = lax.all_gather(jnp.stack([mix_gain, ffn_gain]), ax, axis=1, tiled=True)
    w = cols_in(gather(value_w, 0, 1), gather(output_w.T, 0, 1), gains)
    mix_full = gather(mixing, 2, 1).reshape(2, HA, Z, 2, QB, G, KB).transpose(0, 3, 5, 2, 1, 4, 6)
    mix_full = mix_full.reshape(2, 2, G, Z, HR, KB)
    a = mix_full[0]
    starts = [min(max(m - 1, 0), G - WIN) for m in range(Z)]
    b = jnp.stack([mix_full[1][:, s : s + WIN, m] for m, s in enumerate(starts)], axis=1)
    u = gather(up_w, 0, 1).reshape(G, DB, Z, 2, FB).transpose(3, 0, 2, 1, 4)
    d = gather(down_w.T, 0, 1).reshape(G, DB, Z, 2, FB).transpose(3, 0, 2, 1, 4)
    w = w.reshape((2, 2, 2) + w.shape[2:]).swapaxes(1, 2).reshape(w.shape)
    d = d.reshape((2, 2, 2) + d.shape[2:]).swapaxes(1, 2).reshape(d.shape)
    tab = jnp.array([0, 0, 2, 1, 3] + [0, 1, 2, 3] * 2 + [0], jnp.int32)

    rows_out, grads = [], None
    for s in range(seqs):
        docs = lax.dynamic_slice_in_dim(doc_ids, me + s, 1, 0)
        part = slice(s * L, (s + 1) * L)
        out, g_in, *rest = compute(tab, layer_in[part], docs, cot[part], a, b, w, u, d)
        rows_out.append((out, g_in))
        rest = jax.tree.map(lambda v: v.astype(F32), rest) if seqs > 1 else rest
        grads = rest if grads is None else jax.tree.map(jnp.add, grads, rest)
    layer_out = jnp.concatenate([r[0] for r in rows_out], axis=0)
    grad_in = jnp.concatenate([r[1] for r in rows_out], axis=0)
    gu, gd, ga, gb, go, gv = jax.tree.map(lambda v: v.astype(BF16), grads)

    def by_a(v):
        return v.reshape((2, 2) + v.shape[1:]).swapaxes(0, 1).reshape(v.shape)

    def ffn_out(pair):
        return jnp.stack(pair).transpose(1, 3, 2, 0, 4).reshape(D, FF)

    value_full, dg_one = cols_out(*[by_a(v) for v in gv])
    output_full, dg_two = cols_out(*[by_a(v) for v in go])
    gb = jnp.stack(gb)
    gb = jnp.stack(
        [
            jnp.pad(gb[:, m], ((0, 0), (s, G - WIN - s), (0, 0), (0, 0)))
            for m, s in enumerate(starts)
        ],
        axis=2,
    )
    gm = jnp.stack([jnp.stack(ga), gb]).reshape(2, 2, G, Z, HA, QB, KB).transpose(0, 4, 3, 1, 5, 2, 6)
    gd = [by_a(v) for v in gd]
    dgs = jnp.stack([dg_one, dg_two]).astype(F32)
    dgs = lax.psum_scatter(dgs, ax, scatter_dimension=1, tiled=True)
    return (
        layer_out, grad_in, dgs[0], scatter(value_full, 0, 1), scatter(gm.reshape(H, L, L), 2, 1),
        scatter(output_full, 0, 1).T, dgs[1], scatter(ffn_out(gu), 0, 1), scatter(ffn_out(gd), 0, 1).T,
    )


def solution(mesh):
    tok = P(("gx", "gy"), None)
    vec = P(("gx", "gy"))
    wgt = P("gx", "gy")
    twg = P("gy", "gx")
    mix = P(None, "gy", "gx")
    in_specs = (tok, P("gx", None), vec, wgt, mix, twg, vec, wgt, twg, tok)
    out_specs = (tok, tok, vec, wgt, mix, twg, vec, wgt, twg)

    def run(*args):
        small = (mesh.shape["gx"], mesh.shape["gy"], args[0].shape[0]) == (G, 2 * Z, L)
        return (small_shards if small else any_shards)(*args)

    return jax.shard_map(run, mesh=mesh, in_specs=in_specs, out_specs=out_specs, check_vma=False)
```

```python
import functools

import jax
import jax.numpy as jnp
from jax import lax
from jax.experimental import pallas as pl
from jax.experimental.pallas import tpu as pltpu
from jax.sharding import PartitionSpec as P

D = 768
H = 12
HS = 64
FF = 3072
L = 512
EPS = 1e-05
G = 4
Z = 4
DB = D // G
CB = D // (2 * Z)
FB = FF // (2 * Z)
QB = L // (2 * Z)
KB = L // G
LN = 128
GW = 2 * LN
GN = CB // 4
HA = H // 2
ZS = 2
HR = HA * QB
TM = 128
WIN = 3
HZ = H // Z
GC = 0.7978845608
GA = 0.044715
VMEM_LIMIT = 40 * 1024 * 1024
COST = 1 << 38
CFG = {
    "fz": ("c1",),
    "aw1": ("bxy",),
    "aw2": ("fz1",),
    "bz": ("c1",),
    "f1": ("aw1",),
    "wc": ("f1",),
    "ac": ("bz", "f1"),
    "k1": ("ac", "bc"),
    "cp": ("f1r",),
    "m1": ("f2r",),
    "m2": ("fzr",),
}

F32 = jnp.float32
BF16 = jnp.bfloat16


def dot(a, b, ca, cb):
    return lax.dot_general(a, b, (((ca,), (cb,)), ((), ())), preferred_element_type=F32)


def call(body, grid, in_specs, out_specs, out_shape, scratch=(), flops=0, nbytes=0, vmem=VMEM_LIMIT):
    return pl.pallas_call(
        body,
        grid_spec=pltpu.PrefetchScalarGridSpec(
            num_scalar_prefetch=1,
            grid=grid,
            in_specs=in_specs,
            out_specs=out_specs,
            scratch_shapes=list(scratch),
        ),
        out_shape=out_shape,
        compiler_params=pltpu.CompilerParams(
            dimension_semantics=("arbitrary",) * len(grid), vmem_limit_bytes=vmem
        ),
        cost_estimate=pl.CostEstimate(flops=COST, bytes_accessed=nbytes, transcendentals=0),
    )


def whole(shape):
    return pl.BlockSpec(memory_space=pltpu.VMEM)


def rows(width):
    return pl.BlockSpec((TM, width), lambda i, t: (i, 0))


def out_whole(shape):
    return pl.BlockSpec(memory_space=pltpu.VMEM)


def tab_a(t, g):
    return t[1 + g]


def tab_b(t, g):
    return t[1 + G + g]


def tab_z(t, z):
    return t[1 + 2 * G + z]


def g_of(t, r, order_b):
    return t[1 + 2 * G + Z] ^ (r if order_b else (r % 2) * 2 + r // 2)


def norm_stats(x):
    mean = jnp.mean(x, axis=-1, keepdims=True)
    cen = x - mean
    rstd = lax.rsqrt(jnp.mean(cen * cen, axis=-1, keepdims=True) + EPS)
    return cen, rstd


def weight_z(own, oth, t, z, base):
    parts = [
        jnp.concatenate(
            [ref[tab_a(t, g), tab_z(t, z), base : base + DB, :] for g in range(G)], axis=0
        )
        for ref in (own, oth)
    ]
    return jnp.concatenate(parts, axis=1)


def head_masks(core, nrows):
    lane = lax.broadcasted_iota(jnp.int32, (nrows, GW), 1)
    tile = lane // LN
    place = lane - tile * LN
    side = jnp.where(core == 0, tile, 1 - tile)
    col = jnp.where(place < CB, side * CB + place, -1)
    return [jnp.logical_and(col >= HS * i, col < HS * (i + 1)) for i in range(HZ)]


def halves(ref, core, lead=None, base=0):
    lo = pl.multiple_of(base + core * QB, QB)
    hi = pl.multiple_of(base + (1 - core) * QB, QB)
    if lead is None:
        return jnp.concatenate([ref[pl.ds(lo, QB), :], ref[pl.ds(hi, QB), :]], axis=0)
    return jnp.concatenate([ref[lead, pl.ds(lo, QB), :], ref[lead, pl.ds(hi, QB), :]], axis=0)


def put_halves(ref, core, val, lead=None, base=0):
    lo = pl.multiple_of(base + core * QB, QB)
    hi = pl.multiple_of(base + (1 - core) * QB, QB)
    if lead is None:
        ref[pl.ds(lo, QB), :] = val[:QB]
        ref[pl.ds(hi, QB), :] = val[QB:]
    else:
        ref[lead, pl.ds(lo, QB), :] = val[:QB]
        ref[lead, pl.ds(hi, QB), :] = val[QB:]


def window(m):
    return jnp.clip(m - 1, 0, G - WIN)


def exp_scores(a_own, a_oth, b_own, b_oth, t, m, head, mask):
    parts = []
    for i in range(WIN):
        both = []
        for a, b in ((a_own, b_own), (a_oth, b_oth)):
            if head < HA:
                both.append(a[tab_b(t, window(m) + i), tab_z(t, m), head * QB : (head + 1) * QB, :])
            else:
                h = head - HA
                both.append(b[tab_z(t, m), i, h * QB : (h + 1) * QB, :])
        parts.append(jnp.concatenate(both, axis=0))
    scores = jnp.concatenate(parts, axis=1).astype(F32)
    return jnp.where(mask, jnp.exp(scores), 0.0)


def gain_spots():
    for g in range(G):
        for z in range(Z):
            for c in range(2):
                yield g, z, c, DB * g + (2 * GN) * z + GN * c


def pick(core, c, own, oth):
    return jnp.where(core == c, own, oth)


def gains_row(own, oth, t, base):
    lane = lax.broadcasted_iota(jnp.int32, (1, LN), 1)
    tiles = [jnp.zeros((1, LN), F32) for _ in range(D // LN)]
    for g, z, c, at in gain_spots():
        a, b = (r[tab_a(t, g), tab_z(t, z), base : base + 16, :].astype(F32)[:1] for r in (own, oth))
        row = pick(t[0], c, a, b)
        tile, off = at // LN, at % LN
        row = pltpu.roll(row, (off - CB) % LN, 1)
        tiles[tile] = jnp.where(jnp.logical_and(lane >= off, lane < off + GN), row, tiles[tile])
        if off + GN > LN:
            tiles[tile + 1] = jnp.where(lane < off + GN - LN, row, tiles[tile + 1])
    return jnp.concatenate(tiles, axis=1)


def with_gains(full, dg, t):
    lane = lax.broadcasted_iota(jnp.int32, (1, LN), 1)
    top = lax.broadcasted_iota(jnp.int32, (16, LN), 0) == 0
    spot = jnp.logical_and(top, jnp.logical_and(lane >= CB, lane < CB + GN))
    rows_of = {}
    for g, z, c, at in gain_spots():
        tile, off = at // LN, at % LN
        row = dg[:, tile * LN : (tile + 1) * LN]
        if off + GN > LN:
            row = jnp.where(lane < off, dg[:, (tile + 1) * LN : (tile + 2) * LN], row)
        rows_of[g, z, c] = pltpu.roll(row, (CB - off) % LN, 1)
    for z in range(Z):
        for g in range(G):
            for p in range(2):
                row = pick(t[0], p, rows_of[g, z, 0], rows_of[g, z, 1])
                at = z, slice(g * DB, g * DB + 16), slice(p * LN, (p + 1) * LN)
                full[at] = jnp.where(spot, row, full[at].astype(F32)).astype(BF16)


def by_rows(body):
    def step(i, carry):
        body(pl.ds(pl.multiple_of(i * TM, TM), TM))
        return carry

    lax.fori_loop(0, L // TM, step, 0)


def values_body(t, x_ref, own_ref, oth_ref, n_ref, val_ref, gain_ref):
    gain_ref[0:1, :] = gains_row(own_ref, oth_ref, t, 0)
    gain_ref[1:2, :] = gains_row(own_ref, oth_ref, t, DB)

    def norm(at):
        cen, rstd = norm_stats(x_ref[at, :].astype(F32))
        n_ref[at, :] = (cen * rstd * gain_ref[0:1, :]).astype(BF16)

    by_rows(norm)
    for z in range(Z):
        val_ref[z] = dot(n_ref[...], weight_z(own_ref, oth_ref, t, z, 0), 1, 0).astype(BF16)


def probs_of(units, t, m, z, mask):
    parts = []
    for i in range(HZ):
        e = exp_scores(*units, t, m, HZ * z + i, mask)
        inv = 1.0 / jnp.sum(e, axis=-1, keepdims=True)
        parts.append(e * inv)
    return parts


def mixer_body(
    t, x_ref, gain_ref, dq_ref, dk_ref, val_ref, a_own, a_oth, b_own, b_oth, w_own, w_oth,
    mix_ref, mid_ref, n_ref,
):
    m = pl.program_id(0)
    core = t[0]
    base = m * TM
    k0 = pl.multiple_of(window(m) * KB, KB)
    mask = halves(dq_ref, core) == dk_ref[:, pl.ds(k0, WIN * KB)]
    heads = head_masks(core, TM)
    for z in range(Z):
        win = val_ref[z, pl.ds(k0, WIN * KB), :]
        prob = probs_of((a_own, a_oth, b_own, b_oth), t, m, z, mask)
        part = dot(jnp.concatenate([p.astype(BF16) for p in prob], axis=0), win, 1, 0)
        out = jnp.zeros((TM, GW), F32)
        for i in range(HZ):
            out = jnp.where(heads[i], part[i * TM : (i + 1) * TM], out)
        put_halves(mix_ref, core, out.astype(BF16), z, base)

    @pl.when(m == Z - 1)
    def _():
        acc = dot(mix_ref[0], weight_z(w_own, w_oth, t, 0, DB), 1, 1)
        for z in range(1, Z):
            acc = acc + dot(mix_ref[z], weight_z(w_own, w_oth, t, z, DB), 1, 1)
        mid_ref[...] = acc

        def norm(at):
            mid = x_ref[at, :].astype(F32) + mid_ref[at, :]
            mid_ref[at, :] = mid
            cen, rstd = norm_stats(mid)
            n_ref[at, :] = (cen * rstd * gain_ref[1:2, :]).astype(BF16)

        by_rows(norm)


def ffn_body(pair, t, *refs):
    refs = list(refs)
    n_refs, refs = refs[: 1 + pair], refs[1 + pair :]
    c_refs, refs = refs[: 1 + pair], refs[1 + pair :]
    u_refs, d_refs = refs[:2], refs[2:4]
    ku, su, kd, sd = refs[4:8]
    out_refs = refs[8:]
    n_all, c_all, a_acc, b_acc, gu_all, gd_all = out_refs[2 + 2 * pair :]
    out_refs = out_refs[: 2 + 2 * pair]
    j = pl.program_id(0)

    @pl.when(j == 0)
    def _():
        for i in range(1 + pair):
            n_all[i * L : (i + 1) * L] = n_refs[i][...]
            c_all[i * L : (i + 1) * L] = c_refs[i][...]
        a_acc[...] = jnp.zeros_like(a_acc)
        b_acc[...] = jnp.zeros_like(b_acc)

    n, cot = n_all[...], c_all[...]
    def weights(parts, tab):
        cols = []
        for i in range(ZS):
            blocks = []
            for g in range(G):
                at = tab(t, g)
                one, two = (r[at % 2, i] for r in parts)
                blocks.append(jnp.where(at < 2, one, two))
            cols.append(jnp.concatenate(blocks, axis=0))
        return jnp.concatenate(cols, axis=1)

    up_w, dn_w = weights(u_refs, tab_b), weights(d_refs, tab_a)
    up = dot(n, up_w, 1, 0)
    sq = up * up
    th = jnp.tanh(GC * up * (1.0 + GA * sq))
    half = 0.5 + 0.5 * th
    act = (up * half).astype(BF16)
    slope = half + (0.5 * GC) * up * (1.0 - th * th) * (1.0 + (3.0 * GA) * sq)
    a_acc[...] += dot(act, dn_w, 1, 1)
    gd_all[...] = dot(cot, act, 0, 0).astype(BF16)
    up_g = (dot(cot, dn_w, 1, 0) * slope).astype(BF16)
    gu_all[...] = dot(n, up_g, 0, 0).astype(BF16)
    b_acc[...] += dot(up_g, up_w, 1, 1)
    for src, order_b, keep, send in ((gu_all, True, ku, su), (gd_all, False, kd, sd)):
        for r in range(G):
            at = pl.ds(pl.multiple_of(g_of(t, r, order_b) * DB, DB), DB)
            for i in range(ZS):
                (keep, send)[r // 2][r % 2, i] = src[at, i * FB : (i + 1) * FB]

    @pl.when(j == Z // ZS - 1)
    def _():
        for i in range(1 + pair):
            part = slice(i * L, (i + 1) * L)
            out_refs[i][...] = a_acc[part].astype(out_refs[i].dtype)
            out_refs[1 + pair + i][...] = b_acc[part].astype(out_refs[1 + pair + i].dtype)


def norm_back(cen, rstd, gain, dn):
    xhat = cen * rstd
    e = dn * gain
    dv = (
        e
        - jnp.mean(e, axis=-1, keepdims=True)
        - xhat * jnp.mean(e * xhat, axis=-1, keepdims=True)
    ) * rstd
    return dv, jnp.sum(dn * xhat, axis=0, keepdims=True)


def back_body(
    t, dna_ref, dnb_ref, mid_ref, c_ref, x_ref, low_ref, gain_ref, dq_ref, dk_ref, mix_ref, val_ref,
    a_own, a_oth, b_own, b_oth, w_own, w_oth,
    gi_ref, kp_ref, sp_ref, kq_ref, sq_ref,
    dg_acc, br_ref, grad_ref, vg_acc, vg_ref, full_ref, mg_ref, dn_ref,
):
    m = pl.program_id(0)
    core = t[0]
    base = m * TM
    start = window(m)
    k0 = pl.multiple_of(start * KB, KB)

    def put(tab, refs):
        for z in range(Z):
            for g in range(G):
                for p, ref in enumerate(refs):
                    blk = full_ref[z, g * DB : (g + 1) * DB, p * LN : (p + 1) * LN]
                    ref[tab(t, g), tab_z(t, z), HR:, :] = blk

    @pl.when(m == 0)
    def _():
        vg_acc[...] = jnp.zeros_like(vg_acc)
        dg_acc[...] = jnp.zeros_like(dg_acc)

        def norm(at):
            cen, rstd = norm_stats(mid_ref[at, :])
            dn = dna_ref[at, :] + dnb_ref[at, :].astype(F32)
            dv, dg = norm_back(cen, rstd, gain_ref[1:2, :], dn)
            dg_acc[0:1, :] += dg
            mid_grad = c_ref[at, :].astype(F32) + dv
            mg_ref[at, :] = mid_grad
            br_ref[at, :] = mid_grad.astype(BF16)

        by_rows(norm)
        branch = br_ref[...]
        for z in range(Z):
            grad_ref[z] = dot(branch, weight_z(w_own, w_oth, t, z, DB), 1, 0).astype(BF16)
            full_ref[z] = dot(branch, mix_ref[z], 0, 0).astype(BF16)
        with_gains(full_ref, dg_acc[0:1, :], t)
        put(tab_b, (kp_ref, sp_ref))
        dg_acc[...] = jnp.zeros_like(dg_acc)

    mask = halves(dq_ref, core) == dk_ref[:, pl.ds(k0, WIN * KB)]
    heads = head_masks(core, TM)
    at_z = tab_z(t, m)
    rest = jnp.where(start == 0, G - 1, 0)
    for refs, tab in (((kp_ref, sp_ref), tab_b), ((kq_ref, sq_ref), tab_a)):
        for ref in refs:
            ref[tab(t, rest), at_z, 0:HR, :] = jnp.zeros((HR, KB), BF16)
    for z in range(Z):
        grad = halves(grad_ref, core, z, base)
        mine = jnp.concatenate(
            [jnp.where(heads[i], grad, jnp.zeros_like(grad)) for i in range(HZ)], axis=0
        )
        win = val_ref[z, pl.ds(k0, WIN * KB), :]
        prob = probs_of((a_own, a_oth, b_own, b_oth), t, m, z, mask)
        dp = dot(mine, win, 1, 1)
        low = jnp.concatenate([p.astype(BF16) for p in prob], axis=0)
        vg_acc[z, pl.ds(k0, WIN * KB), :] += dot(low, mine, 0, 0)
        for i in range(HZ):
            head = HZ * z + i
            pd = prob[i] * dp[i * TM : (i + 1) * TM]
            ds = (pd - prob[i] * jnp.sum(pd, axis=-1, keepdims=True)).astype(BF16)
            refs, tab = ((kp_ref, sp_ref), tab_b) if head < HA else ((kq_ref, sq_ref), tab_a)
            row = head % HA * QB
            for k in range(WIN):
                for p, ref in enumerate(refs):
                    ref[tab(t, start + k), at_z, row : row + QB, :] = ds[
                        p * QB : (p + 1) * QB, k * KB : (k + 1) * KB
                    ]

    @pl.when(m == Z - 1)
    def _():
        vg_ref[...] = vg_acc[...].astype(BF16)
        acc = dot(vg_ref[0], weight_z(w_own, w_oth, t, 0, 0), 1, 1)
        for z in range(1, Z):
            acc = acc + dot(vg_ref[z], weight_z(w_own, w_oth, t, z, 0), 1, 1)
        dn_ref[...] = acc

        def norm(at):
            cen, rstd = norm_stats(x_ref[at, :].astype(F32))
            dv, dg = norm_back(cen, rstd, gain_ref[0:1, :], dn_ref[at, :])
            dg_acc[0:1, :] += dg
            gi_ref[at, :] = mg_ref[at, :] + dv

        by_rows(norm)
        low = low_ref[...]
        for z in range(Z):
            full_ref[z] = dot(low, vg_ref[z], 0, 0).astype(BF16)
        with_gains(full_ref, dg_acc[0:1, :], t)
        put(tab_a, (kq_ref, sq_ref))


def sds(shape, dtype):
    return jax.ShapeDtypeStruct(shape, dtype)


W_SHAPE = (G, Z, 2 * DB, LN)
V_SHAPE = (G, Z, DB, LN)
A_SHAPE = (G, Z, HR, KB)
S_SHAPE = (G, Z, HR + DB, KB)
B_SHAPE = (Z, WIN, HR, KB)
F_SHAPE = (G, Z, DB, FB)
Z_ROWS = pl.BlockSpec((Z, TM, GW), lambda i, t: (0, i, 0))


def run_values(tab, x, w):
    return call(
        values_body,
        (1,),
        [whole((L, D)), whole(W_SHAPE), whole(W_SHAPE)],
        [out_whole((L, D)), out_whole((Z, L, GW)), out_whole((8, D))],
        [sds((L, D), BF16), sds((Z, L, GW), BF16), sds((8, D), F32)],
        flops=2 * L * D * Z * GW,
        nbytes=6 << 20,
    )(tab, x, *w)


def run_mixer(tab, x, gain, dq, dk, vals, a, b, w):
    return call(
        mixer_body,
        (L // TM,),
        [
            whole((L, D)), whole((8, D)), rows(1), whole((1, L)), whole((Z, L, GW)),
            whole(A_SHAPE), whole(A_SHAPE), whole(B_SHAPE), whole(B_SHAPE),
            whole(W_SHAPE), whole(W_SHAPE),
        ],
        [out_whole((Z, L, GW)), out_whole((L, D)), out_whole((L, D))],
        [sds((Z, L, GW), BF16), sds((L, D), F32), sds((L, D), BF16)],
        flops=2 * L * D * Z * GW + 2 * H * L * WIN * KB * GW,
        nbytes=14 << 20,
    )(tab, x, gain, dq, dk, vals, *a, *b, *w)


def run_ffn(tab, ns, cots, u_w, d_w):
    n = len(ns)
    out = pl.BlockSpec((2, ZS, DB, FB), lambda i, t: (0, i, 0, 0))
    types = [F32, BF16][:n] * 2
    return call(
        functools.partial(ffn_body, n - 1),
        (Z // ZS,),
        [whole((L, D))] * (2 * n) + [out] * 4,
        [out] * 4 + [out_whole((L, D))] * (2 * n),
        [sds((2, Z, DB, FB), BF16)] * 4 + [sds((L, D), k) for k in types],
        scratch=(
            pltpu.VMEM((n * L, D), BF16), pltpu.VMEM((n * L, D), BF16), pltpu.VMEM((n * L, D), F32),
            pltpu.VMEM((n * L, D), F32), pltpu.VMEM((D, ZS * FB), BF16), pltpu.VMEM((D, ZS * FB), BF16),
        ),
        flops=6 * L * D * FF,
        nbytes=20 << 20,
        vmem=54 << 20,
    )(tab, *ns, *cots, *u_w, *d_w)


def run_back(tab, dn, mid, cot, x, low, gain, dq, dk, mixed, vals, a, b, w):
    args = [*dn, mid, cot, x, low, gain, dq, dk, mixed, vals, *a, *b, *w]
    specs = [whole(None)] * len(args)
    specs[7] = rows(1)
    return call(
        back_body,
        (L // TM,),
        specs,
        [whole(None)] * 5,
        [sds((L, D), F32)] + [sds(S_SHAPE, BF16)] * 4,
        scratch=(
            pltpu.VMEM((8, D), F32), pltpu.VMEM((L, D), BF16), pltpu.VMEM((Z, L, GW), BF16),
            pltpu.VMEM((Z, L, GW), F32), pltpu.VMEM((Z, L, GW), BF16), pltpu.VMEM((Z, D, GW), BF16),
            pltpu.VMEM((L, D), F32), pltpu.VMEM((L, D), F32),
        ),
        flops=8 * L * D * Z * GW,
        nbytes=40 << 20,
        vmem=32 << 20,
    )(tab, *args)


def add_up(terms):
    total = terms[0].astype(F32)
    for term in terms[1:]:
        total = total + term.astype(F32)
    return total


def after(val, *deps):
    return lax.optimization_barrier((val, deps))[0]


class Grid:
    def __init__(self, gx, gy):
        self.gy = gy
        self.size = {"y": gx // 2, "x": 2, "z": gy // 2, "c": 2}
        i, j = lax.axis_index("gx"), lax.axis_index("gy")
        self.at = {"y": i // 2, "x": i % 2, "z": j // 2, "c": j % 2}

    def fetch(self, val, axis, k):
        sizes = self.size
        pairs = []
        for y in range(sizes["y"]):
            for x in range(sizes["x"]):
                for z in range(sizes["z"]):
                    for c in range(sizes["c"]):
                        src = {"y": y, "x": x, "z": z, "c": c}
                        dst = dict(src)
                        dst[axis] = src[axis] ^ k
                        pairs.append(tuple((p["y"] * 2 + p["x"]) * self.gy + p["z"] * 2 + p["c"] for p in (src, dst)))
        return lax.ppermute(val, ("gx", "gy"), pairs)

    def rel(self, axis, v):
        return self.at[axis] ^ v

    def spread(self, val, axis):
        return jnp.stack([val] + [self.fetch(val, axis, k) for k in range(1, self.size[axis])])

    def reduce(self, terms, stage, axis, *deps):
        if deps:
            terms = terms[:-1] + [(after(terms[-1][0], *deps), terms[-1][1])]
        got = []
        for k in range(1, self.size[axis]):
            part = add_up([v[(0,) * (stage - born) + (k,)] for v, born in terms]).astype(BF16)
            got.append((self.fetch(part, axis, k), stage + 1))
        return terms + got

    def total(self, terms, stage):
        return add_up([v[(0,) * (stage - born)] for v, born in terms])

    def reduce_joined(self, groups, axis, *deps):
        groups = list(groups)
        if deps:
            groups[-1] = groups[-1][:-1] + [(after(groups[-1][-1][0], *deps), groups[-1][-1][1])]
        got = []
        for k in range(1, self.size[axis]):
            parts = [
                add_up([v[(0,) * (2 - born) + (k,)] for v, born in terms]).astype(BF16)
                for terms in groups
            ]
            got.append(self.fetch(jnp.concatenate(parts, axis=0), axis, k))
        out, at_row = [], 0
        for terms in groups:
            n = terms[0][0].shape[-2]
            own = [v[(0,) * (3 - born)] for v, born in terms]
            out.append(add_up(own + [v[at_row : at_row + n] for v in got]))
            at_row += n
        return out


def compute(tab, x, docs, cot, a, b, w, u, d):
    dq, dk = docs.reshape(L, 1), docs
    low, vals, gain = run_values(tab, x, w)
    mixed, mid, n_two = run_mixer(tab, x, gain, dq, dk, vals, a, b, w)
    sides = [
        run_ffn(tab, [n_two], [cot], (u[p, :2], u[p, 2:]), (d[p, :2], d[p, 2:])) for p in range(2)
    ]
    gu, gd = ([jnp.concatenate(v[i : i + 2], axis=0) for v in sides] for i in (0, 2))
    layer_out = (mid + sides[0][4] + sides[1][4]).astype(BF16)
    grad_in, kp, sp, kq, sq = run_back(
        tab, (sides[0][5], sides[1][5]), mid, cot, x, low, gain, dq, dk, mixed, vals, a, b, w
    )
    return layer_out, grad_in, gu, gd, (kp, sp), (kq, sq)


def lane_pad(mat, gains):
    row = jnp.pad(gains.reshape(1, GN), ((0, DB - 1), (0, LN - CB - GN)))
    return jnp.concatenate([mat, row], axis=1)


def small_shards(layer_in, doc_ids, mix_gain, value_w, mixing, output_w, ffn_gain, up_w, down_w, cot):
    grid = Grid(G, 2 * Z)
    at = grid.at
    order_a = [grid.rel("x", g % 2) * 2 + grid.rel("y", g // 2) for g in range(G)]
    order_b = [grid.rel("y", g // 2) * 2 + grid.rel("x", g % 2) for g in range(G)]
    order_z = [grid.rel("z", z) for z in range(Z)]
    own = [at["y"] * 2 + at["x"]]
    tab = jnp.stack([at["c"]] + order_a + order_b + order_z + own).astype(jnp.int32)
    docs = lax.dynamic_slice_in_dim(doc_ids, lax.axis_index("gy"), 1, 0)

    dq, dk = docs.reshape(L, 1), docs
    mix = mixing.reshape(2, HR, KB)
    fetch, spread = grid.fetch, grid.spread
    wts = jnp.concatenate([lane_pad(value_w, mix_gain), lane_pad(output_w.T, ffn_gain)], axis=0)

    def both(val, *deps):
        return val, fetch(after(val, *deps) if deps else val, "c", 1)

    def along_z(val):
        return [val] + [fetch(val, "z", k) for k in range(1, Z)]

    events = {}

    def mark(name, *vals):
        events[name] = vals

    def hook(name, val):
        deps = [events[d] for d in CFG.get(name, ())]
        return after(val, *deps) if deps else val

    c1 = along_z(jnp.concatenate([mix[0], wts], axis=0))
    mark("c1", c1[1:])
    cots = [cot, fetch(cot, "c", 1)]
    b = spread(spread(mix[1], "x"), "y").reshape(G, HR, KB)
    mark("bxy", b)
    start = window(at["z"])
    order = jnp.stack(order_b)
    b = jnp.stack([lax.dynamic_index_in_dim(b, order[start + i], 0, False) for i in range(WIN)])
    a, w = (jnp.stack([v[i * HR : (i + 1) * HR] for v in c1]) for i in range(2))
    ffn = along_z(hook("fz", jnp.stack([up_w, down_w.T])))
    for i in range(1, Z):
        mark("fz%d" % i, ffn[i])
    mark("fz", ffn[1:])
    a, w = hook("aw1", (a, w))
    ra, rw = fetch(a, "x", 1), fetch(w, "y", 1)
    mark("aw1", ra, rw)
    a, w = hook("aw2", (jnp.stack([a, ra]), jnp.stack([w, rw])))
    ra, rw = fetch(a, "y", 1), fetch(w, "x", 1)
    mark("aw2", ra, rw)
    mark("w2", rw)
    a, w = jnp.stack([a, ra]).reshape(A_SHAPE), jnp.stack([w, rw]).reshape(W_SHAPE)
    b = along_z(hook("bz", b))
    mark("bz1", b[1])
    mark("bz", b[1:])
    u, d = hook("f1", tuple(jnp.stack([v[i] for v in ffn]) for i in range(2)))
    ru, rd = fetch(u, "x", 1), fetch(d, "y", 1)
    mark("f1", ru, rd)
    w = both(hook("wc", w))
    mark("wc", w[1])
    a = both(hook("ac", a))
    mark("ac", a[1])
    u, d = hook("f2", (jnp.stack([u, ru]), jnp.stack([d, rd])))
    u, d = [u, fetch(u, "y", 1)], [d, fetch(d, "x", 1)]
    mark("f2", u[1], d[1])
    if CFG.get("bc") == ("k1",):
        low, vals, gain = run_values(tab, hook("k1", layer_in), w)
        mark("k1", low)
        b = both(hook("bc", jnp.stack(b)))
        mark("bc", b[1])
    else:
        b = both(hook("bc", jnp.stack(b)))
        mark("bc", b[1])
        low, vals, gain = run_values(tab, hook("k1", layer_in), w)
    mixed, mid, n_two = run_mixer(tab, layer_in, hook("k2", gain), dq, dk, vals, a, b, w)

    def begin(keep, send):
        got = fetch(send, "c", 1)
        return [(v.reshape((2, 2) + v.shape[1:]), 0) for v in (keep, got)]

    def last(*groups):
        return [terms[-1][0] for terms in groups]

    ku, su, kd, sd, out_a, out_b, ng_a, ng_b = run_ffn(
        tab, [n_two, fetch(n_two, "c", 1)], cots, u, d
    )
    ng_b = fetch(ng_b, "c", 1)
    gu = [(ku, 1), (fetch(su, "y", 1), 1)]
    gd = [(kd, 1), (fetch(sd, "x", 1), 1)]
    out_b = fetch(out_b, "c", 1)
    layer_out = (mid + out_a + out_b.astype(F32)).astype(BF16)
    grad_in, kp, sp, kq, sq = run_back(
        tab, (ng_a, ng_b), mid, cot, layer_in, low, gain, dq, dk, mixed, vals, a, b, w
    )
    mark("f1r", last(gu, gd))
    sp, sq = hook("cp", (sp, sq))
    gp, gq = begin(kp, sp), begin(kq, sq)
    mark("cp", last(gp, gq))
    gu, gd = grid.reduce(gu, 1, "x", sp), grid.reduce(gd, 1, "y", sp)
    mark("f2r", last(gu, gd))
    gp[-1] = (hook("m1", gp[-1][0]), 0)
    gp, gq = grid.reduce(gp, 0, "y"), grid.reduce(gq, 0, "x")
    mark("m1", last(gp, gq))
    gu[-1] = (hook("fzr", gu[-1][0]), 2)
    gu, gd = grid.reduce_joined((gu, gd), "z")
    mark("fzr", gu)
    gp[-1] = (hook("m2", gp[-1][0]), 1)
    gq[-1] = (hook("m2", gq[-1][0]), 1)
    gp, gq = grid.reduce(gp, 1, "x"), grid.reduce(gq, 1, "y")
    mark("m2", last(gp, gq))
    gp, gq = grid.reduce_joined((gp, gq), "z")

    go, gv = gp[HR:], gq[HR:]
    grad_mixing = jnp.concatenate([gp[:HR], gq[:HR]], axis=0).reshape(H, QB, KB)
    return (
        layer_out, grad_in, gv[0, CB : CB + GN], gv[:, :CB], grad_mixing, go[:, :CB].T,
        go[0, CB : CB + GN], gu, gd.T,
    )


def cols_in(v, o, gains):
    def blocks(mat, gain):
        mat = mat.reshape(G, DB, Z, 2, CB).transpose(3, 0, 2, 1, 4)
        gain = gain.reshape(G, Z, 2, 1, GN).transpose(2, 0, 1, 3, 4)
        gain = jnp.pad(gain, ((0, 0),) * 3 + ((0, DB - 1), (0, LN - CB - GN)))
        return jnp.concatenate([mat, gain], axis=-1)

    return jnp.concatenate([blocks(v, gains[0]), blocks(o, gains[1])], axis=3)


def cols_out(keep, send):
    mat = jnp.stack([keep, send])
    dg = mat[:, :, :, 0, CB : CB + GN].transpose(1, 2, 0, 3).reshape(D)
    return mat[..., :CB].transpose(1, 3, 2, 0, 4).reshape(D, D), dg


def any_shards(layer_in, doc_ids, mix_gain, value_w, mixing, output_w, ffn_gain, up_w, down_w, cot):
    ax = ("gx", "gy")
    seqs = layer_in.shape[0] // L
    me = lax.axis_index("gy") * seqs

    def gather(arr, d0, d1):
        arr = lax.all_gather(arr, "gx", axis=d0, tiled=True)
        return lax.all_gather(arr, "gy", axis=d1, tiled=True)

    def scatter(arr, d0, d1):
        arr = lax.psum_scatter(arr, "gx", scatter_dimension=d0, tiled=True)
        return lax.psum_scatter(arr, "gy", scatter_dimension=d1, tiled=True).astype(F32)

    gains = lax.all_gather(jnp.stack([mix_gain, ffn_gain]), ax, axis=1, tiled=True)
    w = cols_in(gather(value_w, 0, 1), gather(output_w.T, 0, 1), gains)
    mix_full = gather(mixing, 2, 1).reshape(2, HA, Z, 2, QB, G, KB).transpose(0, 3, 5, 2, 1, 4, 6)
    mix_full = mix_full.reshape(2, 2, G, Z, HR, KB)
    a = mix_full[0]
    starts = [min(max(m - 1, 0), G - WIN) for m in range(Z)]
    b = jnp.stack([mix_full[1][:, s : s + WIN, m] for m, s in enumerate(starts)], axis=1)
    u = gather(up_w, 0, 1).reshape(G, DB, Z, 2, FB).transpose(3, 0, 2, 1, 4)
    d = gather(down_w.T, 0, 1).reshape(G, DB, Z, 2, FB).transpose(3, 0, 2, 1, 4)
    w = w.reshape((2, 2, 2) + w.shape[2:]).swapaxes(1, 2).reshape(w.shape)
    d = d.reshape((2, 2, 2) + d.shape[2:]).swapaxes(1, 2).reshape(d.shape)
    tab = jnp.array([0, 0, 2, 1, 3] + [0, 1, 2, 3] * 2 + [0], jnp.int32)

    rows_out, grads = [], None
    for s in range(seqs):
        docs = lax.dynamic_slice_in_dim(doc_ids, me + s, 1, 0)
        part = slice(s * L, (s + 1) * L)
        out, g_in, *rest = compute(tab, layer_in[part], docs, cot[part], a, b, w, u, d)
        rows_out.append((out, g_in))
        rest = jax.tree.map(lambda v: v.astype(F32), rest) if seqs > 1 else rest
        grads = rest if grads is None else jax.tree.map(jnp.add, grads, rest)
    layer_out = jnp.concatenate([r[0] for r in rows_out], axis=0)
    grad_in = jnp.concatenate([r[1] for r in rows_out], axis=0)
    gu, gd, gp, gq = jax.tree.map(lambda v: v.astype(BF16), grads)

    def by_a(v):
        return v.reshape((2, 2) + v.shape[1:]).swapaxes(0, 1).reshape(v.shape)

    def ffn_out(pair):
        return jnp.stack(pair).transpose(1, 3, 2, 0, 4).reshape(D, FF)

    value_full, dg_one = cols_out(*[by_a(v[:, :, HR:]) for v in gq])
    output_full, dg_two = cols_out(*[v[:, :, HR:] for v in gp])
    ga = jnp.stack([v[:, :, :HR] for v in gp])
    gb = jnp.stack([by_a(v[:, :, :HR]) for v in gq])
    gm = jnp.stack([ga, gb]).reshape(2, 2, G, Z, HA, QB, KB).transpose(0, 4, 3, 1, 5, 2, 6)
    gd = [by_a(v) for v in gd]
    dgs = jnp.stack([dg_one, dg_two]).astype(F32)
    dgs = lax.psum_scatter(dgs, ax, scatter_dimension=1, tiled=True)
    return (
        layer_out, grad_in, dgs[0], scatter(value_full, 0, 1), scatter(gm.reshape(H, L, L), 2, 1),
        scatter(output_full, 0, 1).T, dgs[1], scatter(ffn_out(gu), 0, 1), scatter(ffn_out(gd), 0, 1).T,
    )


def solution(mesh):
    tok = P(("gx", "gy"), None)
    vec = P(("gx", "gy"))
    wgt = P("gx", "gy")
    twg = P("gy", "gx")
    mix = P(None, "gy", "gx")
    in_specs = (tok, P("gx", None), vec, wgt, mix, twg, vec, wgt, twg, tok)
    out_specs = (tok, tok, vec, wgt, mix, twg, vec, wgt, twg)

    def run(*args):
        small = (mesh.shape["gx"], mesh.shape["gy"], args[0].shape[0]) == (G, 2 * Z, L)
        return (small_shards if small else any_shards)(*args)

    return jax.shard_map(run, mesh=mesh, in_specs=in_specs, out_specs=out_specs, check_vma=False)
```

```python
import functools

import jax
import jax.numpy as jnp
from jax import lax
from jax.experimental import pallas as pl
from jax.experimental.pallas import tpu as pltpu
from jax.sharding import PartitionSpec as P

D = 768
H = 12
HS = 64
FF = 3072
L = 512
EPS = 1e-05
G = 4
Z = 4
DB = D // G
CB = D // (2 * Z)
FB = FF // (2 * Z)
QB = L // (2 * Z)
KB = L // G
LN = 128
GW = 2 * LN
GN = CB // 4
HA = H // 2
ZS = 2
HR = HA * QB
TM = 128
WIN = 3
HZ = H // Z
GC = 0.7978845608
GA = 0.044715
VMEM_LIMIT = 40 * 1024 * 1024
COST = 1
CFG = {
    "fz": ("c1",),
    "aw1": ("bxy",),
    "aw2": ("fz1",),
    "bz": ("c1",),
    "f1": ("aw1",),
    "wc": ("f1",),
    "ac": ("bz", "f1"),
    "k1": ("ac", "bc"),
    "cp": ("f1r",),
    "m1": ("f2r",),
    "m2": ("fzr",),
}

F32 = jnp.float32
BF16 = jnp.bfloat16


def dot(a, b, ca, cb):
    return lax.dot_general(a, b, (((ca,), (cb,)), ((), ())), preferred_element_type=F32)


def call(body, grid, in_specs, out_specs, out_shape, scratch=(), flops=0, nbytes=0, vmem=VMEM_LIMIT):
    return pl.pallas_call(
        body,
        grid_spec=pltpu.PrefetchScalarGridSpec(
            num_scalar_prefetch=1,
            grid=grid,
            in_specs=in_specs,
            out_specs=out_specs,
            scratch_shapes=list(scratch),
        ),
        out_shape=out_shape,
        compiler_params=pltpu.CompilerParams(
            dimension_semantics=("arbitrary",) * len(grid), vmem_limit_bytes=vmem
        ),
        cost_estimate=pl.CostEstimate(flops=COST, bytes_accessed=nbytes, transcendentals=0),
    )


def whole(shape):
    return pl.BlockSpec(memory_space=pltpu.VMEM)


def rows(width):
    return pl.BlockSpec((TM, width), lambda i, t: (i, 0))


def out_whole(shape):
    return pl.BlockSpec(memory_space=pltpu.VMEM)


def tab_a(t, g):
    return t[1 + g]


def tab_b(t, g):
    return t[1 + G + g]


def tab_z(t, z):
    return t[1 + 2 * G + z]


def g_of(t, r, order_b):
    return t[1 + 2 * G + Z] ^ (r if order_b else (r % 2) * 2 + r // 2)


def norm_stats(x):
    mean = jnp.mean(x, axis=-1, keepdims=True)
    cen = x - mean
    rstd = lax.rsqrt(jnp.mean(cen * cen, axis=-1, keepdims=True) + EPS)
    return cen, rstd


def weight_z(own, oth, t, z, base):
    parts = [
        jnp.concatenate(
            [ref[tab_a(t, g), tab_z(t, z), base : base + DB, :] for g in range(G)], axis=0
        )
        for ref in (own, oth)
    ]
    return jnp.concatenate(parts, axis=1)


def head_masks(core, nrows):
    lane = lax.broadcasted_iota(jnp.int32, (nrows, GW), 1)
    tile = lane // LN
    place = lane - tile * LN
    side = jnp.where(core == 0, tile, 1 - tile)
    col = jnp.where(place < CB, side * CB + place, -1)
    return [jnp.logical_and(col >= HS * i, col < HS * (i + 1)) for i in range(HZ)]


def halves(ref, core, lead=None, base=0):
    lo = pl.multiple_of(base + core * QB, QB)
    hi = pl.multiple_of(base + (1 - core) * QB, QB)
    if lead is None:
        return jnp.concatenate([ref[pl.ds(lo, QB), :], ref[pl.ds(hi, QB), :]], axis=0)
    return jnp.concatenate([ref[lead, pl.ds(lo, QB), :], ref[lead, pl.ds(hi, QB), :]], axis=0)


def put_halves(ref, core, val, lead=None, base=0):
    lo = pl.multiple_of(base + core * QB, QB)
    hi = pl.multiple_of(base + (1 - core) * QB, QB)
    if lead is None:
        ref[pl.ds(lo, QB), :] = val[:QB]
        ref[pl.ds(hi, QB), :] = val[QB:]
    else:
        ref[lead, pl.ds(lo, QB), :] = val[:QB]
        ref[lead, pl.ds(hi, QB), :] = val[QB:]


def window(m):
    return jnp.clip(m - 1, 0, G - WIN)


def exp_scores(a_own, a_oth, b_own, b_oth, t, m, head, mask):
    parts = []
    for i in range(WIN):
        both = []
        for a, b in ((a_own, b_own), (a_oth, b_oth)):
            if head < HA:
                both.append(a[tab_b(t, window(m) + i), tab_z(t, m), head * QB : (head + 1) * QB, :])
            else:
                h = head - HA
                both.append(b[tab_z(t, m), i, h * QB : (h + 1) * QB, :])
        parts.append(jnp.concatenate(both, axis=0))
    scores = jnp.concatenate(parts, axis=1).astype(F32)
    return jnp.where(mask, jnp.exp(scores), 0.0)


def gain_spots():
    for g in range(G):
        for z in range(Z):
            for c in range(2):
                yield g, z, c, DB * g + (2 * GN) * z + GN * c


def pick(core, c, own, oth):
    return jnp.where(core == c, own, oth)


def gains_row(own, oth, t, base):
    lane = lax.broadcasted_iota(jnp.int32, (1, LN), 1)
    tiles = [jnp.zeros((1, LN), F32) for _ in range(D // LN)]
    for g, z, c, at in gain_spots():
        a, b = (r[tab_a(t, g), tab_z(t, z), base : base + 16, :].astype(F32)[:1] for r in (own, oth))
        row = pick(t[0], c, a, b)
        tile, off = at // LN, at % LN
        row = pltpu.roll(row, (off - CB) % LN, 1)
        tiles[tile] = jnp.where(jnp.logical_and(lane >= off, lane < off + GN), row, tiles[tile])
        if off + GN > LN:
            tiles[tile + 1] = jnp.where(lane < off + GN - LN, row, tiles[tile + 1])
    return jnp.concatenate(tiles, axis=1)


def with_gains(full, dg, t):
    lane = lax.broadcasted_iota(jnp.int32, (1, LN), 1)
    top = lax.broadcasted_iota(jnp.int32, (16, LN), 0) == 0
    spot = jnp.logical_and(top, jnp.logical_and(lane >= CB, lane < CB + GN))
    rows_of = {}
    for g, z, c, at in gain_spots():
        tile, off = at // LN, at % LN
        row = dg[:, tile * LN : (tile + 1) * LN]
        if off + GN > LN:
            row = jnp.where(lane < off, dg[:, (tile + 1) * LN : (tile + 2) * LN], row)
        rows_of[g, z, c] = pltpu.roll(row, (CB - off) % LN, 1)
    for z in range(Z):
        for g in range(G):
            for p in range(2):
                row = pick(t[0], p, rows_of[g, z, 0], rows_of[g, z, 1])
                at = z, slice(g * DB, g * DB + 16), slice(p * LN, (p + 1) * LN)
                full[at] = jnp.where(spot, row, full[at].astype(F32)).astype(BF16)


def by_rows(body):
    def step(i, carry):
        body(pl.ds(pl.multiple_of(i * TM, TM), TM))
        return carry

    lax.fori_loop(0, L // TM, step, 0)


def values_body(t, x_ref, own_ref, oth_ref, n_ref, val_ref, gain_ref):
    gain_ref[0:1, :] = gains_row(own_ref, oth_ref, t, 0)
    gain_ref[1:2, :] = gains_row(own_ref, oth_ref, t, DB)

    def norm(at):
        cen, rstd = norm_stats(x_ref[at, :].astype(F32))
        n_ref[at, :] = (cen * rstd * gain_ref[0:1, :]).astype(BF16)

    by_rows(norm)
    for z in range(Z):
        val_ref[z] = dot(n_ref[...], weight_z(own_ref, oth_ref, t, z, 0), 1, 0).astype(BF16)


def probs_of(units, t, m, z, mask):
    parts = []
    for i in range(HZ):
        e = exp_scores(*units, t, m, HZ * z + i, mask)
        inv = 1.0 / jnp.sum(e, axis=-1, keepdims=True)
        parts.append(e * inv)
    return parts


def mixer_body(
    t, x_ref, gain_ref, dq_ref, dk_ref, val_ref, a_own, a_oth, b_own, b_oth, w_own, w_oth,
    mix_ref, mid_ref, n_ref,
):
    m = pl.program_id(0)
    core = t[0]
    base = m * TM
    k0 = pl.multiple_of(window(m) * KB, KB)
    mask = halves(dq_ref, core) == dk_ref[:, pl.ds(k0, WIN * KB)]
    heads = head_masks(core, TM)
    for z in range(Z):
        win = val_ref[z, pl.ds(k0, WIN * KB), :]
        prob = probs_of((a_own, a_oth, b_own, b_oth), t, m, z, mask)
        part = dot(jnp.concatenate([p.astype(BF16) for p in prob], axis=0), win, 1, 0)
        out = jnp.zeros((TM, GW), F32)
        for i in range(HZ):
            out = jnp.where(heads[i], part[i * TM : (i + 1) * TM], out)
        put_halves(mix_ref, core, out.astype(BF16), z, base)

    @pl.when(m == Z - 1)
    def _():
        acc = dot(mix_ref[0], weight_z(w_own, w_oth, t, 0, DB), 1, 1)
        for z in range(1, Z):
            acc = acc + dot(mix_ref[z], weight_z(w_own, w_oth, t, z, DB), 1, 1)
        mid_ref[...] = acc

        def norm(at):
            mid = x_ref[at, :].astype(F32) + mid_ref[at, :]
            mid_ref[at, :] = mid
            cen, rstd = norm_stats(mid)
            n_ref[at, :] = (cen * rstd * gain_ref[1:2, :]).astype(BF16)

        by_rows(norm)


def ffn_body(pair, t, *refs):
    refs = list(refs)
    n_refs, refs = refs[: 1 + pair], refs[1 + pair :]
    c_refs, refs = refs[: 1 + pair], refs[1 + pair :]
    u_refs, d_refs = refs[:2], refs[2:4]
    ku, su, kd, sd = refs[4:8]
    out_refs = refs[8:]
    n_all, c_all, a_acc, b_acc, gu_all, gd_all = out_refs[2 + 2 * pair :]
    out_refs = out_refs[: 2 + 2 * pair]
    j = pl.program_id(0)

    @pl.when(j == 0)
    def _():
        for i in range(1 + pair):
            n_all[i * L : (i + 1) * L] = n_refs[i][...]
            c_all[i * L : (i + 1) * L] = c_refs[i][...]
        a_acc[...] = jnp.zeros_like(a_acc)
        b_acc[...] = jnp.zeros_like(b_acc)

    n, cot = n_all[...], c_all[...]
    def weights(parts, tab):
        cols = []
        for i in range(ZS):
            blocks = []
            for g in range(G):
                at = tab(t, g)
                one, two = (r[at % 2, i] for r in parts)
                blocks.append(jnp.where(at < 2, one, two))
            cols.append(jnp.concatenate(blocks, axis=0))
        return jnp.concatenate(cols, axis=1)

    up_w, dn_w = weights(u_refs, tab_b), weights(d_refs, tab_a)
    up = dot(n, up_w, 1, 0)
    sq = up * up
    th = jnp.tanh(GC * up * (1.0 + GA * sq))
    half = 0.5 + 0.5 * th
    act = (up * half).astype(BF16)
    slope = half + (0.5 * GC) * up * (1.0 - th * th) * (1.0 + (3.0 * GA) * sq)
    a_acc[...] += dot(act, dn_w, 1, 1)
    gd_all[...] = dot(cot, act, 0, 0).astype(BF16)
    up_g = (dot(cot, dn_w, 1, 0) * slope).astype(BF16)
    gu_all[...] = dot(n, up_g, 0, 0).astype(BF16)
    b_acc[...] += dot(up_g, up_w, 1, 1)
    for src, order_b, keep, send in ((gu_all, True, ku, su), (gd_all, False, kd, sd)):
        for r in range(G):
            at = pl.ds(pl.multiple_of(g_of(t, r, order_b) * DB, DB), DB)
            for i in range(ZS):
                (keep, send)[r // 2][r % 2, i] = src[at, i * FB : (i + 1) * FB]

    @pl.when(j == Z // ZS - 1)
    def _():
        for i in range(1 + pair):
            part = slice(i * L, (i + 1) * L)
            out_refs[i][...] = a_acc[part].astype(out_refs[i].dtype)
            out_refs[1 + pair + i][...] = b_acc[part].astype(out_refs[1 + pair + i].dtype)


def norm_back(cen, rstd, gain, dn):
    xhat = cen * rstd
    e = dn * gain
    dv = (
        e
        - jnp.mean(e, axis=-1, keepdims=True)
        - xhat * jnp.mean(e * xhat, axis=-1, keepdims=True)
    ) * rstd
    return dv, jnp.sum(dn * xhat, axis=0, keepdims=True)


def back_body(
    t, dna_ref, dnb_ref, mid_ref, c_ref, x_ref, low_ref, gain_ref, dq_ref, dk_ref, mix_ref, val_ref,
    a_own, a_oth, b_own, b_oth, w_own, w_oth,
    gi_ref, kp_ref, sp_ref, kq_ref, sq_ref,
    dg_acc, br_ref, grad_ref, vg_acc, vg_ref, full_ref, mg_ref, dn_ref,
):
    m = pl.program_id(0)
    core = t[0]
    base = m * TM
    start = window(m)
    k0 = pl.multiple_of(start * KB, KB)

    def put(tab, refs):
        for z in range(Z):
            for g in range(G):
                for p, ref in enumerate(refs):
                    blk = full_ref[z, g * DB : (g + 1) * DB, p * LN : (p + 1) * LN]
                    ref[tab(t, g), tab_z(t, z), HR:, :] = blk

    @pl.when(m == 0)
    def _():
        vg_acc[...] = jnp.zeros_like(vg_acc)
        dg_acc[...] = jnp.zeros_like(dg_acc)

        def norm(at):
            cen, rstd = norm_stats(mid_ref[at, :])
            dn = dna_ref[at, :] + dnb_ref[at, :].astype(F32)
            dv, dg = norm_back(cen, rstd, gain_ref[1:2, :], dn)
            dg_acc[0:1, :] += dg
            mid_grad = c_ref[at, :].astype(F32) + dv
            mg_ref[at, :] = mid_grad
            br_ref[at, :] = mid_grad.astype(BF16)

        by_rows(norm)
        branch = br_ref[...]
        for z in range(Z):
            grad_ref[z] = dot(branch, weight_z(w_own, w_oth, t, z, DB), 1, 0).astype(BF16)
            full_ref[z] = dot(branch, mix_ref[z], 0, 0).astype(BF16)
        with_gains(full_ref, dg_acc[0:1, :], t)
        put(tab_b, (kp_ref, sp_ref))
        dg_acc[...] = jnp.zeros_like(dg_acc)

    mask = halves(dq_ref, core) == dk_ref[:, pl.ds(k0, WIN * KB)]
    heads = head_masks(core, TM)
    at_z = tab_z(t, m)
    rest = jnp.where(start == 0, G - 1, 0)
    for refs, tab in (((kp_ref, sp_ref), tab_b), ((kq_ref, sq_ref), tab_a)):
        for ref in refs:
            ref[tab(t, rest), at_z, 0:HR, :] = jnp.zeros((HR, KB), BF16)
    for z in range(Z):
        grad = halves(grad_ref, core, z, base)
        mine = jnp.concatenate(
            [jnp.where(heads[i], grad, jnp.zeros_like(grad)) for i in range(HZ)], axis=0
        )
        win = val_ref[z, pl.ds(k0, WIN * KB), :]
        prob = probs_of((a_own, a_oth, b_own, b_oth), t, m, z, mask)
        dp = dot(mine, win, 1, 1)
        low = jnp.concatenate([p.astype(BF16) for p in prob], axis=0)
        vg_acc[z, pl.ds(k0, WIN * KB), :] += dot(low, mine, 0, 0)
        for i in range(HZ):
            head = HZ * z + i
            pd = prob[i] * dp[i * TM : (i + 1) * TM]
            ds = (pd - prob[i] * jnp.sum(pd, axis=-1, keepdims=True)).astype(BF16)
            refs, tab = ((kp_ref, sp_ref), tab_b) if head < HA else ((kq_ref, sq_ref), tab_a)
            row = head % HA * QB
            for k in range(WIN):
                for p, ref in enumerate(refs):
                    ref[tab(t, start + k), at_z, row : row + QB, :] = ds[
                        p * QB : (p + 1) * QB, k * KB : (k + 1) * KB
                    ]

    @pl.when(m == Z - 1)
    def _():
        vg_ref[...] = vg_acc[...].astype(BF16)
        acc = dot(vg_ref[0], weight_z(w_own, w_oth, t, 0, 0), 1, 1)
        for z in range(1, Z):
            acc = acc + dot(vg_ref[z], weight_z(w_own, w_oth, t, z, 0), 1, 1)
        dn_ref[...] = acc

        def norm(at):
            cen, rstd = norm_stats(x_ref[at, :].astype(F32))
            dv, dg = norm_back(cen, rstd, gain_ref[0:1, :], dn_ref[at, :])
            dg_acc[0:1, :] += dg
            gi_ref[at, :] = mg_ref[at, :] + dv

        by_rows(norm)
        low = low_ref[...]
        for z in range(Z):
            full_ref[z] = dot(low, vg_ref[z], 0, 0).astype(BF16)
        with_gains(full_ref, dg_acc[0:1, :], t)
        put(tab_a, (kq_ref, sq_ref))


def sds(shape, dtype):
    return jax.ShapeDtypeStruct(shape, dtype)


W_SHAPE = (G, Z, 2 * DB, LN)
V_SHAPE = (G, Z, DB, LN)
A_SHAPE = (G, Z, HR, KB)
S_SHAPE = (G, Z, HR + DB, KB)
B_SHAPE = (Z, WIN, HR, KB)
F_SHAPE = (G, Z, DB, FB)
Z_ROWS = pl.BlockSpec((Z, TM, GW), lambda i, t: (0, i, 0))


def run_values(tab, x, w):
    return call(
        values_body,
        (1,),
        [whole((L, D)), whole(W_SHAPE), whole(W_SHAPE)],
        [out_whole((L, D)), out_whole((Z, L, GW)), out_whole((8, D))],
        [sds((L, D), BF16), sds((Z, L, GW), BF16), sds((8, D), F32)],
        flops=2 * L * D * Z * GW,
        nbytes=6 << 20,
    )(tab, x, *w)


def run_mixer(tab, x, gain, dq, dk, vals, a, b, w):
    return call(
        mixer_body,
        (L // TM,),
        [
            whole((L, D)), whole((8, D)), rows(1), whole((1, L)), whole((Z, L, GW)),
            whole(A_SHAPE), whole(A_SHAPE), whole(B_SHAPE), whole(B_SHAPE),
            whole(W_SHAPE), whole(W_SHAPE),
        ],
        [out_whole((Z, L, GW)), out_whole((L, D)), out_whole((L, D))],
        [sds((Z, L, GW), BF16), sds((L, D), F32), sds((L, D), BF16)],
        flops=2 * L * D * Z * GW + 2 * H * L * WIN * KB * GW,
        nbytes=14 << 20,
    )(tab, x, gain, dq, dk, vals, *a, *b, *w)


def run_ffn(tab, ns, cots, u_w, d_w):
    n = len(ns)
    out = pl.BlockSpec((2, ZS, DB, FB), lambda i, t: (0, i, 0, 0))
    types = [F32, BF16][:n] * 2
    return call(
        functools.partial(ffn_body, n - 1),
        (Z // ZS,),
        [whole((L, D))] * (2 * n) + [out] * 4,
        [out] * 4 + [out_whole((L, D))] * (2 * n),
        [sds((2, Z, DB, FB), BF16)] * 4 + [sds((L, D), k) for k in types],
        scratch=(
            pltpu.VMEM((n * L, D), BF16), pltpu.VMEM((n * L, D), BF16), pltpu.VMEM((n * L, D), F32),
            pltpu.VMEM((n * L, D), F32), pltpu.VMEM((D, ZS * FB), BF16), pltpu.VMEM((D, ZS * FB), BF16),
        ),
        flops=6 * L * D * FF,
        nbytes=20 << 20,
        vmem=54 << 20,
    )(tab, *ns, *cots, *u_w, *d_w)


def run_back(tab, dn, mid, cot, x, low, gain, dq, dk, mixed, vals, a, b, w):
    args = [*dn, mid, cot, x, low, gain, dq, dk, mixed, vals, *a, *b, *w]
    specs = [whole(None)] * len(args)
    specs[7] = rows(1)
    return call(
        back_body,
        (L // TM,),
        specs,
        [whole(None)] * 5,
        [sds((L, D), F32)] + [sds(S_SHAPE, BF16)] * 4,
        scratch=(
            pltpu.VMEM((8, D), F32), pltpu.VMEM((L, D), BF16), pltpu.VMEM((Z, L, GW), BF16),
            pltpu.VMEM((Z, L, GW), F32), pltpu.VMEM((Z, L, GW), BF16), pltpu.VMEM((Z, D, GW), BF16),
            pltpu.VMEM((L, D), F32), pltpu.VMEM((L, D), F32),
        ),
        flops=8 * L * D * Z * GW,
        nbytes=40 << 20,
        vmem=32 << 20,
    )(tab, *args)


def add_up(terms):
    total = terms[0].astype(F32)
    for term in terms[1:]:
        total = total + term.astype(F32)
    return total


def after(val, *deps):
    return lax.optimization_barrier((val, deps))[0]


class Grid:
    def __init__(self, gx, gy):
        self.gy = gy
        self.size = {"y": gx // 2, "x": 2, "z": gy // 2, "c": 2}
        i, j = lax.axis_index("gx"), lax.axis_index("gy")
        self.at = {"y": i // 2, "x": i % 2, "z": j // 2, "c": j % 2}

    def fetch(self, val, axis, k):
        sizes = self.size
        pairs = []
        for y in range(sizes["y"]):
            for x in range(sizes["x"]):
                for z in range(sizes["z"]):
                    for c in range(sizes["c"]):
                        src = {"y": y, "x": x, "z": z, "c": c}
                        dst = dict(src)
                        dst[axis] = src[axis] ^ k
                        pairs.append(tuple((p["y"] * 2 + p["x"]) * self.gy + p["z"] * 2 + p["c"] for p in (src, dst)))
        return lax.ppermute(val, ("gx", "gy"), pairs)

    def rel(self, axis, v):
        return self.at[axis] ^ v

    def spread(self, val, axis):
        return jnp.stack([val] + [self.fetch(val, axis, k) for k in range(1, self.size[axis])])

    def reduce(self, terms, stage, axis, *deps):
        if deps:
            terms = terms[:-1] + [(after(terms[-1][0], *deps), terms[-1][1])]
        got = []
        for k in range(1, self.size[axis]):
            part = add_up([v[(0,) * (stage - born) + (k,)] for v, born in terms]).astype(BF16)
            got.append((self.fetch(part, axis, k), stage + 1))
        return terms + got

    def total(self, terms, stage):
        return add_up([v[(0,) * (stage - born)] for v, born in terms])

    def reduce_joined(self, groups, axis, *deps):
        groups = list(groups)
        if deps:
            groups[-1] = groups[-1][:-1] + [(after(groups[-1][-1][0], *deps), groups[-1][-1][1])]
        got = []
        for k in range(1, self.size[axis]):
            parts = [
                add_up([v[(0,) * (2 - born) + (k,)] for v, born in terms]).astype(BF16)
                for terms in groups
            ]
            got.append(self.fetch(jnp.concatenate(parts, axis=0), axis, k))
        out, at_row = [], 0
        for terms in groups:
            n = terms[0][0].shape[-2]
            own = [v[(0,) * (3 - born)] for v, born in terms]
            out.append(add_up(own + [v[at_row : at_row + n] for v in got]))
            at_row += n
        return out


def compute(tab, x, docs, cot, a, b, w, u, d):
    dq, dk = docs.reshape(L, 1), docs
    low, vals, gain = run_values(tab, x, w)
    mixed, mid, n_two = run_mixer(tab, x, gain, dq, dk, vals, a, b, w)
    sides = [
        run_ffn(tab, [n_two], [cot], (u[p, :2], u[p, 2:]), (d[p, :2], d[p, 2:])) for p in range(2)
    ]
    gu, gd = ([jnp.concatenate(v[i : i + 2], axis=0) for v in sides] for i in (0, 2))
    layer_out = (mid + sides[0][4] + sides[1][4]).astype(BF16)
    grad_in, kp, sp, kq, sq = run_back(
        tab, (sides[0][5], sides[1][5]), mid, cot, x, low, gain, dq, dk, mixed, vals, a, b, w
    )
    return layer_out, grad_in, gu, gd, (kp, sp), (kq, sq)


def lane_pad(mat, gains):
    row = jnp.pad(gains.reshape(1, GN), ((0, DB - 1), (0, LN - CB - GN)))
    return jnp.concatenate([mat, row], axis=1)


def small_shards(layer_in, doc_ids, mix_gain, value_w, mixing, output_w, ffn_gain, up_w, down_w, cot):
    grid = Grid(G, 2 * Z)
    at = grid.at
    order_a = [grid.rel("x", g % 2) * 2 + grid.rel("y", g // 2) for g in range(G)]
    order_b = [grid.rel("y", g // 2) * 2 + grid.rel("x", g % 2) for g in range(G)]
    order_z = [grid.rel("z", z) for z in range(Z)]
    own = [at["y"] * 2 + at["x"]]
    tab = jnp.stack([at["c"]] + order_a + order_b + order_z + own).astype(jnp.int32)
    docs = lax.dynamic_slice_in_dim(doc_ids, lax.axis_index("gy"), 1, 0)

    dq, dk = docs.reshape(L, 1), docs
    mix = mixing.reshape(2, HR, KB)
    fetch, spread = grid.fetch, grid.spread
    wts = jnp.concatenate([lane_pad(value_w, mix_gain), lane_pad(output_w.T, ffn_gain)], axis=0)

    def both(val, *deps):
        return val, fetch(after(val, *deps) if deps else val, "c", 1)

    def along_z(val):
        return [val] + [fetch(val, "z", k) for k in range(1, Z)]

    events = {}

    def mark(name, *vals):
        events[name] = vals

    def hook(name, val):
        deps = [events[d] for d in CFG.get(name, ())]
        return after(val, *deps) if deps else val

    c1 = along_z(jnp.concatenate([mix[0], wts], axis=0))
    mark("c1", c1[1:])
    cots = [cot, fetch(cot, "c", 1)]
    b = spread(spread(mix[1], "x"), "y").reshape(G, HR, KB)
    mark("bxy", b)
    start = window(at["z"])
    order = jnp.stack(order_b)
    b = jnp.stack([lax.dynamic_index_in_dim(b, order[start + i], 0, False) for i in range(WIN)])
    a, w = (jnp.stack([v[i * HR : (i + 1) * HR] for v in c1]) for i in range(2))
    ffn = along_z(hook("fz", jnp.stack([up_w, down_w.T])))
    for i in range(1, Z):
        mark("fz%d" % i, ffn[i])
    mark("fz", ffn[1:])
    a, w = hook("aw1", (a, w))
    ra, rw = fetch(a, "x", 1), fetch(w, "y", 1)
    mark("aw1", ra, rw)
    a, w = hook("aw2", (jnp.stack([a, ra]), jnp.stack([w, rw])))
    ra, rw = fetch(a, "y", 1), fetch(w, "x", 1)
    mark("aw2", ra, rw)
    mark("w2", rw)
    a, w = jnp.stack([a, ra]).reshape(A_SHAPE), jnp.stack([w, rw]).reshape(W_SHAPE)
    b = along_z(hook("bz", b))
    mark("bz1", b[1])
    mark("bz", b[1:])
    u, d = hook("f1", tuple(jnp.stack([v[i] for v in ffn]) for i in range(2)))
    ru, rd = fetch(u, "x", 1), fetch(d, "y", 1)
    mark("f1", ru, rd)
    w = both(hook("wc", w))
    mark("wc", w[1])
    a = both(hook("ac", a))
    mark("ac", a[1])
    u, d = hook("f2", (jnp.stack([u, ru]), jnp.stack([d, rd])))
    u, d = [u, fetch(u, "y", 1)], [d, fetch(d, "x", 1)]
    mark("f2", u[1], d[1])
    if CFG.get("bc") == ("k1",):
        low, vals, gain = run_values(tab, hook("k1", layer_in), w)
        mark("k1", low)
        b = both(hook("bc", jnp.stack(b)))
        mark("bc", b[1])
    else:
        b = both(hook("bc", jnp.stack(b)))
        mark("bc", b[1])
        low, vals, gain = run_values(tab, hook("k1", layer_in), w)
    mixed, mid, n_two = run_mixer(tab, layer_in, hook("k2", gain), dq, dk, vals, a, b, w)

    def begin(keep, send):
        got = fetch(send, "c", 1)
        return [(v.reshape((2, 2) + v.shape[1:]), 0) for v in (keep, got)]

    def last(*groups):
        return [terms[-1][0] for terms in groups]

    ku, su, kd, sd, out_a, out_b, ng_a, ng_b = run_ffn(
        tab, [n_two, fetch(n_two, "c", 1)], cots, u, d
    )
    ng_b = fetch(ng_b, "c", 1)
    gu = [(ku, 1), (fetch(su, "y", 1), 1)]
    gd = [(kd, 1), (fetch(sd, "x", 1), 1)]
    out_b = fetch(out_b, "c", 1)
    layer_out = (mid + out_a + out_b.astype(F32)).astype(BF16)
    grad_in, kp, sp, kq, sq = run_back(
        tab, (ng_a, ng_b), mid, cot, layer_in, low, gain, dq, dk, mixed, vals, a, b, w
    )
    mark("f1r", last(gu, gd))
    sp, sq = hook("cp", (sp, sq))
    gp, gq = begin(kp, sp), begin(kq, sq)
    mark("cp", last(gp, gq))
    gu, gd = grid.reduce(gu, 1, "x", sp), grid.reduce(gd, 1, "y", sp)
    mark("f2r", last(gu, gd))
    gp[-1] = (hook("m1", gp[-1][0]), 0)
    gp, gq = grid.reduce(gp, 0, "y"), grid.reduce(gq, 0, "x")
    mark("m1", last(gp, gq))
    gu[-1] = (hook("fzr", gu[-1][0]), 2)
    gu, gd = grid.reduce_joined((gu, gd), "z")
    mark("fzr", gu)
    gp[-1] = (hook("m2", gp[-1][0]), 1)
    gq[-1] = (hook("m2", gq[-1][0]), 1)
    gp, gq = grid.reduce(gp, 1, "x"), grid.reduce(gq, 1, "y")
    mark("m2", last(gp, gq))
    gp, gq = grid.reduce_joined((gp, gq), "z")

    go, gv = gp[HR:], gq[HR:]
    grad_mixing = jnp.concatenate([gp[:HR], gq[:HR]], axis=0).reshape(H, QB, KB)
    return (
        layer_out, grad_in, gv[0, CB : CB + GN], gv[:, :CB], grad_mixing, go[:, :CB].T,
        go[0, CB : CB + GN], gu, gd.T,
    )


def cols_in(v, o, gains):
    def blocks(mat, gain):
        mat = mat.reshape(G, DB, Z, 2, CB).transpose(3, 0, 2, 1, 4)
        gain = gain.reshape(G, Z, 2, 1, GN).transpose(2, 0, 1, 3, 4)
        gain = jnp.pad(gain, ((0, 0),) * 3 + ((0, DB - 1), (0, LN - CB - GN)))
        return jnp.concatenate([mat, gain], axis=-1)

    return jnp.concatenate([blocks(v, gains[0]), blocks(o, gains[1])], axis=3)


def cols_out(keep, send):
    mat = jnp.stack([keep, send])
    dg = mat[:, :, :, 0, CB : CB + GN].transpose(1, 2, 0, 3).reshape(D)
    return mat[..., :CB].transpose(1, 3, 2, 0, 4).reshape(D, D), dg


def any_shards(layer_in, doc_ids, mix_gain, value_w, mixing, output_w, ffn_gain, up_w, down_w, cot):
    ax = ("gx", "gy")
    seqs = layer_in.shape[0] // L
    me = lax.axis_index("gy") * seqs

    def gather(arr, d0, d1):
        arr = lax.all_gather(arr, "gx", axis=d0, tiled=True)
        return lax.all_gather(arr, "gy", axis=d1, tiled=True)

    def scatter(arr, d0, d1):
        arr = lax.psum_scatter(arr, "gx", scatter_dimension=d0, tiled=True)
        return lax.psum_scatter(arr, "gy", scatter_dimension=d1, tiled=True).astype(F32)

    gains = lax.all_gather(jnp.stack([mix_gain, ffn_gain]), ax, axis=1, tiled=True)
    w = cols_in(gather(value_w, 0, 1), gather(output_w.T, 0, 1), gains)
    mix_full = gather(mixing, 2, 1).reshape(2, HA, Z, 2, QB, G, KB).transpose(0, 3, 5, 2, 1, 4, 6)
    mix_full = mix_full.reshape(2, 2, G, Z, HR, KB)
    a = mix_full[0]
    starts = [min(max(m - 1, 0), G - WIN) for m in range(Z)]
    b = jnp.stack([mix_full[1][:, s : s + WIN, m] for m, s in enumerate(starts)], axis=1)
    u = gather(up_w, 0, 1).reshape(G, DB, Z, 2, FB).transpose(3, 0, 2, 1, 4)
    d = gather(down_w.T, 0, 1).reshape(G, DB, Z, 2, FB).transpose(3, 0, 2, 1, 4)
    w = w.reshape((2, 2, 2) + w.shape[2:]).swapaxes(1, 2).reshape(w.shape)
    d = d.reshape((2, 2, 2) + d.shape[2:]).swapaxes(1, 2).reshape(d.shape)
    tab = jnp.array([0, 0, 2, 1, 3] + [0, 1, 2, 3] * 2 + [0], jnp.int32)

    rows_out, grads = [], None
    for s in range(seqs):
        docs = lax.dynamic_slice_in_dim(doc_ids, me + s, 1, 0)
        part = slice(s * L, (s + 1) * L)
        out, g_in, *rest = compute(tab, layer_in[part], docs, cot[part], a, b, w, u, d)
        rows_out.append((out, g_in))
        rest = jax.tree.map(lambda v: v.astype(F32), rest) if seqs > 1 else rest
        grads = rest if grads is None else jax.tree.map(jnp.add, grads, rest)
    layer_out = jnp.concatenate([r[0] for r in rows_out], axis=0)
    grad_in = jnp.concatenate([r[1] for r in rows_out], axis=0)
    gu, gd, gp, gq = jax.tree.map(lambda v: v.astype(BF16), grads)

    def by_a(v):
        return v.reshape((2, 2) + v.shape[1:]).swapaxes(0, 1).reshape(v.shape)

    def ffn_out(pair):
        return jnp.stack(pair).transpose(1, 3, 2, 0, 4).reshape(D, FF)

    value_full, dg_one = cols_out(*[by_a(v[:, :, HR:]) for v in gq])
    output_full, dg_two = cols_out(*[v[:, :, HR:] for v in gp])
    ga = jnp.stack([v[:, :, :HR] for v in gp])
    gb = jnp.stack([by_a(v[:, :, :HR]) for v in gq])
    gm = jnp.stack([ga, gb]).reshape(2, 2, G, Z, HA, QB, KB).transpose(0, 4, 3, 1, 5, 2, 6)
    gd = [by_a(v) for v in gd]
    dgs = jnp.stack([dg_one, dg_two]).astype(F32)
    dgs = lax.psum_scatter(dgs, ax, scatter_dimension=1, tiled=True)
    return (
        layer_out, grad_in, dgs[0], scatter(value_full, 0, 1), scatter(gm.reshape(H, L, L), 2, 1),
        scatter(output_full, 0, 1).T, dgs[1], scatter(ffn_out(gu), 0, 1), scatter(ffn_out(gd), 0, 1).T,
    )


def solution(mesh):
    tok = P(("gx", "gy"), None)
    vec = P(("gx", "gy"))
    wgt = P("gx", "gy")
    twg = P("gy", "gx")
    mix = P(None, "gy", "gx")
    in_specs = (tok, P("gx", None), vec, wgt, mix, twg, vec, wgt, twg, tok)
    out_specs = (tok, tok, vec, wgt, mix, twg, vec, wgt, twg)

    def run(*args):
        small = (mesh.shape["gx"], mesh.shape["gy"], args[0].shape[0]) == (G, 2 * Z, L)
        return (small_shards if small else any_shards)(*args)

    return jax.shard_map(run, mesh=mesh, in_specs=in_specs, out_specs=out_specs, check_vma=False)
```

```python
import functools

import jax
import jax.numpy as jnp
from jax import lax
from jax.experimental import pallas as pl
from jax.experimental.pallas import tpu as pltpu
from jax.sharding import PartitionSpec as P

D = 768
H = 12
HS = 64
FF = 3072
L = 512
EPS = 1e-05
G = 4
Z = 4
DB = D // G
CB = D // (2 * Z)
FB = FF // (2 * Z)
QB = L // (2 * Z)
KB = L // G
LN = 128
GW = 2 * LN
GN = CB // 4
HA = H // 2
ZS = 2
HR = HA * QB
TM = 128
WIN = 3
HZ = H // Z
GC = 0.7978845608
GA = 0.044715
VMEM_LIMIT = 40 * 1024 * 1024
COST = 1
CFG = {
    "fz": ("c1",),
    "aw1": ("bxy",),
    "aw2": ("fz1",),
    "bz": ("c1",),
    "f1": ("aw1",),
    "wc": ("bz", "f1"),
    "ac": ("bz", "f1"),
    "k1": ("ac", "bc"),
    "cp": ("f1r",),
    "m1": ("f2r",),
    "m2": ("fzr",),
    "f2": ("aw2",),
}

F32 = jnp.float32
BF16 = jnp.bfloat16


def dot(a, b, ca, cb):
    return lax.dot_general(a, b, (((ca,), (cb,)), ((), ())), preferred_element_type=F32)


def call(body, grid, in_specs, out_specs, out_shape, scratch=(), flops=0, nbytes=0, vmem=VMEM_LIMIT):
    return pl.pallas_call(
        body,
        grid_spec=pltpu.PrefetchScalarGridSpec(
            num_scalar_prefetch=1,
            grid=grid,
            in_specs=in_specs,
            out_specs=out_specs,
            scratch_shapes=list(scratch),
        ),
        out_shape=out_shape,
        compiler_params=pltpu.CompilerParams(
            dimension_semantics=("arbitrary",) * len(grid), vmem_limit_bytes=vmem
        ),
        cost_estimate=pl.CostEstimate(flops=COST, bytes_accessed=nbytes, transcendentals=0),
    )


def whole(shape):
    return pl.BlockSpec(memory_space=pltpu.VMEM)


def rows(width):
    return pl.BlockSpec((TM, width), lambda i, t: (i, 0))


def out_whole(shape):
    return pl.BlockSpec(memory_space=pltpu.VMEM)


def tab_a(t, g):
    return t[1 + g]


def tab_b(t, g):
    return t[1 + G + g]


def tab_z(t, z):
    return t[1 + 2 * G + z]


def g_of(t, r, order_b):
    return t[1 + 2 * G + Z] ^ (r if order_b else (r % 2) * 2 + r // 2)


def norm_stats(x):
    mean = jnp.mean(x, axis=-1, keepdims=True)
    cen = x - mean
    rstd = lax.rsqrt(jnp.mean(cen * cen, axis=-1, keepdims=True) + EPS)
    return cen, rstd


def weight_z(own, oth, t, z, base):
    parts = [
        jnp.concatenate(
            [ref[tab_a(t, g), tab_z(t, z), base : base + DB, :] for g in range(G)], axis=0
        )
        for ref in (own, oth)
    ]
    return jnp.concatenate(parts, axis=1)


def head_masks(core, nrows):
    lane = lax.broadcasted_iota(jnp.int32, (nrows, GW), 1)
    tile = lane // LN
    place = lane - tile * LN
    side = jnp.where(core == 0, tile, 1 - tile)
    col = jnp.where(place < CB, side * CB + place, -1)
    return [jnp.logical_and(col >= HS * i, col < HS * (i + 1)) for i in range(HZ)]


def halves(ref, core, lead=None, base=0):
    lo = pl.multiple_of(base + core * QB, QB)
    hi = pl.multiple_of(base + (1 - core) * QB, QB)
    if lead is None:
        return jnp.concatenate([ref[pl.ds(lo, QB), :], ref[pl.ds(hi, QB), :]], axis=0)
    return jnp.concatenate([ref[lead, pl.ds(lo, QB), :], ref[lead, pl.ds(hi, QB), :]], axis=0)


def put_halves(ref, core, val, lead=None, base=0):
    lo = pl.multiple_of(base + core * QB, QB)
    hi = pl.multiple_of(base + (1 - core) * QB, QB)
    if lead is None:
        ref[pl.ds(lo, QB), :] = val[:QB]
        ref[pl.ds(hi, QB), :] = val[QB:]
    else:
        ref[lead, pl.ds(lo, QB), :] = val[:QB]
        ref[lead, pl.ds(hi, QB), :] = val[QB:]


def window(m):
    return jnp.clip(m - 1, 0, G - WIN)


def exp_scores(a_own, a_oth, b_own, b_oth, t, m, head, mask):
    parts = []
    for i in range(WIN):
        both = []
        for a, b in ((a_own, b_own), (a_oth, b_oth)):
            if head < HA:
                both.append(a[tab_b(t, window(m) + i), tab_z(t, m), head * QB : (head + 1) * QB, :])
            else:
                h = head - HA
                both.append(b[tab_z(t, m), i, h * QB : (h + 1) * QB, :])
        parts.append(jnp.concatenate(both, axis=0))
    scores = jnp.concatenate(parts, axis=1).astype(F32)
    return jnp.where(mask, jnp.exp(scores), 0.0)


def gain_spots():
    for g in range(G):
        for z in range(Z):
            for c in range(2):
                yield g, z, c, DB * g + (2 * GN) * z + GN * c


def pick(core, c, own, oth):
    return jnp.where(core == c, own, oth)


def gains_row(own, oth, t, base):
    lane = lax.broadcasted_iota(jnp.int32, (1, LN), 1)
    tiles = [jnp.zeros((1, LN), F32) for _ in range(D // LN)]
    for g, z, c, at in gain_spots():
        a, b = (r[tab_a(t, g), tab_z(t, z), base : base + 16, :].astype(F32)[:1] for r in (own, oth))
        row = pick(t[0], c, a, b)
        tile, off = at // LN, at % LN
        row = pltpu.roll(row, (off - CB) % LN, 1)
        tiles[tile] = jnp.where(jnp.logical_and(lane >= off, lane < off + GN), row, tiles[tile])
        if off + GN > LN:
            tiles[tile + 1] = jnp.where(lane < off + GN - LN, row, tiles[tile + 1])
    return jnp.concatenate(tiles, axis=1)


def with_gains(full, dg, t):
    lane = lax.broadcasted_iota(jnp.int32, (1, LN), 1)
    top = lax.broadcasted_iota(jnp.int32, (16, LN), 0) == 0
    spot = jnp.logical_and(top, jnp.logical_and(lane >= CB, lane < CB + GN))
    rows_of = {}
    for g, z, c, at in gain_spots():
        tile, off = at // LN, at % LN
        row = dg[:, tile * LN : (tile + 1) * LN]
        if off + GN > LN:
            row = jnp.where(lane < off, dg[:, (tile + 1) * LN : (tile + 2) * LN], row)
        rows_of[g, z, c] = pltpu.roll(row, (CB - off) % LN, 1)
    for z in range(Z):
        for g in range(G):
            for p in range(2):
                row = pick(t[0], p, rows_of[g, z, 0], rows_of[g, z, 1])
                at = z, slice(g * DB, g * DB + 16), slice(p * LN, (p + 1) * LN)
                full[at] = jnp.where(spot, row, full[at].astype(F32)).astype(BF16)


def by_rows(body):
    def step(i, carry):
        body(pl.ds(pl.multiple_of(i * TM, TM), TM))
        return carry

    lax.fori_loop(0, L // TM, step, 0)


def values_body(t, x_ref, own_ref, oth_ref, n_ref, val_ref, gain_ref):
    gain_ref[0:1, :] = gains_row(own_ref, oth_ref, t, 0)
    gain_ref[1:2, :] = gains_row(own_ref, oth_ref, t, DB)

    def norm(at):
        cen, rstd = norm_stats(x_ref[at, :].astype(F32))
        n_ref[at, :] = (cen * rstd * gain_ref[0:1, :]).astype(BF16)

    by_rows(norm)
    for z in range(Z):
        val_ref[z] = dot(n_ref[...], weight_z(own_ref, oth_ref, t, z, 0), 1, 0).astype(BF16)


def probs_of(units, t, m, z, mask):
    parts = []
    for i in range(HZ):
        e = exp_scores(*units, t, m, HZ * z + i, mask)
        inv = 1.0 / jnp.sum(e, axis=-1, keepdims=True)
        parts.append(e * inv)
    return parts


def mixer_body(
    t, x_ref, gain_ref, dq_ref, dk_ref, val_ref, a_own, a_oth, b_own, b_oth, w_own, w_oth,
    mix_ref, mid_ref, n_ref,
):
    m = pl.program_id(0)
    core = t[0]
    base = m * TM
    k0 = pl.multiple_of(window(m) * KB, KB)
    mask = halves(dq_ref, core) == dk_ref[:, pl.ds(k0, WIN * KB)]
    heads = head_masks(core, TM)
    for z in range(Z):
        win = val_ref[z, pl.ds(k0, WIN * KB), :]
        prob = probs_of((a_own, a_oth, b_own, b_oth), t, m, z, mask)
        part = dot(jnp.concatenate([p.astype(BF16) for p in prob], axis=0), win, 1, 0)
        out = jnp.zeros((TM, GW), F32)
        for i in range(HZ):
            out = jnp.where(heads[i], part[i * TM : (i + 1) * TM], out)
        put_halves(mix_ref, core, out.astype(BF16), z, base)

    @pl.when(m == Z - 1)
    def _():
        acc = dot(mix_ref[0], weight_z(w_own, w_oth, t, 0, DB), 1, 1)
        for z in range(1, Z):
            acc = acc + dot(mix_ref[z], weight_z(w_own, w_oth, t, z, DB), 1, 1)
        mid_ref[...] = acc

        def norm(at):
            mid = x_ref[at, :].astype(F32) + mid_ref[at, :]
            mid_ref[at, :] = mid
            cen, rstd = norm_stats(mid)
            n_ref[at, :] = (cen * rstd * gain_ref[1:2, :]).astype(BF16)

        by_rows(norm)


def ffn_body(pair, t, *refs):
    refs = list(refs)
    n_refs, refs = refs[: 1 + pair], refs[1 + pair :]
    c_refs, refs = refs[: 1 + pair], refs[1 + pair :]
    u_refs, d_refs = refs[:2], refs[2:4]
    ku, su, kd, sd = refs[4:8]
    out_refs = refs[8:]
    n_all, c_all, a_acc, b_acc, gu_all, gd_all = out_refs[2 + 2 * pair :]
    out_refs = out_refs[: 2 + 2 * pair]
    j = pl.program_id(0)

    @pl.when(j == 0)
    def _():
        for i in range(1 + pair):
            n_all[i * L : (i + 1) * L] = n_refs[i][...]
            c_all[i * L : (i + 1) * L] = c_refs[i][...]
        a_acc[...] = jnp.zeros_like(a_acc)
        b_acc[...] = jnp.zeros_like(b_acc)

    n, cot = n_all[...], c_all[...]
    def weights(parts, tab):
        cols = []
        for i in range(ZS):
            blocks = []
            for g in range(G):
                at = tab(t, g)
                one, two = (r[at % 2, i] for r in parts)
                blocks.append(jnp.where(at < 2, one, two))
            cols.append(jnp.concatenate(blocks, axis=0))
        return jnp.concatenate(cols, axis=1)

    up_w, dn_w = weights(u_refs, tab_b), weights(d_refs, tab_a)
    up = dot(n, up_w, 1, 0)
    sq = up * up
    th = jnp.tanh(GC * up * (1.0 + GA * sq))
    half = 0.5 + 0.5 * th
    act = (up * half).astype(BF16)
    slope = half + (0.5 * GC) * up * (1.0 - th * th) * (1.0 + (3.0 * GA) * sq)
    a_acc[...] += dot(act, dn_w, 1, 1)
    gd_all[...] = dot(cot, act, 0, 0).astype(BF16)
    up_g = (dot(cot, dn_w, 1, 0) * slope).astype(BF16)
    gu_all[...] = dot(n, up_g, 0, 0).astype(BF16)
    b_acc[...] += dot(up_g, up_w, 1, 1)
    for src, order_b, keep, send in ((gu_all, True, ku, su), (gd_all, False, kd, sd)):
        for r in range(G):
            at = pl.ds(pl.multiple_of(g_of(t, r, order_b) * DB, DB), DB)
            for i in range(ZS):
                (keep, send)[r // 2][r % 2, i] = src[at, i * FB : (i + 1) * FB]

    @pl.when(j == Z // ZS - 1)
    def _():
        for i in range(1 + pair):
            part = slice(i * L, (i + 1) * L)
            out_refs[i][...] = a_acc[part].astype(out_refs[i].dtype)
            out_refs[1 + pair + i][...] = b_acc[part].astype(out_refs[1 + pair + i].dtype)


def norm_back(cen, rstd, gain, dn):
    xhat = cen * rstd
    e = dn * gain
    dv = (
        e
        - jnp.mean(e, axis=-1, keepdims=True)
        - xhat * jnp.mean(e * xhat, axis=-1, keepdims=True)
    ) * rstd
    return dv, jnp.sum(dn * xhat, axis=0, keepdims=True)


def back_body(
    t, dna_ref, dnb_ref, mid_ref, c_ref, x_ref, low_ref, gain_ref, dq_ref, dk_ref, mix_ref, val_ref,
    a_own, a_oth, b_own, b_oth, w_own, w_oth,
    gi_ref, kp_ref, sp_ref, kq_ref, sq_ref,
    dg_acc, br_ref, grad_ref, vg_acc, vg_ref, full_ref, mg_ref, dn_ref,
):
    m = pl.program_id(0)
    core = t[0]
    base = m * TM
    start = window(m)
    k0 = pl.multiple_of(start * KB, KB)

    def put(tab, refs):
        for z in range(Z):
            for g in range(G):
                for p, ref in enumerate(refs):
                    blk = full_ref[z, g * DB : (g + 1) * DB, p * LN : (p + 1) * LN]
                    ref[tab(t, g), tab_z(t, z), HR:, :] = blk

    @pl.when(m == 0)
    def _():
        vg_acc[...] = jnp.zeros_like(vg_acc)
        dg_acc[...] = jnp.zeros_like(dg_acc)

        def norm(at):
            cen, rstd = norm_stats(mid_ref[at, :])
            dn = dna_ref[at, :] + dnb_ref[at, :].astype(F32)
            dv, dg = norm_back(cen, rstd, gain_ref[1:2, :], dn)
            dg_acc[0:1, :] += dg
            mid_grad = c_ref[at, :].astype(F32) + dv
            mg_ref[at, :] = mid_grad
            br_ref[at, :] = mid_grad.astype(BF16)

        by_rows(norm)
        branch = br_ref[...]
        for z in range(Z):
            grad_ref[z] = dot(branch, weight_z(w_own, w_oth, t, z, DB), 1, 0).astype(BF16)
            full_ref[z] = dot(branch, mix_ref[z], 0, 0).astype(BF16)
        with_gains(full_ref, dg_acc[0:1, :], t)
        put(tab_b, (kp_ref, sp_ref))
        dg_acc[...] = jnp.zeros_like(dg_acc)

    mask = halves(dq_ref, core) == dk_ref[:, pl.ds(k0, WIN * KB)]
    heads = head_masks(core, TM)
    at_z = tab_z(t, m)
    rest = jnp.where(start == 0, G - 1, 0)
    for refs, tab in (((kp_ref, sp_ref), tab_b), ((kq_ref, sq_ref), tab_a)):
        for ref in refs:
            ref[tab(t, rest), at_z, 0:HR, :] = jnp.zeros((HR, KB), BF16)
    for z in range(Z):
        grad = halves(grad_ref, core, z, base)
        mine = jnp.concatenate(
            [jnp.where(heads[i], grad, jnp.zeros_like(grad)) for i in range(HZ)], axis=0
        )
        win = val_ref[z, pl.ds(k0, WIN * KB), :]
        prob = probs_of((a_own, a_oth, b_own, b_oth), t, m, z, mask)
        dp = dot(mine, win, 1, 1)
        low = jnp.concatenate([p.astype(BF16) for p in prob], axis=0)
        vg_acc[z, pl.ds(k0, WIN * KB), :] += dot(low, mine, 0, 0)
        for i in range(HZ):
            head = HZ * z + i
            pd = prob[i] * dp[i * TM : (i + 1) * TM]
            ds = (pd - prob[i] * jnp.sum(pd, axis=-1, keepdims=True)).astype(BF16)
            refs, tab = ((kp_ref, sp_ref), tab_b) if head < HA else ((kq_ref, sq_ref), tab_a)
            row = head % HA * QB
            for k in range(WIN):
                for p, ref in enumerate(refs):
                    ref[tab(t, start + k), at_z, row : row + QB, :] = ds[
                        p * QB : (p + 1) * QB, k * KB : (k + 1) * KB
                    ]

    @pl.when(m == Z - 1)
    def _():
        vg_ref[...] = vg_acc[...].astype(BF16)
        acc = dot(vg_ref[0], weight_z(w_own, w_oth, t, 0, 0), 1, 1)
        for z in range(1, Z):
            acc = acc + dot(vg_ref[z], weight_z(w_own, w_oth, t, z, 0), 1, 1)
        dn_ref[...] = acc

        def norm(at):
            cen, rstd = norm_stats(x_ref[at, :].astype(F32))
            dv, dg = norm_back(cen, rstd, gain_ref[0:1, :], dn_ref[at, :])
            dg_acc[0:1, :] += dg
            gi_ref[at, :] = mg_ref[at, :] + dv

        by_rows(norm)
        low = low_ref[...]
        for z in range(Z):
            full_ref[z] = dot(low, vg_ref[z], 0, 0).astype(BF16)
        with_gains(full_ref, dg_acc[0:1, :], t)
        put(tab_a, (kq_ref, sq_ref))


def sds(shape, dtype):
    return jax.ShapeDtypeStruct(shape, dtype)


W_SHAPE = (G, Z, 2 * DB, LN)
V_SHAPE = (G, Z, DB, LN)
A_SHAPE = (G, Z, HR, KB)
S_SHAPE = (G, Z, HR + DB, KB)
B_SHAPE = (Z, WIN, HR, KB)
F_SHAPE = (G, Z, DB, FB)
Z_ROWS = pl.BlockSpec((Z, TM, GW), lambda i, t: (0, i, 0))


def run_values(tab, x, w):
    return call(
        values_body,
        (1,),
        [whole((L, D)), whole(W_SHAPE), whole(W_SHAPE)],
        [out_whole((L, D)), out_whole((Z, L, GW)), out_whole((8, D))],
        [sds((L, D), BF16), sds((Z, L, GW), BF16), sds((8, D), F32)],
        flops=2 * L * D * Z * GW,
        nbytes=6 << 20,
    )(tab, x, *w)


def run_mixer(tab, x, gain, dq, dk, vals, a, b, w):
    return call(
        mixer_body,
        (L // TM,),
        [
            whole((L, D)), whole((8, D)), rows(1), whole((1, L)), whole((Z, L, GW)),
            whole(A_SHAPE), whole(A_SHAPE), whole(B_SHAPE), whole(B_SHAPE),
            whole(W_SHAPE), whole(W_SHAPE),
        ],
        [out_whole((Z, L, GW)), out_whole((L, D)), out_whole((L, D))],
        [sds((Z, L, GW), BF16), sds((L, D), F32), sds((L, D), BF16)],
        flops=2 * L * D * Z * GW + 2 * H * L * WIN * KB * GW,
        nbytes=14 << 20,
    )(tab, x, gain, dq, dk, vals, *a, *b, *w)


def run_ffn(tab, ns, cots, u_w, d_w):
    n = len(ns)
    out = pl.BlockSpec((2, ZS, DB, FB), lambda i, t: (0, i, 0, 0))
    types = [F32, BF16][:n] * 2
    return call(
        functools.partial(ffn_body, n - 1),
        (Z // ZS,),
        [whole((L, D))] * (2 * n) + [out] * 4,
        [out] * 4 + [out_whole((L, D))] * (2 * n),
        [sds((2, Z, DB, FB), BF16)] * 4 + [sds((L, D), k) for k in types],
        scratch=(
            pltpu.VMEM((n * L, D), BF16), pltpu.VMEM((n * L, D), BF16), pltpu.VMEM((n * L, D), F32),
            pltpu.VMEM((n * L, D), F32), pltpu.VMEM((D, ZS * FB), BF16), pltpu.VMEM((D, ZS * FB), BF16),
        ),
        flops=6 * L * D * FF,
        nbytes=20 << 20,
        vmem=54 << 20,
    )(tab, *ns, *cots, *u_w, *d_w)


def run_back(tab, dn, mid, cot, x, low, gain, dq, dk, mixed, vals, a, b, w):
    args = [*dn, mid, cot, x, low, gain, dq, dk, mixed, vals, *a, *b, *w]
    specs = [whole(None)] * len(args)
    specs[7] = rows(1)
    return call(
        back_body,
        (L // TM,),
        specs,
        [whole(None)] * 5,
        [sds((L, D), F32)] + [sds(S_SHAPE, BF16)] * 4,
        scratch=(
            pltpu.VMEM((8, D), F32), pltpu.VMEM((L, D), BF16), pltpu.VMEM((Z, L, GW), BF16),
            pltpu.VMEM((Z, L, GW), F32), pltpu.VMEM((Z, L, GW), BF16), pltpu.VMEM((Z, D, GW), BF16),
            pltpu.VMEM((L, D), F32), pltpu.VMEM((L, D), F32),
        ),
        flops=8 * L * D * Z * GW,
        nbytes=40 << 20,
        vmem=32 << 20,
    )(tab, *args)


def add_up(terms):
    total = terms[0].astype(F32)
    for term in terms[1:]:
        total = total + term.astype(F32)
    return total


def after(val, *deps):
    return lax.optimization_barrier((val, deps))[0]


class Grid:
    def __init__(self, gx, gy):
        self.gy = gy
        self.size = {"y": gx // 2, "x": 2, "z": gy // 2, "c": 2}
        i, j = lax.axis_index("gx"), lax.axis_index("gy")
        self.at = {"y": i // 2, "x": i % 2, "z": j // 2, "c": j % 2}

    def fetch(self, val, axis, k):
        sizes = self.size
        pairs = []
        for y in range(sizes["y"]):
            for x in range(sizes["x"]):
                for z in range(sizes["z"]):
                    for c in range(sizes["c"]):
                        src = {"y": y, "x": x, "z": z, "c": c}
                        dst = dict(src)
                        dst[axis] = src[axis] ^ k
                        pairs.append(tuple((p["y"] * 2 + p["x"]) * self.gy + p["z"] * 2 + p["c"] for p in (src, dst)))
        return lax.ppermute(val, ("gx", "gy"), pairs)

    def rel(self, axis, v):
        return self.at[axis] ^ v

    def spread(self, val, axis):
        return jnp.stack([val] + [self.fetch(val, axis, k) for k in range(1, self.size[axis])])

    def reduce(self, terms, stage, axis, *deps):
        if deps:
            terms = terms[:-1] + [(after(terms[-1][0], *deps), terms[-1][1])]
        got = []
        for k in range(1, self.size[axis]):
            part = add_up([v[(0,) * (stage - born) + (k,)] for v, born in terms]).astype(BF16)
            got.append((self.fetch(part, axis, k), stage + 1))
        return terms + got

    def total(self, terms, stage):
        return add_up([v[(0,) * (stage - born)] for v, born in terms])

    def reduce_joined(self, groups, axis, *deps):
        groups = list(groups)
        if deps:
            groups[-1] = groups[-1][:-1] + [(after(groups[-1][-1][0], *deps), groups[-1][-1][1])]
        got = []
        for k in range(1, self.size[axis]):
            parts = [
                add_up([v[(0,) * (2 - born) + (k,)] for v, born in terms]).astype(BF16)
                for terms in groups
            ]
            got.append(self.fetch(jnp.concatenate(parts, axis=0), axis, k))
        out, at_row = [], 0
        for terms in groups:
            n = terms[0][0].shape[-2]
            own = [v[(0,) * (3 - born)] for v, born in terms]
            out.append(add_up(own + [v[at_row : at_row + n] for v in got]))
            at_row += n
        return out


def compute(tab, x, docs, cot, a, b, w, u, d):
    dq, dk = docs.reshape(L, 1), docs
    low, vals, gain = run_values(tab, x, w)
    mixed, mid, n_two = run_mixer(tab, x, gain, dq, dk, vals, a, b, w)
    sides = [
        run_ffn(tab, [n_two], [cot], (u[p, :2], u[p, 2:]), (d[p, :2], d[p, 2:])) for p in range(2)
    ]
    gu, gd = ([jnp.concatenate(v[i : i + 2], axis=0) for v in sides] for i in (0, 2))
    layer_out = (mid + sides[0][4] + sides[1][4]).astype(BF16)
    grad_in, kp, sp, kq, sq = run_back(
        tab, (sides[0][5], sides[1][5]), mid, cot, x, low, gain, dq, dk, mixed, vals, a, b, w
    )
    return layer_out, grad_in, gu, gd, (kp, sp), (kq, sq)


def lane_pad(mat, gains):
    row = jnp.pad(gains.reshape(1, GN), ((0, DB - 1), (0, LN - CB - GN)))
    return jnp.concatenate([mat, row], axis=1)


def small_shards(layer_in, doc_ids, mix_gain, value_w, mixing, output_w, ffn_gain, up_w, down_w, cot):
    grid = Grid(G, 2 * Z)
    at = grid.at
    order_a = [grid.rel("x", g % 2) * 2 + grid.rel("y", g // 2) for g in range(G)]
    order_b = [grid.rel("y", g // 2) * 2 + grid.rel("x", g % 2) for g in range(G)]
    order_z = [grid.rel("z", z) for z in range(Z)]
    own = [at["y"] * 2 + at["x"]]
    tab = jnp.stack([at["c"]] + order_a + order_b + order_z + own).astype(jnp.int32)
    docs = lax.dynamic_slice_in_dim(doc_ids, lax.axis_index("gy"), 1, 0)

    dq, dk = docs.reshape(L, 1), docs
    mix = mixing.reshape(2, HR, KB)
    fetch, spread = grid.fetch, grid.spread
    wts = jnp.concatenate([lane_pad(value_w, mix_gain), lane_pad(output_w.T, ffn_gain)], axis=0)

    def both(val, *deps):
        return val, fetch(after(val, *deps) if deps else val, "c", 1)

    def along_z(val):
        return [val] + [fetch(val, "z", k) for k in range(1, Z)]

    events = {}

    def mark(name, *vals):
        events[name] = vals

    def hook(name, val):
        deps = [events[d] for d in CFG.get(name, ())]
        return after(val, *deps) if deps else val

    c1 = along_z(jnp.concatenate([mix[0], wts], axis=0))
    mark("c1", c1[1:])
    cots = [cot, fetch(cot, "c", 1)]
    b = spread(spread(mix[1], "x"), "y").reshape(G, HR, KB)
    mark("bxy", b)
    start = window(at["z"])
    order = jnp.stack(order_b)
    b = jnp.stack([lax.dynamic_index_in_dim(b, order[start + i], 0, False) for i in range(WIN)])
    a, w = (jnp.stack([v[i * HR : (i + 1) * HR] for v in c1]) for i in range(2))
    ffn = along_z(hook("fz", jnp.stack([up_w, down_w.T])))
    for i in range(1, Z):
        mark("fz%d" % i, ffn[i])
    mark("fz", ffn[1:])
    a, w = hook("aw1", (a, w))
    ra, rw = fetch(a, "x", 1), fetch(w, "y", 1)
    mark("aw1", ra, rw)
    a, w = hook("aw2", (jnp.stack([a, ra]), jnp.stack([w, rw])))
    ra, rw = fetch(a, "y", 1), fetch(w, "x", 1)
    mark("aw2", ra, rw)
    mark("w2", rw)
    a, w = jnp.stack([a, ra]).reshape(A_SHAPE), jnp.stack([w, rw]).reshape(W_SHAPE)
    b = along_z(hook("bz", b))
    mark("bz1", b[1])
    mark("bz", b[1:])
    u, d = hook("f1", tuple(jnp.stack([v[i] for v in ffn]) for i in range(2)))
    ru, rd = fetch(u, "x", 1), fetch(d, "y", 1)
    mark("f1", ru, rd)
    w = both(hook("wc", w))
    mark("wc", w[1])
    a = both(hook("ac", a))
    mark("ac", a[1])
    u, d = hook("f2", (jnp.stack([u, ru]), jnp.stack([d, rd])))
    u, d = [u, fetch(u, "y", 1)], [d, fetch(d, "x", 1)]
    mark("f2", u[1], d[1])
    if CFG.get("bc") == ("k1",):
        low, vals, gain = run_values(tab, hook("k1", layer_in), w)
        mark("k1", low)
        b = both(hook("bc", jnp.stack(b)))
        mark("bc", b[1])
    else:
        b = both(hook("bc", jnp.stack(b)))
        mark("bc", b[1])
        low, vals, gain = run_values(tab, hook("k1", layer_in), w)
    mixed, mid, n_two = run_mixer(tab, layer_in, hook("k2", gain), dq, dk, vals, a, b, w)

    def begin(keep, send):
        got = fetch(send, "c", 1)
        return [(v.reshape((2, 2) + v.shape[1:]), 0) for v in (keep, got)]

    def last(*groups):
        return [terms[-1][0] for terms in groups]

    ku, su, kd, sd, out_a, out_b, ng_a, ng_b = run_ffn(
        tab, [n_two, fetch(n_two, "c", 1)], cots, u, d
    )
    ng_b = fetch(ng_b, "c", 1)
    gu = [(ku, 1), (fetch(su, "y", 1), 1)]
    gd = [(kd, 1), (fetch(sd, "x", 1), 1)]
    out_b = fetch(out_b, "c", 1)
    layer_out = (mid + out_a + out_b.astype(F32)).astype(BF16)
    grad_in, kp, sp, kq, sq = run_back(
        tab, (ng_a, ng_b), mid, cot, layer_in, low, gain, dq, dk, mixed, vals, a, b, w
    )
    mark("f1r", last(gu, gd))
    sp, sq = hook("cp", (sp, sq))
    gp, gq = begin(kp, sp), begin(kq, sq)
    mark("cp", last(gp, gq))
    gu, gd = grid.reduce(gu, 1, "x", sp), grid.reduce(gd, 1, "y", sp)
    mark("f2r", last(gu, gd))
    gp[-1] = (hook("m1", gp[-1][0]), 0)
    gp, gq = grid.reduce(gp, 0, "y"), grid.reduce(gq, 0, "x")
    mark("m1", last(gp, gq))
    gu[-1] = (hook("fzr", gu[-1][0]), 2)
    gu, gd = grid.reduce_joined((gu, gd), "z")
    mark("fzr", gu)
    gp[-1] = (hook("m2", gp[-1][0]), 1)
    gq[-1] = (hook("m2", gq[-1][0]), 1)
    gp, gq = grid.reduce(gp, 1, "x"), grid.reduce(gq, 1, "y")
    mark("m2", last(gp, gq))
    gp, gq = grid.reduce_joined((gp, gq), "z")

    go, gv = gp[HR:], gq[HR:]
    grad_mixing = jnp.concatenate([gp[:HR], gq[:HR]], axis=0).reshape(H, QB, KB)
    return (
        layer_out, grad_in, gv[0, CB : CB + GN], gv[:, :CB], grad_mixing, go[:, :CB].T,
        go[0, CB : CB + GN], gu, gd.T,
    )


def cols_in(v, o, gains):
    def blocks(mat, gain):
        mat = mat.reshape(G, DB, Z, 2, CB).transpose(3, 0, 2, 1, 4)
        gain = gain.reshape(G, Z, 2, 1, GN).transpose(2, 0, 1, 3, 4)
        gain = jnp.pad(gain, ((0, 0),) * 3 + ((0, DB - 1), (0, LN - CB - GN)))
        return jnp.concatenate([mat, gain], axis=-1)

    return jnp.concatenate([blocks(v, gains[0]), blocks(o, gains[1])], axis=3)


def cols_out(keep, send):
    mat = jnp.stack([keep, send])
    dg = mat[:, :, :, 0, CB : CB + GN].transpose(1, 2, 0, 3).reshape(D)
    return mat[..., :CB].transpose(1, 3, 2, 0, 4).reshape(D, D), dg


def any_shards(layer_in, doc_ids, mix_gain, value_w, mixing, output_w, ffn_gain, up_w, down_w, cot):
    ax = ("gx", "gy")
    seqs = layer_in.shape[0] // L
    me = lax.axis_index("gy") * seqs

    def gather(arr, d0, d1):
        arr = lax.all_gather(arr, "gx", axis=d0, tiled=True)
        return lax.all_gather(arr, "gy", axis=d1, tiled=True)

    def scatter(arr, d0, d1):
        arr = lax.psum_scatter(arr, "gx", scatter_dimension=d0, tiled=True)
        return lax.psum_scatter(arr, "gy", scatter_dimension=d1, tiled=True).astype(F32)

    gains = lax.all_gather(jnp.stack([mix_gain, ffn_gain]), ax, axis=1, tiled=True)
    w = cols_in(gather(value_w, 0, 1), gather(output_w.T, 0, 1), gains)
    mix_full = gather(mixing, 2, 1).reshape(2, HA, Z, 2, QB, G, KB).transpose(0, 3, 5, 2, 1, 4, 6)
    mix_full = mix_full.reshape(2, 2, G, Z, HR, KB)
    a = mix_full[0]
    starts = [min(max(m - 1, 0), G - WIN) for m in range(Z)]
    b = jnp.stack([mix_full[1][:, s : s + WIN, m] for m, s in enumerate(starts)], axis=1)
    u = gather(up_w, 0, 1).reshape(G, DB, Z, 2, FB).transpose(3, 0, 2, 1, 4)
    d = gather(down_w.T, 0, 1).reshape(G, DB, Z, 2, FB).transpose(3, 0, 2, 1, 4)
    w = w.reshape((2, 2, 2) + w.shape[2:]).swapaxes(1, 2).reshape(w.shape)
    d = d.reshape((2, 2, 2) + d.shape[2:]).swapaxes(1, 2).reshape(d.shape)
    tab = jnp.array([0, 0, 2, 1, 3] + [0, 1, 2, 3] * 2 + [0], jnp.int32)

    rows_out, grads = [], None
    for s in range(seqs):
        docs = lax.dynamic_slice_in_dim(doc_ids, me + s, 1, 0)
        part = slice(s * L, (s + 1) * L)
        out, g_in, *rest = compute(tab, layer_in[part], docs, cot[part], a, b, w, u, d)
        rows_out.append((out, g_in))
        rest = jax.tree.map(lambda v: v.astype(F32), rest) if seqs > 1 else rest
        grads = rest if grads is None else jax.tree.map(jnp.add, grads, rest)
    layer_out = jnp.concatenate([r[0] for r in rows_out], axis=0)
    grad_in = jnp.concatenate([r[1] for r in rows_out], axis=0)
    gu, gd, gp, gq = jax.tree.map(lambda v: v.astype(BF16), grads)

    def by_a(v):
        return v.reshape((2, 2) + v.shape[1:]).swapaxes(0, 1).reshape(v.shape)

    def ffn_out(pair):
        return jnp.stack(pair).transpose(1, 3, 2, 0, 4).reshape(D, FF)

    value_full, dg_one = cols_out(*[by_a(v[:, :, HR:]) for v in gq])
    output_full, dg_two = cols_out(*[v[:, :, HR:] for v in gp])
    ga = jnp.stack([v[:, :, :HR] for v in gp])
    gb = jnp.stack([by_a(v[:, :, :HR]) for v in gq])
    gm = jnp.stack([ga, gb]).reshape(2, 2, G, Z, HA, QB, KB).transpose(0, 4, 3, 1, 5, 2, 6)
    gd = [by_a(v) for v in gd]
    dgs = jnp.stack([dg_one, dg_two]).astype(F32)
    dgs = lax.psum_scatter(dgs, ax, scatter_dimension=1, tiled=True)
    return (
        layer_out, grad_in, dgs[0], scatter(value_full, 0, 1), scatter(gm.reshape(H, L, L), 2, 1),
        scatter(output_full, 0, 1).T, dgs[1], scatter(ffn_out(gu), 0, 1), scatter(ffn_out(gd), 0, 1).T,
    )


def solution(mesh):
    tok = P(("gx", "gy"), None)
    vec = P(("gx", "gy"))
    wgt = P("gx", "gy")
    twg = P("gy", "gx")
    mix = P(None, "gy", "gx")
    in_specs = (tok, P("gx", None), vec, wgt, mix, twg, vec, wgt, twg, tok)
    out_specs = (tok, tok, vec, wgt, mix, twg, vec, wgt, twg)

    def run(*args):
        small = (mesh.shape["gx"], mesh.shape["gy"], args[0].shape[0]) == (G, 2 * Z, L)
        return (small_shards if small else any_shards)(*args)

    return jax.shard_map(run, mesh=mesh, in_specs=in_specs, out_specs=out_specs, check_vma=False)
```
